32 devices in a mesh: dp: 8 (over z, y), tensor: 4 (over x, core).
Axes of the slice: x: 2, y: 2, z: 4, core: 2. Of those that a mesh axis runs over, the one named last changes fastest.
Arguments:
- hidden: bfloat16 [10240, 768], P(('dp', 'tensor')), may hold values from -6 to 6
- first_gain: float32 [768], replicated, may hold values from 0.5 to 1.5
- first_shift: float32 [768], replicated, may hold values from -1.5 to 1.5
- query_weight: bfloat16 [768, 768], P(None, 'tensor'), may hold values from -0.21875 to 0.21875
- query_bias: float32 [768], P('tensor'), may hold values from -1.5 to 1.5
- key_weight: bfloat16 [768, 768], P(None, 'tensor'), may hold values from -0.21875 to 0.21875
- value_weight: bfloat16 [768, 768], P(None, 'tensor'), may hold values from -0.21875 to 0.21875
- value_bias: float32 [768], P('tensor'), may hold values from -1.5 to 1.5
- output_weight: bfloat16 [768, 768], P('tensor'), may hold values from -3.5 to 3.5
- output_bias: float32 [768], replicated, may hold values from -1.5 to 1.5
- first_scale: float32 [768], replicated, may hold values from 0.5 to 1.5
- second_gain: float32 [768], replicated, may hold values from 0.5 to 1.5
- second_shift: float32 [768], replicated, may hold values from -1.5 to 1.5
- expand_weight: bfloat16 [768, 3072], P(None, 'tensor'), may hold values from -0.21875 to 0.21875
- expand_bias: float32 [3072], P('tensor'), may hold values from -1.5 to 1.5
- reduce_weight: bfloat16 [3072, 768], P('tensor'), may hold values from -0.109375 to 0.109375
- reduce_bias: float32 [768], replicated, may hold values from -1.5 to 1.5
- second_scale: float32 [768], replicated, may hold values from 0.5 to 1.5
- table_low: float32 [732, 12], P(None, 'tensor'), may hold values from -4 to 4
- table_high: float32 [2212, 12], P(None, 'tensor'), may hold values from -4 to 4
- resolution: int32 [16], P('dp'), may hold values from 0 to 1
- counts: int32 [8], P('dp'), may hold values from 1 to 2, as said below
- index_low: int32 [197, 197], replicated, may hold values from 0 to 731
- index_high: int32 [577, 577], replicated, may hold values from 0 to 2211
- cotangent: bfloat16 [10240, 768], P(('dp', 'tensor')), may hold values from -6 to 6
Outputs:
- result: bfloat16 [10240, 768], P(('dp', 'tensor'))
- hidden_grad: float32 [10240, 768], P(('dp', 'tensor'))
- first_gain_grad: float32 [768], replicated
- first_shift_grad: float32 [768], replicated
- query_weight_grad: float32 [768, 768], P(None, 'tensor')
- query_bias_grad: float32 [768], P('tensor')
- key_weight_grad: float32 [768, 768], P(None, 'tensor')
- value_weight_grad: float32 [768, 768], P(None, 'tensor')
- value_bias_grad: float32 [768], P('tensor')
- output_weight_grad: float32 [768, 768], P('tensor')
- output_bias_grad: float32 [768], replicated
- first_scale_grad: float32 [768], replicated
- second_gain_grad: float32 [768], replicated
- second_shift_grad: float32 [768], replicated
- expand_weight_grad: float32 [768, 3072], P(None, 'tensor')
- expand_bias_grad: float32 [3072], P('tensor')
- reduce_weight_grad: float32 [3072, 768], P('tensor')
- reduce_bias_grad: float32 [768], replicated
- second_scale_grad: float32 [768], replicated
- table_low_grad: float32 [732, 12], P(None, 'tensor')
- table_high_grad: float32 [2212, 12], P(None, 'tensor')
The draws below stay inside these ranges and needn't reach their ends.
Inputs may be any that keep to these rules, and one draw needn't show every extreme that they name: `counts`: some index of dp has all 2 slots live in every draw.
All inputs are finite; a program needn't handle non-finite values.
Results may differ from the reference program's by a relative error of at most 0.019.
Values may be sent and summed in bfloat16 or wider, within the bound.
A program may use at most 384 MiB of HBM per device.

```python
import jax
import jax.numpy as jnp
from jax import lax

D = 768
HEADS = 12
HD = 64
FF = 3072
P_LO = 197
P_HI = 577
NREL_LO = 732
NREL_HI = 2212
SEQ = 640
SLOTS = 2
IMAGES = 16
N_DP = 8


def draw_counts(key, part):
    first_key, second_key = jax.random.split(jax.random.fold_in(key, 17))
    values = jax.random.randint(first_key, (N_DP,), (SLOTS + 1) // 2, SLOTS + 1)
    full_shard = jax.random.randint(second_key, (), 0, N_DP)
    return jnp.where(jnp.arange(N_DP) == full_shard, SLOTS, values).astype(jnp.int32)


def set_ends(values, key, low, top_value):
    longest = values.shape.index(max(values.shape))
    spots = []
    for shift in (0, 1):
        where = [jax.random.randint(jax.random.fold_in(key, axis), (), 0, length) for axis, length in enumerate(values.shape)]
        where[longest] = (where[longest] + shift) % values.shape[longest]
        spots.append(tuple(where))
    return values.at[spots[0]].set(low).at[spots[1]].set(top_value)


def steps_of(own_key, dims, cuts, low, largest):
    def one(position, blocks):
        draws = jax.random.uniform(jax.random.fold_in(jax.random.fold_in(own_key, 6), position), (blocks,), jnp.float32, low / len(cuts), largest / len(cuts))
        return jnp.repeat(jnp.exp(draws), dims[position] // blocks).reshape((-1,) + (1,) * (len(dims) - position - 1))

    loudness = one(*cuts[0])
    for cut in cuts[1:]:
        loudness = loudness * one(*cut)
    return loudness


def bell_draw(stream_key, dims, spread, bound, cuts=(), kind=jnp.bfloat16):
    result = jax.random.normal(stream_key, dims, jnp.float32) * spread
    if len(cuts) > 0:
        result = steps_of(stream_key, dims, cuts, -0.22, 0.18) * result
    return jnp.clip(result, min=-bound, max=bound).astype(kind)


def setup_inputs(seed: int = 0) -> dict:
    arg_keys = jax.random.split(jax.random.key(seed), 26)
    hidden = bell_draw(arg_keys[0], (IMAGES * SEQ, D), 1.0, 6.0, ((0, 32),))
    first_gain = jnp.clip(1.0 + 0.1 * jax.random.normal(arg_keys[1], (D,), jnp.float32), 0.5, 1.5)
    first_shift = bell_draw(arg_keys[2], (D,), 0.3, 1.5, (), jnp.float32)
    query_weight = bell_draw(arg_keys[3], (D, D), D ** -0.5, 0.21875, ((1, 4),))
    query_bias = bell_draw(arg_keys[4], (D,), 0.3, 1.5, ((0, 4),), jnp.float32)
    key_weight = bell_draw(arg_keys[5], (D, D), D ** -0.5, 0.21875, ((1, 4),))
    value_weight = bell_draw(arg_keys[6], (D, D), D ** -0.5, 0.21875, ((1, 4),))
    value_bias = bell_draw(arg_keys[7], (D,), 0.3, 1.5, ((0, 4),), jnp.float32)
    output_weight = bell_draw(arg_keys[8], (D, D), (max(1, D // 256)) ** -0.5, 3.5, ((0, 4),))
    output_bias = bell_draw(arg_keys[9], (D,), 0.3, 1.5, (), jnp.float32)
    first_scale = jnp.clip(1.0 + 0.1 * jax.random.normal(arg_keys[10], (D,), jnp.float32), 0.5, 1.5)
    second_gain = jnp.clip(1.0 + 0.1 * jax.random.normal(arg_keys[11], (D,), jnp.float32), 0.5, 1.5)
    second_shift = bell_draw(arg_keys[12], (D,), 0.3, 1.5, (), jnp.float32)
    expand_weight = bell_draw(arg_keys[13], (D, FF), D ** -0.5, 0.21875, ((1, 4),))
    expand_bias = bell_draw(arg_keys[14], (FF,), 0.3, 1.5, ((0, 4),), jnp.float32)
    reduce_weight = bell_draw(arg_keys[15], (FF, D), FF ** -0.5, 0.109375, ((0, 4),))
    reduce_bias = bell_draw(arg_keys[16], (D,), 0.3, 1.5, (), jnp.float32)
    second_scale = jnp.clip(1.0 + 0.1 * jax.random.normal(arg_keys[17], (D,), jnp.float32), 0.5, 1.5)
    table_low = bell_draw(arg_keys[18], (NREL_LO, HEADS), 1.0, 4.0, ((1, 4),), jnp.float32)
    table_high = bell_draw(arg_keys[19], (NREL_HI, HEADS), 1.0, 4.0, ((1, 4),), jnp.float32)
    resolution = set_ends(jax.random.randint(arg_keys[20], (IMAGES,), 0, 2), jax.random.fold_in(arg_keys[20], 1), 0, 1).astype(jnp.int32)
    counts = draw_counts(jax.random.fold_in(arg_keys[25], 71), 0)
    index_low = set_ends(jax.random.randint(arg_keys[22], (P_LO, P_LO), 0, NREL_LO), jax.random.fold_in(arg_keys[22], 1), 0, NREL_LO - 1).astype(jnp.int32)
    index_high = set_ends(jax.random.randint(arg_keys[23], (P_HI, P_HI), 0, NREL_HI), jax.random.fold_in(arg_keys[23], 1), 0, NREL_HI - 1).astype(jnp.int32)
    cotangent = bell_draw(arg_keys[24], (IMAGES * SEQ, D), 1.0, 6.0, ((0, 32),))
    return {"hidden": hidden, "first_gain": first_gain, "first_shift": first_shift, "query_weight": query_weight, "query_bias": query_bias, "key_weight": key_weight, "value_weight": value_weight, "value_bias": value_bias, "output_weight": output_weight, "output_bias": output_bias, "first_scale": first_scale, "second_gain": second_gain, "second_shift": second_shift, "expand_weight": expand_weight, "expand_bias": expand_bias, "reduce_weight": reduce_weight, "reduce_bias": reduce_bias, "second_scale": second_scale, "table_low": table_low, "table_high": table_high, "resolution": resolution, "counts": counts, "index_low": index_low, "index_high": index_high, "cotangent": cotangent}


@jax.custom_vjp
def low(v):
    return lax.optimization_barrier(v.astype(jnp.bfloat16)).astype(jnp.float32)

@jax.custom_vjp
def low_back(v):
    return v

def low_keep(v):
    return (low(v), None)

def low_pass(kept, grad):
    return (grad,)

def back_keep(v):
    return (v, None)

def back_low(kept, grad):
    return (low(grad),)
low.defvjp(low_keep, low_pass)
low_back.defvjp(back_keep, back_low)
highest = lax.Precision.HIGHEST
eps_norm = 1e-06
masked_score = -1e+30

def matmul(left, right):
    return jnp.dot(left, right, precision=highest, preferred_element_type=jnp.float32)

def normalize(values, gain, shift):
    center = lax.optimization_barrier(jnp.mean(values, axis=-1, keepdims=True))
    centered = values - center
    variance = lax.optimization_barrier(jnp.mean(centered * centered, axis=-1, keepdims=True))
    return centered * lax.rsqrt(variance + eps_norm) * gain + shift

def row_mask(resolution, counts):
    row_ids = jnp.arange(IMAGES * SEQ)
    image_ids = row_ids // SEQ
    positions = row_ids % SEQ
    res_rows = resolution[image_ids]
    limits = jnp.where(res_rows == 1, P_HI, P_LO)
    shard_counts = counts[image_ids // SLOTS]
    live_rows = (positions < limits) & (image_ids % SLOTS < shard_counts)
    return live_rows.astype(jnp.float32)

def bias_map(table, index, length):
    picked = jnp.transpose(table[index], (2, 0, 1))
    return jnp.pad(picked, ((0, 0), (0, SEQ - length), (0, SEQ - length)))

def layer(hidden, first_gain, first_shift, query_weight, query_bias, key_weight, value_weight, value_bias, output_weight, output_bias, first_scale, second_gain, second_shift, expand_weight, expand_bias, reduce_weight, reduce_bias, second_scale, table_low, table_high, resolution, index_low, index_high):
    normed_one = low(normalize(hidden, first_gain, first_shift))
    head_scale = HD ** (-0.5)
    queries = low((low_back(matmul(normed_one, query_weight)) + query_bias) * head_scale)
    keys = low(low_back(matmul(normed_one, key_weight)))
    values = low(low_back(matmul(normed_one, value_weight)) + value_bias)
    bias_low = bias_map(table_low, index_low, P_LO)
    bias_high = bias_map(table_high, index_high, P_HI)
    positions = jnp.arange(SEQ)

    def attend(inputs):
        query_img, key_img, value_img, res_img = inputs
        chosen = jnp.where(res_img == 1, bias_high, bias_low)
        key_bound = jnp.where(res_img == 1, P_HI, P_LO)
        product = jnp.einsum('qhd,khd->hqk', query_img, key_img, precision=highest)
        scores = low_back(product) + chosen
        scores = jnp.where((positions < key_bound)[None, None, :], scores, masked_score)
        attention = jax.nn.softmax(scores, axis=-1)
        return jnp.einsum('hqk,khd->qhd', low(attention), value_img, precision=highest)
    shaped = (IMAGES, SEQ, HEADS, HD)
    mixture = lax.map(jax.checkpoint(attend), (queries.reshape(shaped), keys.reshape(shaped), values.reshape(shaped), resolution))
    mixture = low(low_back(mixture.reshape(IMAGES * SEQ, D)))
    attn_out = low_back(matmul(mixture, output_weight)) + output_bias
    after_attn = hidden + first_scale * attn_out
    normed_two = low(normalize(after_attn, second_gain, second_shift))
    pre_act = low_back(matmul(normed_two, expand_weight)) + expand_bias
    activated = low(jax.nn.gelu(pre_act, approximate=False))
    mlp_out = low_back(matmul(activated, reduce_weight)) + reduce_bias
    return after_attn + second_scale * mlp_out

def reference(hidden, first_gain, first_shift, query_weight, query_bias, key_weight, value_weight, value_bias, output_weight, output_bias, first_scale, second_gain, second_shift, expand_weight, expand_bias, reduce_weight, reduce_bias, second_scale, table_low, table_high, resolution, counts, index_low, index_high, cotangent):
    floats = [item.astype(jnp.float32) for item in (hidden, first_gain, first_shift, query_weight, query_bias, key_weight, value_weight, value_bias, output_weight, output_bias, first_scale, second_gain, second_shift, expand_weight, expand_bias, reduce_weight, reduce_bias, second_scale, table_low, table_high)]
    live_rows = row_mask(resolution, counts)

    def forward(*params):
        return layer(*params, resolution, index_low, index_high) * live_rows[:, None]
    output, pullback = jax.vjp(forward, *floats)
    grads = pullback(cotangent.astype(jnp.float32))
    return (output.astype(jnp.bfloat16), grads[0], grads[1], grads[2], grads[3], grads[4], grads[5], grads[6], grads[7], grads[8], grads[9], grads[10], grads[11], grads[12], grads[13], grads[14], grads[15], grads[16], grads[17], grads[18], grads[19])
```

```python
import functools

import jax
import jax.numpy as jnp
from jax import lax
from jax.experimental import pallas as pl
from jax.experimental.pallas import tpu as pltpu
from jax.sharding import PartitionSpec as P

HD = 64
P_LO = 197
P_HI = 577
SEQ = 640
SLOTS = 2


eps_norm = 1e-06
masked_score = -1e30
inv_sqrt_two = 0.7071067811865476
inv_sqrt_two_pi = 0.3989422804014327


def normalize(values, gain, shift):
    center = jnp.mean(values, axis=-1, keepdims=True)
    centered = values - center
    variance = jnp.mean(centered * centered, axis=-1, keepdims=True)
    inverse = lax.rsqrt(variance + eps_norm)
    scaled = centered * inverse
    return (scaled * gain + shift, scaled, inverse)


def normalize_back(upstream, scaled, inverse, gain):
    inner = upstream * gain
    mean_inner = jnp.mean(inner, axis=-1, keepdims=True)
    mean_mixed = jnp.mean(inner * scaled, axis=-1, keepdims=True)
    return inverse * (inner - mean_inner - scaled * mean_mixed)


def gelu_value(values):
    return 0.5 * values * (1.0 + jax.scipy.special.erf(values * inv_sqrt_two))


def gelu_slope(values):
    return 0.5 * (
        1.0 + jax.scipy.special.erf(values * inv_sqrt_two)
    ) + values * inv_sqrt_two_pi * jnp.exp(-0.5 * values * values)


F32=jnp.float32; BF=jnp.bfloat16
NT=(((1,),(1,)),((),()))
def head_mask(h, width):
    lane = lax.broadcasted_iota(jnp.int32, (1, width), 1)
    return ((lane >= h*HD) & (lane < (h+1)*HD)).astype(F32).astype(BF)

def attend_kernel(chunk, res, q_ref, k_ref, v_ref, blo, bhi, mix_ref, p_ref):
    heads = bhi.shape[0]
    width = q_ref.shape[1]
    image = pl.program_id(0)
    def run(bias, rows, cols):
        k = k_ref[0:cols, :]
        v = v_ref[0:cols, :]
        vm = [v * head_mask(h, width) for h in range(heads)]
        for start in range(0, rows, chunk):
            size = min(chunk, rows - start)
            q = q_ref[start:start+size, :]
            acc = jnp.zeros((size, width), F32)
            for h in range(heads):
                s = lax.dot_general(q * head_mask(h, width), k, NT, preferred_element_type=F32)
                s = s + bias[h, start:start+size, 0:cols]
                peak = jnp.max(s, axis=1, keepdims=True)
                e = jnp.exp(s - peak)
                total = jnp.sum(e, axis=1, keepdims=True)
                p = (e * (1.0 / total)).astype(BF)
                p_ref[0, h, start:start+size, 0:cols] = p
                acc = acc + jnp.dot(p, vm[h], preferred_element_type=F32)
            mix_ref[start:start+size, :] = acc.astype(BF)
        if rows < SEQ:
            mix_ref[rows:SEQ, :] = jnp.zeros((SEQ-rows, width), BF)
    @pl.when(res[image] == 1)
    def _(): run(bhi, SEQ, SEQ)
    @pl.when(res[image] != 1)
    def _(): run(blo, blo.shape[1], blo.shape[2])

def attend(res, q, k, v, blo, bhi, chunk=320):
    heads = bhi.shape[0]; slots = q.shape[0]//SEQ; width = q.shape[1]
    row = pl.BlockSpec((SEQ, width), lambda i: (i, 0))
    full = lambda a: pl.BlockSpec(a.shape, lambda i: (0,)*a.ndim, pipeline_mode=pl.Buffered(1))
    return pl.pallas_call(functools.partial(attend_kernel, chunk),
        grid=(slots,),
        out_shape=(jax.ShapeDtypeStruct(q.shape, BF), jax.ShapeDtypeStruct((slots, heads, SEQ, SEQ), BF)),
        in_specs=[pl.BlockSpec(memory_space=pltpu.SMEM), row, row, row, full(blo), full(bhi)],
        out_specs=(row, pl.BlockSpec((1, heads, SEQ, SEQ), lambda i: (i,0,0,0))),
        name="attend", compiler_params=pltpu.CompilerParams(vmem_limit_bytes=40<<20))(res, q, k, v, blo, bhi)

BB=32; UN=16
def scatter_run(idx_ref, g_ref, out, n):
    heads = g_ref.shape[0]; na = out.shape[1]; m = idx_ref.shape[1]
    out[...] = jnp.zeros_like(out)
    ib = lax.broadcasted_iota(jnp.int32, (16, m), 0).astype(F32)
    def body(r, c):
        ms = []; os = []
        for u in range(UN):
            row = r*UN+u
            idx = jnp.broadcast_to(idx_ref[pl.ds(row,1), :], (16, m))
            ia = (idx >> 5).astype(F32).astype(BF); il = (idx & 31).astype(F32).astype(BF)
            g = [jnp.broadcast_to(g_ref[h, pl.ds(row,1), :], (16, m)).astype(BF) for h in range(heads)]
            hits = [il == (ib + 16.0*k).astype(BF) for k in range(BB//16)]
            ms.append(jnp.concatenate([jnp.where(hits[k], g[h], jnp.zeros_like(g[h])) for h in range(heads) for k in range(BB//16)], axis=0))
            os.append(jnp.concatenate([jnp.where(ia == (ib + 16.0*k).astype(BF), jnp.ones_like(ia), jnp.zeros_like(ia)) for k in range(na//16)], axis=0))
        out[...] += lax.dot_general(jnp.concatenate(ms, axis=1), jnp.concatenate(os, axis=1), NT, preferred_element_type=F32)
        return c
    lax.fori_loop(0, n//UN, body, 0)

def back_kernel(scale, res, q_ref, k_ref, v_ref, p_ref, d_ref, ilo, ihi, dq_ref, dk_ref, dv_ref, sq_ref, sv_ref, tlo, thi, glo, ghi):
    heads = ghi.shape[0]
    width = q_ref.shape[1]
    image = pl.program_id(0)
    @pl.when(image == 0)
    def _():
        glo[...] = jnp.zeros_like(glo)
        ghi[...] = jnp.zeros_like(ghi)
        sq_ref[...] = jnp.zeros_like(sq_ref)
        sv_ref[...] = jnp.zeros_like(sv_ref)
    def run(g_ref, rows, cols):
        k = k_ref[0:cols, :]
        v = v_ref[0:cols, :]
        q = q_ref[0:rows, :]
        d = d_ref[0:rows, :]
        qt = q.T
        dt = d.T
        dq = jnp.zeros((rows, width), F32)
        dks = []; dvs = []
        gr = min(rows, g_ref.shape[1])
        for h in range(heads):
            mask = head_mask(h, width)
            p = p_ref[0, h, 0:rows, 0:cols]
            dp = lax.dot_general(d * mask, v, NT, preferred_element_type=F32)
            pf = p.astype(F32)
            t = pf * dp
            ds = t - pf * jnp.sum(t, axis=1, keepdims=True)
            g_ref[h, 0:gr, 0:cols] += ds[0:gr]
            low = ds.astype(BF)
            dq = dq + jnp.dot(low, k * mask, preferred_element_type=F32)
            dks.append(jnp.dot(qt[h*HD:(h+1)*HD], low, preferred_element_type=F32))
            dvs.append(jnp.dot(dt[h*HD:(h+1)*HD], p, preferred_element_type=F32))
        dq = dq * scale
        dk = jnp.concatenate(dks, axis=0).T
        dv = jnp.concatenate(dvs, axis=0).T
        sq_ref[...] += jnp.sum(dq, axis=0, keepdims=True)
        sv_ref[...] += jnp.sum(dv, axis=0, keepdims=True)
        for ref, val, n in ((dq_ref, dq, rows), (dk_ref, dk, cols), (dv_ref, dv, cols)):
            ref[0:n, :] = val.astype(BF)
            if n < SEQ:
                ref[n:SEQ, :] = jnp.zeros((SEQ-n, width), BF)
    @pl.when(res[image] == 1)
    def _(): run(ghi, SEQ, SEQ)
    @pl.when(res[image] != 1)
    def _(): run(glo, glo.shape[1], glo.shape[2])
    @pl.when(image == pl.num_programs(0)-1)
    def _():
        scatter_run(ilo, glo, tlo, 208)
        scatter_run(ihi, ghi, thi, 592)

def attend_back(res, q, k, v, p, d, ilo, ihi, n_lo, n_hi, scale):
    heads = p.shape[1]; slots = q.shape[0]//SEQ; width = q.shape[1]
    na = lambda n: -(-(-(-n//BB))//16)*16
    row = pl.BlockSpec((SEQ, width), lambda i: (i, 0))
    full = lambda shape: pl.BlockSpec(shape, lambda i: (0,)*len(shape), pipeline_mode=pl.Buffered(1))
    outs = ((heads*BB, na(n_lo)), (heads*BB, na(n_hi)))
    dq, dk, dv, sq, sv, tlo, thi = pl.pallas_call(functools.partial(back_kernel, scale),
        grid=(slots,),
        out_shape=(jax.ShapeDtypeStruct(q.shape, BF),)*3+(jax.ShapeDtypeStruct((1, width), F32),)*2+tuple(jax.ShapeDtypeStruct(s, F32) for s in outs),
        in_specs=[pl.BlockSpec(memory_space=pltpu.SMEM), row, row, row, pl.BlockSpec((1, heads, SEQ, SEQ), lambda i: (i,0,0,0)), row, full(ilo.shape), full(ihi.shape)],
        out_specs=(row,)*3+(full((1, width)),)*2+tuple(full(s) for s in outs),
        scratch_shapes=[pltpu.VMEM((heads,)+ilo.shape, F32), pltpu.VMEM((heads,)+ihi.shape, F32)],
        name="attend_back", compiler_params=pltpu.CompilerParams(vmem_limit_bytes=48<<20))(res, q, k, v, p, d, ilo, ihi)
    fix = lambda o, n: o.reshape(heads, BB, -1).transpose(2,1,0).reshape(-1, heads)[:n]
    return dq, dk, dv, sq[0], sv[0], fix(tlo, n_lo), fix(thi, n_hi)

PACK=8191.0
def gather_kernel(tab_lo, tab_hi, idx_lo, idx_hi, out_lo, out_hi):
    heads = out_lo.shape[0]
    def fill(tab, idx_ref, out, rows, limit):
        nch = tab.shape[1]
        ncol = idx_ref.shape[1]//128
        def body(r, c):
            rws = pl.ds(pl.multiple_of(r*8, 8), 8)
            for j in range(ncol):
                cols = pl.ds(j*128, 128)
                idx = idx_ref[rws, cols]
                lane = idx & 127
                ch = idx >> 7
                shift = jnp.where(ch >= nch, 0, 16)
                ch = jnp.where(ch >= nch, ch - nch, ch)
                acc = [None]*heads
                for k in range(nch):
                    hit = ch == k
                    for h in range(heads):
                        v = jnp.take_along_axis(tab[h, k], lane, axis=1)
                        acc[h] = v if k == 0 else jnp.where(hit, v, acc[h])
                for h in range(heads):
                    val = ((acc[h] << shift) >> 16).astype(F32) * (1.0/PACK)
                    if (j+1)*128 > limit:
                        col = lax.broadcasted_iota(jnp.int32, (8,128), 1) + j*128
                        val = jnp.where(col < limit, val, masked_score)
                    out[h, rws, cols] = val
            return c
        lax.fori_loop(0, -(-rows//8), body, 0)
    fill(tab_lo, idx_lo, out_lo, P_LO, P_LO)
    fill(tab_hi, idx_hi, out_hi, P_HI, P_HI)
    out_lo[:, 200:, :] = jnp.zeros((heads, out_lo.shape[1]-200, out_lo.shape[2]), F32)
    out_hi[:, 584:, :] = jnp.zeros((heads, out_hi.shape[1]-584, out_hi.shape[2]), F32)

def gather_maps(table_low, table_high, idx_lo, idx_hi):
    heads = table_low.shape[1]
    def chunks(t):
        n = -(-t.shape[0]//256)*256
        w = jnp.round(jnp.pad(t.T, ((0,0),(0,n-t.shape[0]))) * PACK).astype(jnp.int32)
        w = w.reshape(heads, 2, n//256, 1, 128)
        w = (w[:,1] << 16) | (w[:,0] & 65535)
        return jnp.broadcast_to(w, (heads, n//256, 8, 128))
    vm = pl.BlockSpec(memory_space=pltpu.VMEM)
    return pl.pallas_call(gather_kernel,
        out_shape=(jax.ShapeDtypeStruct((heads,256,256), F32), jax.ShapeDtypeStruct((heads,SEQ,SEQ), F32)),
        in_specs=[vm]*4, out_specs=(vm, vm), name="bias_gather",
        compiler_params=pltpu.CompilerParams(vmem_limit_bytes=24<<20))(chunks(table_low), chunks(table_high), idx_lo, idx_hi)


def local(
    hidden,
    first_gain,
    first_shift,
    query_weight,
    query_bias,
    key_weight,
    value_weight,
    value_bias,
    output_weight,
    output_bias,
    first_scale,
    second_gain,
    second_shift,
    expand_weight,
    expand_bias,
    reduce_weight,
    reduce_bias,
    second_scale,
    table_low,
    table_high,
    resolution,
    counts,
    index_low,
    index_high,
    cotangent,
):
    floating = jnp.float32
    bfloat = jnp.bfloat16
    tensor_size = lax.axis_size("tensor")
    rows_dev = hidden.shape[0]
    group_rows = rows_dev * tensor_size
    heads_dev = table_low.shape[1]
    head_scale = HD ** (-0.5)
    slot_limits = jnp.where(resolution == 1, P_HI, P_LO)
    row_ids = lax.axis_index("tensor") * rows_dev + jnp.arange(rows_dev)
    row_slots = row_ids // SEQ
    picker = row_slots[:, None] == jnp.arange(SLOTS)[None, :]
    row_limits = jnp.sum(jnp.where(picker, slot_limits[None, :], 0), axis=1)
    live_rows = ((row_ids % SEQ < row_limits) & (row_slots < counts[0])).astype(floating)[:, None]
    residual = hidden.astype(floating)
    normed_one, scaled_one, inverse_one = normalize(residual, first_gain, first_shift)
    gathered_one = lax.all_gather(normed_one.astype(bfloat), "tensor", axis=0, tiled=True)
    queries = (
        (jnp.dot(gathered_one, query_weight, preferred_element_type=floating) + query_bias)
        * head_scale
    ).astype(bfloat)
    keys = jnp.dot(gathered_one, key_weight, preferred_element_type=floating).astype(bfloat)
    values = (
        jnp.dot(gathered_one, value_weight, preferred_element_type=floating) + value_bias
    ).astype(bfloat)
    index_low_pad = jnp.pad(index_low, ((0, 256 - P_LO), (0, 256 - P_LO)))
    index_high_pad = jnp.pad(index_high, ((0, 592 - P_HI), (0, SEQ - P_HI)))
    bias_low, bias_high = gather_maps(table_low, table_high, index_low_pad, index_high_pad)
    mixture_rows, attention = attend(resolution, queries, keys, values, bias_low, bias_high)
    attn_out = (
        lax.psum_scatter(
            jnp.dot(mixture_rows, output_weight, preferred_element_type=floating).astype(
                jnp.bfloat16
            ),
            "tensor",
            scatter_dimension=0,
            tiled=True,
        ).astype(jnp.float32)
        + output_bias
    )
    after_attn = residual + first_scale * attn_out
    normed_two, scaled_two, inverse_two = normalize(after_attn, second_gain, second_shift)
    normed_two_low = normed_two.astype(bfloat)
    gathered_two = lax.all_gather(normed_two_low, "tensor", axis=0, tiled=True)
    pre_act = jnp.dot(gathered_two, expand_weight, preferred_element_type=floating) + expand_bias
    activated = gelu_value(pre_act).astype(bfloat)
    mlp_out = (
        lax.psum_scatter(
            jnp.dot(activated, reduce_weight, preferred_element_type=floating).astype(jnp.bfloat16),
            "tensor",
            scatter_dimension=0,
            tiled=True,
        ).astype(jnp.float32)
        + reduce_bias
    )
    result = ((after_attn + second_scale * mlp_out) * live_rows).astype(bfloat)
    upstream = cotangent.astype(floating) * live_rows
    second_scale_grad = jnp.sum(upstream * mlp_out, axis=0)
    mlp_grad = upstream * second_scale
    reduce_bias_grad = jnp.sum(mlp_grad, axis=0)
    mlp_grad_low = mlp_grad.astype(bfloat)
    gathered_mlp_grad = lax.all_gather(mlp_grad_low, "tensor", axis=0, tiled=True)
    reduce_weight_grad = jnp.einsum(
        "rf,rd->fd", activated, gathered_mlp_grad, preferred_element_type=floating
    )
    act_grad = jnp.einsum(
        "rd,fd->rf", gathered_mlp_grad, reduce_weight, preferred_element_type=floating
    )
    pre_grad = act_grad * gelu_slope(pre_act)
    expand_bias_grad = jnp.sum(pre_grad, axis=0)
    pre_grad_low = pre_grad.astype(bfloat)
    expand_weight_grad = jnp.einsum(
        "rd,rf->df", gathered_two, pre_grad_low, preferred_element_type=floating
    )
    normed_two_grad = lax.psum_scatter(
        jnp.einsum(
            "rf,df->rd", pre_grad_low, expand_weight, preferred_element_type=floating
        ).astype(jnp.bfloat16),
        "tensor",
        scatter_dimension=0,
        tiled=True,
    ).astype(jnp.float32)
    second_gain_grad = jnp.sum(normed_two_grad * scaled_two, axis=0)
    second_shift_grad = jnp.sum(normed_two_grad, axis=0)
    after_grad = upstream + normalize_back(normed_two_grad, scaled_two, inverse_two, second_gain)
    first_scale_grad = jnp.sum(after_grad * attn_out, axis=0)
    attn_grad = after_grad * first_scale
    output_bias_grad = jnp.sum(attn_grad, axis=0)
    gathered_attn_grad = lax.all_gather(attn_grad.astype(bfloat), "tensor", axis=0, tiled=True)
    output_weight_grad = jnp.einsum(
        "rc,rd->cd", mixture_rows, gathered_attn_grad, preferred_element_type=floating
    )
    mixture_grad = jnp.einsum(
        "rd,cd->rc", gathered_attn_grad, output_weight, preferred_element_type=floating
    ).astype(bfloat)

    (
        query_low,
        key_low,
        value_low,
        query_bias_grad,
        value_bias_grad,
        table_low_grad,
        table_high_grad,
    ) = attend_back(
        resolution,
        queries,
        keys,
        values,
        attention,
        mixture_grad,
        index_low_pad,
        index_high_pad,
        table_low.shape[0],
        table_high.shape[0],
        head_scale,
    )
    query_weight_grad = jnp.einsum(
        "rd,rc->dc", gathered_one, query_low, preferred_element_type=floating
    )
    key_weight_grad = jnp.einsum(
        "rd,rc->dc", gathered_one, key_low, preferred_element_type=floating
    )
    value_weight_grad = jnp.einsum(
        "rd,rc->dc", gathered_one, value_low, preferred_element_type=floating
    )
    part_query = jnp.einsum("rc,dc->rd", query_low, query_weight, preferred_element_type=floating)
    part_key = jnp.einsum("rc,dc->rd", key_low, key_weight, preferred_element_type=floating)
    part_value = jnp.einsum("rc,dc->rd", value_low, value_weight, preferred_element_type=floating)
    normed_one_grad = lax.psum_scatter(
        (part_query + part_key + part_value).astype(jnp.bfloat16),
        "tensor",
        scatter_dimension=0,
        tiled=True,
    ).astype(jnp.float32)
    first_gain_grad = jnp.sum(normed_one_grad * scaled_one, axis=0)
    first_shift_grad = jnp.sum(normed_one_grad, axis=0)
    hidden_grad = after_grad + normalize_back(normed_one_grad, scaled_one, inverse_one, first_gain)
    (
        query_weight_grad,
        query_bias_grad,
        key_weight_grad,
        value_weight_grad,
        value_bias_grad,
        output_weight_grad,
        table_low_grad,
        table_high_grad,
        expand_weight_grad,
        expand_bias_grad,
        reduce_weight_grad,
    ) = lax.psum(
        (
            query_weight_grad,
            query_bias_grad,
            key_weight_grad,
            value_weight_grad,
            value_bias_grad,
            output_weight_grad,
            table_low_grad,
            table_high_grad,
            expand_weight_grad,
            expand_bias_grad,
            reduce_weight_grad,
        ),
        "dp",
    )
    (
        first_gain_grad,
        first_shift_grad,
        first_scale_grad,
        output_bias_grad,
        second_gain_grad,
        second_shift_grad,
        second_scale_grad,
        reduce_bias_grad,
    ) = lax.psum(
        (
            first_gain_grad,
            first_shift_grad,
            first_scale_grad,
            output_bias_grad,
            second_gain_grad,
            second_shift_grad,
            second_scale_grad,
            reduce_bias_grad,
        ),
        ("dp", "tensor"),
    )
    return (
        result,
        hidden_grad,
        first_gain_grad,
        first_shift_grad,
        query_weight_grad,
        query_bias_grad,
        key_weight_grad,
        value_weight_grad,
        value_bias_grad,
        output_weight_grad,
        output_bias_grad,
        first_scale_grad,
        second_gain_grad,
        second_shift_grad,
        expand_weight_grad,
        expand_bias_grad,
        reduce_weight_grad,
        reduce_bias_grad,
        second_scale_grad,
        table_low_grad,
        table_high_grad,
    )


def solution(mesh):
    in_specs = (
        P(("dp", "tensor"), None),
        P(),
        P(),
        P(None, "tensor"),
        P("tensor"),
        P(None, "tensor"),
        P(None, "tensor"),
        P("tensor"),
        P("tensor", None),
        P(),
        P(),
        P(),
        P(),
        P(None, "tensor"),
        P("tensor"),
        P("tensor", None),
        P(),
        P(),
        P(None, "tensor"),
        P(None, "tensor"),
        P("dp"),
        P("dp"),
        P(),
        P(),
        P(("dp", "tensor"), None),
    )
    out_specs = (
        P(("dp", "tensor"), None),
        P(("dp", "tensor"), None),
        P(),
        P(),
        P(None, "tensor"),
        P("tensor"),
        P(None, "tensor"),
        P(None, "tensor"),
        P("tensor"),
        P("tensor", None),
        P(),
        P(),
        P(),
        P(),
        P(None, "tensor"),
        P("tensor"),
        P("tensor", None),
        P(),
        P(),
        P(None, "tensor"),
        P(None, "tensor"),
    )
    return jax.shard_map(local, mesh=mesh, in_specs=in_specs, out_specs=out_specs, check_vma=False)
```

```python
import functools

import jax
import jax.numpy as jnp
from jax import lax
from jax.experimental import pallas as pl
from jax.experimental.pallas import tpu as pltpu
from jax.sharding import PartitionSpec as P

HD = 64
P_LO = 197
P_HI = 577
SEQ = 640
SLOTS = 2


eps_norm = 1e-06
masked_score = -1e30
inv_sqrt_two = 0.7071067811865476
inv_sqrt_two_pi = 0.3989422804014327


def normalize(values, gain, shift):
    center = jnp.mean(values, axis=-1, keepdims=True)
    centered = values - center
    variance = jnp.mean(centered * centered, axis=-1, keepdims=True)
    inverse = lax.rsqrt(variance + eps_norm)
    return centered * inverse * gain + shift


F32=jnp.float32; BF=jnp.bfloat16
NT=(((1,),(1,)),((),()))
def head_mask(h, width):
    lane = lax.broadcasted_iota(jnp.int32, (1, width), 1)
    return ((lane >= h*HD) & (lane < (h+1)*HD)).astype(F32).astype(BF)

def row(ref):
    return ref[...].reshape(1, ref.shape[0])

def live_of(t, rows, res, counts):
    slot = t * rows // SEQ
    first = t * rows - slot * SEQ
    limit = jnp.where(res[slot] == 1, P_HI, P_LO)
    limit = jnp.where(slot < counts[0], limit, 0)
    place = lax.broadcasted_iota(jnp.int32, (rows, 1), 0) + first
    return jnp.where(place < limit, 1.0, 0.0).astype(F32)

def moments(values):
    center = jnp.mean(values, axis=1, keepdims=True)
    centered = values - center
    inverse = lax.rsqrt(jnp.mean(centered * centered, axis=1, keepdims=True) + eps_norm)
    return centered * inverse, inverse


BB=32; UN=16
def scatter_run(idx_ref, g_ref, out, first, last, fresh):
    heads = g_ref.shape[0]; na = out.shape[1]; m = idx_ref.shape[1]
    if fresh:
        out[...] = jnp.zeros_like(out)
    ib = lax.broadcasted_iota(jnp.int32, (16, m), 0).astype(F32)
    def body(r, c):
        ms = []; os = []
        for u in range(UN):
            row = r*UN+u
            idx = jnp.broadcast_to(idx_ref[pl.ds(row,1), :], (16, m))
            ia = (idx >> 5).astype(F32).astype(BF); il = (idx & 31).astype(F32).astype(BF)
            g = [jnp.broadcast_to(g_ref[h, pl.ds(row,1), :], (16, m)).astype(BF) for h in range(heads)]
            hits = [il == (ib + 16.0*k).astype(BF) for k in range(BB//16)]
            ms.append(jnp.concatenate([jnp.where(hits[k], g[h], jnp.zeros_like(g[h])) for h in range(heads) for k in range(BB//16)], axis=0))
            os.append(jnp.concatenate([jnp.where(ia == (ib + 16.0*k).astype(BF), jnp.ones_like(ia), jnp.zeros_like(ia)) for k in range(na//16)], axis=0))
        out[...] += lax.dot_general(jnp.concatenate(ms, axis=1), jnp.concatenate(os, axis=1), NT, preferred_element_type=F32)
        return c
    lax.fori_loop(first, last, body, 0)

PACK=8191.0
def gather_kernel(res, tab_lo, tab_hi, idx_lo, idx_hi, out):
    heads = out.shape[1]
    slots = out.shape[0]
    def fill(code, tab, idx_ref, rows, limit):
        nch = tab.shape[1]
        ncol = idx_ref.shape[1]//128
        def body(r, c):
            rws = pl.ds(pl.multiple_of(r*8, 8), 8)
            vals = []
            for j in range(ncol):
                idx = idx_ref[rws, pl.ds(j*128, 128)]
                lane = idx & 127
                ch = idx >> 7
                shift = jnp.where(ch >= nch, 0, 16)
                ch = jnp.where(ch >= nch, ch - nch, ch)
                acc = [None]*heads
                for k in range(nch):
                    hit = ch == k
                    for h in range(heads):
                        v = jnp.take_along_axis(tab[h, k], lane, axis=1)
                        acc[h] = v if k == 0 else jnp.where(hit, v, acc[h])
                for h in range(heads):
                    val = ((acc[h] << shift) >> 16).astype(F32) * (1.0/PACK)
                    if (j+1)*128 > limit:
                        col = lax.broadcasted_iota(jnp.int32, (8,128), 1) + j*128
                        val = jnp.where(col < limit, val, masked_score)
                    vals.append((h, j, val))
            for s in range(slots):
                @pl.when(res[s] == code)
                def _():
                    for h, j, val in vals:
                        out[s, h, rws, pl.ds(j*128, 128)] = val
            return c
        lax.fori_loop(0, -(-rows//8), body, 0)
    for s in range(slots):
        @pl.when(res[s] == 1)
        def _():
            out[s, :, 584:, :] = jnp.zeros((heads, SEQ-584, SEQ), F32)
        @pl.when(res[s] != 1)
        def _():
            out[s] = jnp.full((heads, SEQ, SEQ), masked_score, F32)
    low = res[0] != 1
    high = res[0] == 1
    for s in range(1, slots):
        low = low | (res[s] != 1)
        high = high | (res[s] == 1)
    @pl.when(low)
    def _(): fill(0, tab_lo, idx_lo, P_LO, P_LO)
    @pl.when(high)
    def _(): fill(1, tab_hi, idx_hi, P_HI, P_HI)

def gather_maps(res, table_low, table_high, idx_lo, idx_hi):
    heads = table_low.shape[1]
    def chunks(t):
        n = -(-t.shape[0]//256)*256
        w = jnp.round(jnp.pad(t.T, ((0,0),(0,n-t.shape[0]))) * PACK).astype(jnp.int32)
        w = w.reshape(heads, 2, n//256, 1, 128)
        w = (w[:,1] << 16) | (w[:,0] & 65535)
        return jnp.broadcast_to(w, (heads, n//256, 8, 128))
    vm = pl.BlockSpec(memory_space=pltpu.VMEM)
    return pl.pallas_call(gather_kernel,
        out_shape=jax.ShapeDtypeStruct((SLOTS,heads,SEQ,SEQ), F32),
        in_specs=[pl.BlockSpec(memory_space=pltpu.SMEM)]+[vm]*4, out_specs=vm, name="bias_gather", cost_estimate=pl.CostEstimate(flops=20*10**9, bytes_accessed=8*10**6, transcendentals=0),
        compiler_params=pltpu.CompilerParams(vmem_limit_bytes=24<<20))(res, chunks(table_low), chunks(table_high), idx_lo, idx_hi)

MESH = pl.DeviceIdType.MESH
TN=(((0,),(0,)),((),()))

def middle_kernel(scale, res, counts, g1, wq, bq, wk, wv, bv, bias, wo, bo, resid, scale1, gain2, shift2, we, be, wr, cot, scale2,
                  q_out, k_out, v_out, mix, p_out, part, ga, dmix, x0, x1, after_attn, after_grad, sums, esum,
                  upstream, gm, gt, act, pgl, acc, xhat, inv2, attn,
                  cbuf, ccore, xbuf, xin, m_s, m_r, t_s, t_r, a_s, a_r, o_s, o_r, n_s, n_r):
    d = lax.axis_index("dp")
    t = lax.axis_index("tensor")
    rows = resid.shape[0]
    half = rows // 2
    heads = p_out.shape[1]
    width = q_out.shape[1]
    sibling = t + 1 - 2 * lax.rem(t, 2)
    cross = lax.rem(t + 2, 4)
    diag = 3 - t
    barrier = pltpu.get_barrier_semaphore()
    for k in range(1, 4):
        pl.semaphore_signal(barrier, inc=1, device_id=(d, lax.rem(t + k, 4)), device_id_type=MESH)
    pl.semaphore_wait(barrier, 3)

    def remote(src, dst, send, recv, who):
        return pltpu.make_async_remote_copy(src_ref=src, dst_ref=dst, send_sem=send, recv_sem=recv, device_id=(d, who), device_id_type=MESH)
    def span(who, h):
        return pl.ds(pl.multiple_of(who * rows + h * half, 16), half)
    def gather_x(buf, send, recv, h):
        here = buf.at[span(t, h)]
        return remote(here, here, send.at[h], recv.at[h], cross)
    def gather_near(buf, send, recv, h):
        here = buf.at[span(t, h)]
        return remote(here, here, send.at[2 + h], recv.at[2 + h], sibling)
    def gather_on(buf, send, recv, h):
        here = buf.at[span(cross, h)]
        return remote(here, here, send.at[4 + h], recv.at[4 + h], sibling)
    def sum_far(j, send, recv, h):
        return remote(cbuf.at[j, 0, h], ccore.at[j, 0, h], send.at[h], recv.at[h], sibling)
    def sum_near(j, send, recv, h):
        return remote(cbuf.at[j, 1, h], ccore.at[j, 1, h], send.at[2 + h], recv.at[2 + h], sibling)
    def sum_x(j, send, recv, h):
        return remote(xbuf.at[j, h], xin.at[j, h], send.at[4 + h], recv.at[4 + h], cross)

    upstream[...] = cot[...].astype(F32) * live_of(t, rows, res, counts)
    gm[pl.ds(pl.multiple_of(t * rows, 16), rows)] = (upstream[...] * row(scale2)).astype(BF)
    for h in range(2):
        gather_x(gm, m_s, m_r, h).start()
        gather_near(gm, m_s, m_r, h).start()
    def project(i, c):
        here = pl.ds(pl.multiple_of(i * rows, 16), rows)
        g = g1[here]
        q_out[here] = ((lax.dot_general(g, wq[...], NT, preferred_element_type=F32) + row(bq)) * scale).astype(BF)
        k_out[here] = lax.dot_general(g, wk[...], NT, preferred_element_type=F32).astype(BF)
        v_out[here] = (lax.dot_general(g, wv[...], NT, preferred_element_type=F32) + row(bv)).astype(BF)
        return c
    lax.fori_loop(0, 4, project, 0)

    def attend_image(slot):
        here = pl.ds(pl.multiple_of(slot * SEQ, 16), SEQ)
        k = k_out[here]
        v = v_out[here]
        vm = [v * head_mask(h, width) for h in range(heads)]
        def piece(i, c):
            first = pl.multiple_of(i * rows, 16)
            q = q_out[pl.ds(pl.multiple_of(slot * SEQ + first, 16), rows)]
            out = jnp.zeros((rows, width), F32)
            for h in range(heads):
                s = lax.dot_general(q * head_mask(h, width), k, NT, preferred_element_type=F32)
                s = s + bias[slot, h, pl.ds(first, rows)]
                peak = jnp.max(s, axis=1, keepdims=True)
                e = jnp.exp(s - peak)
                total = jnp.sum(e, axis=1, keepdims=True)
                p = (e * (1.0 / total)).astype(BF)
                p_out[slot, h, pl.ds(first, rows)] = p
                out = out + jnp.dot(p, vm[h], preferred_element_type=F32)
            mix[pl.ds(pl.multiple_of(slot * SEQ + first, 16), rows)] = out.astype(BF)
            return c
        lax.fori_loop(0, SEQ // rows, piece, 0)
    def output_of(who, h):
        return jnp.dot(mix[span(who, h)], wo[...], preferred_element_type=F32)

    mine = t // 2
    attend_image(1 - mine)
    for h in range(2):
        cbuf[0, 0, h] = output_of(diag, h).astype(BF)
        sum_far(0, o_s, o_r, h).start()
    for h in range(2):
        total = output_of(cross, h)
        sum_far(0, o_s, o_r, h).wait()
        xbuf[0, h] = (total + ccore[0, 0, h].astype(F32)).astype(BF)
        sum_x(0, o_s, o_r, h).start()
    attend_image(mine)
    for h in range(2):
        cbuf[0, 1, h] = output_of(sibling, h).astype(BF)
        sum_near(0, o_s, o_r, h).start()
    for h in range(2):
        acc[pl.ds(h * half, half)] = output_of(t, h)
    for h in range(2):
        gather_x(gm, m_s, m_r, h).wait()
        gather_on(gm, m_s, m_r, h).start()
    for h in range(2):
        here = pl.ds(h * half, half)
        sum_near(0, o_s, o_r, h).wait()
        sum_x(0, o_s, o_r, h).wait()
        out = acc[here] + ccore[0, 1, h].astype(F32) + xin[0, h].astype(F32) + row(bo)
        attn[here] = out
        after = resid[here].astype(F32) + row(scale1) * out
        after_attn[here] = after
        center = jnp.mean(after, axis=1, keepdims=True)
        centered = after - center
        inverse = lax.rsqrt(jnp.mean(centered * centered, axis=1, keepdims=True) + eps_norm)
        scaled = centered * inverse
        xhat[here] = scaled
        inv2[here] = inverse
        gt[span(t, h)] = (scaled * row(gain2) + row(shift2)).astype(BF)
        gather_x(gt, t_s, t_r, h).start()
        gather_near(gt, t_s, t_r, h).start()

    esum[...] = jnp.zeros_like(esum)
    def feed(who, h):
        here = span(who, h)
        pre = jnp.dot(gt[here], we[...], preferred_element_type=F32) + row(be)
        grad = lax.dot_general(gm[here], wr[...], NT, preferred_element_type=F32)
        phi = 0.5 * (1.0 + lax.erf(pre * inv_sqrt_two))
        active = (pre * phi).astype(BF)
        act[here] = active
        grad = grad * (phi + pre * inv_sqrt_two_pi * jnp.exp(-0.5 * pre * pre))
        esum[...] += jnp.sum(grad, axis=0, keepdims=True)
        grad = grad.astype(BF)
        pgl[here] = grad
        part[here] = jnp.dot(active, wr[...], preferred_element_type=F32).astype(BF)
        return lax.dot_general(grad, we[...], NT, preferred_element_type=F32)
    def feed_own(h, c):
        acc[pl.ds(pl.multiple_of(h * half, 16), half)] = feed(t, h)
        return c
    lax.fori_loop(0, 2, feed_own, 0)
    for h in range(2):
        gather_near(gm, m_s, m_r, h).wait()
        gather_near(gt, t_s, t_r, h).wait()
    gather_x(gt, t_s, t_r, 0).wait()
    gather_on(gt, t_s, t_r, 0).start()
    def feed_near(h, c):
        cbuf[1, 1, h] = feed(sibling, h).astype(BF)
        return c
    lax.fori_loop(0, 2, feed_near, 0)
    for h in range(2):
        sum_near(1, n_s, n_r, h).start()
    gather_x(gt, t_s, t_r, 1).wait()
    gather_on(gt, t_s, t_r, 1).start()
    for h in range(2):
        gather_on(gm, m_s, m_r, h).wait()
        gather_on(gt, t_s, t_r, h).wait()
    def feed_far(h, c):
        cbuf[1, 0, h] = feed(diag, h).astype(BF)
        sum_far(1, n_s, n_r, h).start()
        total = feed(cross, h)
        sum_far(1, n_s, n_r, h).wait()
        xbuf[1, h] = (total + ccore[1, 0, h].astype(F32)).astype(BF)
        sum_x(1, n_s, n_r, h).start()
        return c
    lax.fori_loop(0, 2, feed_far, 0)

    tile = 128
    def reduce_grad(i, c):
        cols = pl.ds(pl.multiple_of(i * tile, tile), tile)
        x0[cols] = lax.dot_general(act[:, cols], gm[...], TN, preferred_element_type=F32).astype(BF)
        return c
    lax.fori_loop(0, act.shape[1] // tile, reduce_grad, 0)

    sums[...] = jnp.zeros_like(sums)
    for h in range(2):
        here = pl.ds(h * half, half)
        sum_near(1, n_s, n_r, h).wait()
        sum_x(1, n_s, n_r, h).wait()
        grad = acc[here] + ccore[1, 1, h].astype(F32) + xin[1, h].astype(F32)
        scaled = xhat[here]
        up = upstream[here]
        inner = grad * row(gain2)
        mean_inner = jnp.mean(inner, axis=1, keepdims=True)
        mean_mixed = jnp.mean(inner * scaled, axis=1, keepdims=True)
        after = up + inv2[here] * (inner - mean_inner - scaled * mean_mixed)
        after_grad[here] = after
        agrad = after * row(scale1)
        ga[span(t, h)] = agrad.astype(BF)
        gather_x(ga, a_s, a_r, h).start()
        gather_near(ga, a_s, a_r, h).start()
        sums[2:3, :] += jnp.sum(after * attn[here], axis=0, keepdims=True)
        sums[3:4, :] += jnp.sum(agrad, axis=0, keepdims=True)
        sums[4:5, :] += jnp.sum(grad * scaled, axis=0, keepdims=True)
        sums[5:6, :] += jnp.sum(grad, axis=0, keepdims=True)

    def expand_grad(i, c):
        cols = pl.ds(pl.multiple_of(i * tile, tile), tile)
        x1[cols] = lax.dot_general(gt[:, cols], pgl[...], TN, preferred_element_type=F32).astype(BF)
        return c
    def mixture_of(who):
        here = pl.ds(pl.multiple_of(who * rows, 16), rows)
        dmix[here] = lax.dot_general(ga[here], wo[...], NT, preferred_element_type=F32).astype(BF)
    count = gt.shape[1] // tile
    lax.fori_loop(0, count // 2, expand_grad, 0)
    gather_x(ga, a_s, a_r, 0).wait()
    gather_on(ga, a_s, a_r, 0).start()
    lax.fori_loop(count // 2, count, expand_grad, 0)
    mixture_of(t)
    for h in range(2):
        gather_near(ga, a_s, a_r, h).wait()
    mixture_of(sibling)
    gather_x(ga, a_s, a_r, 1).wait()
    gather_on(ga, a_s, a_r, 1).start()
    mixture_of(cross)
    for h in range(2):
        gather_on(ga, a_s, a_r, h).wait()
    mixture_of(diag)

def middle(scale, res, counts, g1, wq, bq, wk, wv, bv, bias, wo, bo, resid, scale1, gain2, shift2, we, be, wr, cot, scale2, cid):
    total, model = g1.shape
    rows = resid.shape[0]
    half = rows // 2
    width = wq.shape[0]
    hidden = we.shape[1]
    slots, heads = bias.shape[:2]
    vm = pl.BlockSpec(memory_space=pltpu.VMEM)
    sm = pl.BlockSpec(memory_space=pltpu.SMEM)
    dma = pltpu.SemaphoreType.DMA
    V = pltpu.VMEM
    S = jax.ShapeDtypeStruct
    operands = (g1, wq, bq, wk, wv, bv, bias, wo, bo, resid, scale1, gain2, shift2, we, be, wr, cot, scale2)
    shapes = (S((total, width), BF),) * 3 + (S((total, width), BF), S((slots, heads, SEQ, SEQ), BF), S((total, model), BF), S((total, model), BF),
        S((total, width), BF), S((hidden, model), BF), S((model, hidden), BF), S((rows, model), F32), S((rows, model), F32), S((8, model), F32), S((1, hidden), F32))
    return pl.pallas_call(functools.partial(middle_kernel, scale),
        out_shape=shapes, in_specs=[sm, sm] + [vm] * len(operands), out_specs=(vm,) * len(shapes),
        scratch_shapes=[V((rows, model), F32), V((total, model), BF), V((total, model), BF), V((total, hidden), BF), V((total, hidden), BF),
            V((rows, model), F32), V((rows, model), F32), V((rows, 1), F32), V((rows, model), F32),
            V((2, 2, 2, half, model), BF), V((2, 2, 2, half, model), BF), V((2, 2, half, model), BF), V((2, 2, half, model), BF)]
            + [dma((6,))] * 10,
        name="middle", cost_estimate=pl.CostEstimate(flops=60 * 10**9, bytes_accessed=60 * 10**6, transcendentals=0),
        compiler_params=pltpu.CompilerParams(collective_id=cid, has_side_effects=True, vmem_limit_bytes=60 << 20))(res, counts, *operands)

CHUNKS = 6

def tail_kernel(rows, scale, sums, res, counts, x0, x1, q_ref, k_ref, v_ref, p_ref, d_ref, g1, mix, ga, ilo, ihi, wq, wk, wv, resid, after_grad, gain,
                part, after_attn, cot, rbias, scale2, wide_in, expand_sum,
                o0, o1, o2, result, hidden_grad, wide, slim, tables,
                dq, dk, dv, glo, ghi, x2, ybuf, pbuf, zbuf, tbuf, abuf, acore, across, bcore, bcross,
                tlo, thi, wmine, wmid, smine, wten, wdp, sdp, tdp,
                y_s, y_r, z_s, z_r, g_s, g_r, e_s, e_r, r_s, r_r, w_s, w_r, v_s, v_r):
    d = lax.axis_index("dp")
    t = lax.axis_index("tensor")
    col = d // 2
    side = lax.rem(d, 2)
    sibling = t + 1 - 2 * lax.rem(t, 2)
    cross = lax.rem(t + 2, 4)
    diag = 3 - t
    neighbour = d + 1 - 2 * side
    heads = p_ref.shape[1]
    width = q_ref.shape[1]
    barrier = pltpu.get_barrier_semaphore()
    for k in range(1, 4):
        pl.semaphore_signal(barrier, inc=1, device_id=(d, lax.rem(t + k, 4)), device_id_type=MESH)
    if sums:
        for k in range(1, 8):
            pl.semaphore_signal(barrier, inc=1, device_id=(lax.rem(d + k, 8), t), device_id_type=MESH)
    pl.semaphore_wait(barrier, 10 if sums else 3)

    def remote(src, dst, send, recv, device):
        return pltpu.make_async_remote_copy(src_ref=src, dst_ref=dst, send_sem=send, recv_sem=recv, device_id=device, device_id_type=MESH)

    arrays = (x0, x1, x2)
    outs = (o0, o1, o2)
    size = 384
    half = size // 2
    block = half // 4
    def at(n, start, count):
        return pl.ds(pl.multiple_of((n % 2) * size + start, 16), count)
    def y_copy(n):
        return remote(arrays[n // 2].at[at(n, (1 - side) * half, half)], ybuf.at[n], y_s.at[n], y_r.at[n], (neighbour, t))
    def z_copy(n, k):
        to = lax.rem(col + k, 4)
        return remote(pbuf.at[n, pl.ds(pl.multiple_of(to * block, 16), block)], zbuf.at[n, k], z_s.at[n, k], z_r.at[n, k], (to * 2 + side, t))
    def g_copy(n, k):
        to = lax.rem(col + k, 4)
        return remote(tbuf.at[n], outs[n // 2].at[at(n, side * half + col * block, block)], g_s.at[n, k], g_r.at[n, k], (to * 2 + side, t))
    def e_copy(n):
        here = outs[n // 2].at[at(n, side * half, half)]
        return remote(here, here, e_s.at[n], e_r.at[n], (neighbour, t))
    def step_a(n):
        y_copy(n).wait()
        if n + 2 < CHUNKS:
            y_copy(n + 2).start()
        pbuf[n] = (arrays[n // 2][at(n, side * half, half)].astype(F32) + ybuf[n].astype(F32)).astype(BF)
        for k in range(1, 4):
            z_copy(n, k).start()
    def step_b(n):
        for k in range(1, 4):
            z_copy(n, k).wait()
        total = pbuf[n, pl.ds(pl.multiple_of(col * block, 16), block)].astype(F32)
        for k in range(1, 4):
            total = total + zbuf[n, k].astype(F32)
        total = total.astype(BF)
        tbuf[n] = total
        outs[n // 2][at(n, side * half + col * block, block)] = total
    def step_c(n):
        for k in range(1, 4):
            g_copy(n, k).start()
    def step_d(n):
        for k in range(1, 4):
            g_copy(n, k).wait()
        e_copy(n).start()

    if not sums:
        step_a = step_b = step_c = step_d = lambda n: None
    else:
        y_copy(0).start()
        y_copy(1).start()

    smine[...] = jnp.zeros_like(smine)
    smine[2:3, :] = expand_sum[...]
    def attention_back(slot):
        here = slice(slot * SEQ, (slot + 1) * SEQ)
        k = k_ref[here]
        v = v_ref[here]
        dd = d_ref[here]
        qt = q_ref[here].T
        dt = dd.T
        is_high = jnp.where(res[slot] == 1, 1.0, 0.0).astype(F32)
        out = jnp.zeros((SEQ, width), F32)
        dks = []
        dvs = []
        nh = ghi.shape[1]
        nl, ml = glo.shape[1:]
        for h in range(heads):
            mask = head_mask(h, width)
            p = p_ref[slot, h]
            dp = lax.dot_general(dd * mask, v, NT, preferred_element_type=F32)
            pf = p.astype(F32)
            m = pf * dp
            ds = m - pf * jnp.sum(m, axis=1, keepdims=True)
            if slot == 0:
                ghi[h] = ds[:nh] * is_high
                glo[h] = ds[:nl, :ml] * (1.0 - is_high)
            else:
                ghi[h] += ds[:nh] * is_high
                glo[h] += ds[:nl, :ml] * (1.0 - is_high)
            low = ds.astype(BF)
            out = out + jnp.dot(low, k * mask, preferred_element_type=F32)
            dks.append(jnp.dot(qt[h*HD:(h+1)*HD], low, preferred_element_type=F32))
            dvs.append(jnp.dot(dt[h*HD:(h+1)*HD], p, preferred_element_type=F32))
        out = out * scale
        smine[0:1, 0:width] += jnp.sum(out, axis=0, keepdims=True)
        dq[here] = out.astype(BF)
        dk[here] = jnp.concatenate(dks, axis=0).T.astype(BF)
        out = jnp.concatenate(dvs, axis=0).T
        smine[1:2, 0:width] += jnp.sum(out, axis=0, keepdims=True)
        dv[here] = out.astype(BF)
    attention_back(0)
    step_a(0)
    attention_back(1)
    step_a(1)

    def rows_of(ref, who):
        return ref[pl.ds(pl.multiple_of(who * rows, 16), rows)]
    def back(who):
        total = jnp.dot(rows_of(dq, who), wq[...], preferred_element_type=F32)
        total = total + jnp.dot(rows_of(dk, who), wk[...], preferred_element_type=F32)
        return total + jnp.dot(rows_of(dv, who), wv[...], preferred_element_type=F32)
    a_far = remote(abuf.at[0], acore.at[0], r_s.at[0], r_r.at[0], (d, sibling))
    a_near = remote(abuf.at[1], acore.at[1], r_s.at[1], r_r.at[1], (d, sibling))
    a_cross = remote(abuf.at[2], across, r_s.at[2], r_r.at[2], (d, cross))
    b_far = remote(part.at[pl.ds(pl.multiple_of(diag * rows, 16), rows)], bcore.at[0], r_s.at[3], r_r.at[3], (d, sibling))
    b_near = remote(part.at[pl.ds(pl.multiple_of(sibling * rows, 16), rows)], bcore.at[1], r_s.at[4], r_r.at[4], (d, sibling))
    b_cross = remote(abuf.at[3], bcross, r_s.at[5], r_r.at[5], (d, cross))
    abuf[0] = back(diag).astype(BF)
    a_far.start()
    b_far.start()
    total = back(cross)
    a_far.wait()
    abuf[2] = (total + acore[0].astype(F32)).astype(BF)
    a_cross.start()
    for j, (left, right) in enumerate(((dq, g1), (dk, g1), (dv, g1), (mix, ga))):
        x2[j * width:(j + 1) * width, :] = lax.dot_general(left[...], right[...], TN, preferred_element_type=F32).astype(BF)
    step_a(2)
    step_b(0)
    abuf[1] = back(sibling).astype(BF)
    a_near.start()
    b_near.start()
    total = back(t)
    a_near.wait()
    hidden_grad[...] = total + acore[1].astype(F32)
    b_far.wait()
    abuf[3] = (rows_of(part, cross).astype(F32) + bcore[0].astype(F32)).astype(BF)
    segments = 7
    n_hi = 592 // UN
    def scatter_part(s):
        lo, hi = n_hi * s // segments, n_hi * (s + 1) // segments
        scatter_run(ihi, ghi, thi, lo, hi, s == 0)
    scatter_part(0)
    step_a(3)
    step_b(1)
    a_cross.wait()
    b_cross.start()
    grad = hidden_grad[...] + across[...].astype(F32)
    xhat, inverse = moments(resid[...].astype(F32))
    wmine[...] = wide_in[...]
    wmine[0:1, :] = jnp.sum(grad * xhat, axis=0, keepdims=True)
    wmine[1:2, :] = jnp.sum(grad, axis=0, keepdims=True)
    inner = grad * row(gain)
    mean_inner = jnp.mean(inner, axis=1, keepdims=True)
    mean_mixed = jnp.mean(inner * xhat, axis=1, keepdims=True)
    hidden_grad[...] = after_grad[...] + inverse * (inner - mean_inner - xhat * mean_mixed)
    scatter_part(1)
    step_a(4)
    step_b(2)
    scatter_part(2)
    step_a(5)
    step_b(3)
    scatter_part(3)
    b_near.wait()
    b_cross.wait()
    out = rows_of(part, t).astype(F32) + bcore[1].astype(F32) + bcross[...].astype(F32) + row(rbias)
    alive = live_of(t, rows, res, counts)
    result[...] = ((after_attn[...] + row(scale2) * out) * alive).astype(BF)
    up = cot[...].astype(F32) * alive
    wmine[6:7, :] = jnp.sum(up * out, axis=0, keepdims=True)
    wmine[7:8, :] = jnp.sum(up * row(scale2), axis=0, keepdims=True)
    step_b(4)
    step_c(0)
    step_c(1)
    def w_copy(k):
        return remote(wmine, wten.at[k], w_s.at[k], w_r.at[k], (d, lax.rem(t + k, 4)))
    if sums:
        for k in range(1, 4):
            w_copy(k).start()
    scatter_part(4)
    step_b(5)
    scatter_part(5)
    step_d(0)
    step_c(2)
    scatter_part(6)
    step_d(1)
    step_c(3)
    scatter_run(ilo, glo, tlo, 0, 208 // UN, True)
    tables[...] = jnp.zeros_like(tables)
    n = tlo.shape[1]
    tables[:, 0:n] = tlo[...]
    tables[:, n:n + thi.shape[1]] = thi[...]
    tbl = tdp.at[0]
    tbl[...] = tables[...]
    total = wmine[...]
    if sums:
        for k in range(1, 4):
            w_copy(k).wait()
            total = total + wten[k]
    wmid[...] = total
    def v_copy(j, k):
        src, dst = ((wmid, wdp), (smine, sdp), (tbl, tdp))[j]
        return remote(src, dst.at[k], v_s.at[j, k], v_r.at[j, k], (lax.rem(d + k, 8), t))
    if sums:
        for k in range(1, 8):
            for j in range(3):
                v_copy(j, k).start()
    step_d(2)
    step_c(4)
    wide[...] = wmid[...]
    slim[...] = smine[...]
    step_d(3)
    step_c(5)
    if not sums:
        o0[...] = x0[...]
        o1[...] = x1[...]
        o2[...] = x2[...]
        return
    for k in range(1, 8):
        for j in range(3):
            v_copy(j, k).wait()
        wide[...] += wdp[k]
        slim[...] += sdp[k]
        tables[...] += tdp[k]
    step_d(4)
    step_d(5)
    for n in range(CHUNKS):
        e_copy(n).wait()

def tail(scale, sums, res, counts, x0, x1, q, k, v, p, dmix, g1, mix, ga, ilo, ihi, wq, wk, wv, resid, after_grad, gain, part, after_attn, cot, rbias, scale2, wide_in, expand_sum, n_lo, n_hi, cid):
    rows, model = after_grad.shape
    total, width = q.shape
    heads = p.shape[1]
    vm = pl.BlockSpec(memory_space=pltpu.VMEM)
    sm = pl.BlockSpec(memory_space=pltpu.SMEM)
    dma = pltpu.SemaphoreType.DMA
    operands = (x0, x1, q, k, v, p, dmix, g1, mix, ga, ilo, ihi, wq, wk, wv, resid, after_grad, gain, part, after_attn, cot, rbias, scale2, wide_in, expand_sum)
    tshape = (heads * BB, 128)
    V = pltpu.VMEM
    S = jax.ShapeDtypeStruct
    return pl.pallas_call(functools.partial(tail_kernel, rows, scale, sums),
        out_shape=(S((768, model), BF),) * 3 + (S((rows, model), BF), S((rows, model), F32), S((8, model), F32), S((8, model), F32), S(tshape, F32)),
        in_specs=[sm, sm] + [vm] * len(operands), out_specs=(vm,) * 8,
        scratch_shapes=[
            V((total, width), BF), V((total, width), BF), V((total, width), BF), V((heads,) + ilo.shape, F32), V((heads,) + ihi.shape, F32), V((4 * width, model), BF),
            V((CHUNKS, 192, model), BF), V((CHUNKS, 192, model), BF), V((CHUNKS, 4, 48, model), BF), V((CHUNKS, 48, model), BF),
            V((4, rows, model), BF), V((2, rows, model), BF), V((rows, model), BF), V((2, rows, model), BF), V((rows, model), BF),
            V((heads * BB, n_lo), F32), V((heads * BB, n_hi), F32),
            V((8, model), F32), V((8, model), F32), V((8, model), F32), V((4, 8, model), F32), V((8, 8, model), F32), V((8, 8, model), F32), V((8,) + tshape, F32),
            dma((CHUNKS,)), dma((CHUNKS,)), dma((CHUNKS, 4)), dma((CHUNKS, 4)), dma((CHUNKS, 4)), dma((CHUNKS, 4)), dma((CHUNKS,)), dma((CHUNKS,)),
            dma((6,)), dma((6,)), dma((4,)), dma((4,)), dma((3, 8)), dma((3, 8))],
        name="tail", cost_estimate=pl.CostEstimate(flops=50 * 10**9, bytes_accessed=60 * 10**6, transcendentals=0),
        compiler_params=pltpu.CompilerParams(collective_id=cid, has_side_effects=True, vmem_limit_bytes=60 << 20))(res, counts, *operands)


def local(
    hidden,
    first_gain,
    first_shift,
    query_weight,
    query_bias,
    key_weight,
    value_weight,
    value_bias,
    output_weight,
    output_bias,
    first_scale,
    second_gain,
    second_shift,
    expand_weight,
    expand_bias,
    reduce_weight,
    reduce_bias,
    second_scale,
    table_low,
    table_high,
    resolution,
    counts,
    index_low,
    index_high,
    cotangent,
):
    floating = jnp.float32
    heads_dev = table_low.shape[1]
    head_scale = HD ** (-0.5)
    normed_one = normalize(hidden.astype(floating), first_gain, first_shift)
    gathered_one = lax.all_gather(normed_one.astype(BF), "tensor", axis=0, tiled=True)
    index_low_pad = jnp.pad(index_low, ((0, 256 - P_LO), (0, 256 - P_LO)))
    index_high_pad = jnp.pad(index_high, ((0, 592 - P_HI), (0, SEQ - P_HI)))
    bias_map = gather_maps(resolution, table_low, table_high, index_low_pad, index_high_pad)
    (
        queries,
        keys,
        values,
        mixture,
        attention,
        mlp_part,
        gathered_grad,
        mixture_grad,
        reduce_part,
        expand_part,
        after_attn,
        after_grad,
        wide,
        expand_sum,
    ) = middle(
        head_scale,
        resolution,
        counts,
        gathered_one,
        query_weight.T,
        query_bias,
        key_weight.T,
        value_weight.T,
        value_bias,
        bias_map,
        output_weight,
        output_bias,
        hidden,
        first_scale,
        second_gain,
        second_shift,
        expand_weight,
        expand_bias,
        reduce_weight,
        cotangent,
        second_scale,
        0,
    )
    n_low = -(-table_low.shape[0] // (BB * 16)) * 16
    n_high = -(-table_high.shape[0] // (BB * 16)) * 16
    known = lax.axis_size("dp") == 8
    reduce_grad, expand_grad, attn_grads, result, hidden_grad, wide, slim, tables = tail(
        head_scale,
        known,
        resolution,
        counts,
        reduce_part,
        expand_part,
        queries,
        keys,
        values,
        attention,
        mixture_grad,
        gathered_one,
        mixture,
        gathered_grad,
        index_low_pad,
        index_high_pad,
        query_weight.T,
        key_weight.T,
        value_weight.T,
        hidden,
        after_grad,
        first_gain,
        mlp_part,
        after_attn,
        cotangent,
        reduce_bias,
        second_scale,
        wide,
        expand_sum,
        n_low,
        n_high,
        1,
    )
    reduce_grad = reduce_grad.astype(floating)
    expand_grad = expand_grad.astype(floating)
    attn_grads = attn_grads.astype(floating)
    if not known:
        reduce_grad, expand_grad, attn_grads, slim, tables = lax.psum(
            (reduce_grad, expand_grad, attn_grads, slim, tables), "dp"
        )
        wide = lax.psum(wide, ("dp", "tensor"))
    width = queries.shape[1]

    def unpack(block, count):
        block = block.reshape(heads_dev, BB, -1).transpose(2, 1, 0)
        return block.reshape(-1, heads_dev)[:count]

    return (
        result,
        hidden_grad,
        wide[0],
        wide[1],
        attn_grads[:width].T,
        slim[0, :width],
        attn_grads[width : 2 * width].T,
        attn_grads[2 * width : 3 * width].T,
        slim[1, :width],
        attn_grads[3 * width :],
        wide[3],
        wide[2],
        wide[4],
        wide[5],
        expand_grad,
        slim[2],
        reduce_grad,
        wide[7],
        wide[6],
        unpack(tables[:, :n_low], table_low.shape[0]),
        unpack(tables[:, n_low : n_low + n_high], table_high.shape[0]),
    )


def solution(mesh):
    in_specs = (
        P(("dp", "tensor"), None),
        P(),
        P(),
        P(None, "tensor"),
        P("tensor"),
        P(None, "tensor"),
        P(None, "tensor"),
        P("tensor"),
        P("tensor", None),
        P(),
        P(),
        P(),
        P(),
        P(None, "tensor"),
        P("tensor"),
        P("tensor", None),
        P(),
        P(),
        P(None, "tensor"),
        P(None, "tensor"),
        P("dp"),
        P("dp"),
        P(),
        P(),
        P(("dp", "tensor"), None),
    )
    out_specs = (
        P(("dp", "tensor"), None),
        P(("dp", "tensor"), None),
        P(),
        P(),
        P(None, "tensor"),
        P("tensor"),
        P(None, "tensor"),
        P(None, "tensor"),
        P("tensor"),
        P("tensor", None),
        P(),
        P(),
        P(),
        P(),
        P(None, "tensor"),
        P("tensor"),
        P("tensor", None),
        P(),
        P(),
        P(None, "tensor"),
        P(None, "tensor"),
    )
    return jax.shard_map(local, mesh=mesh, in_specs=in_specs, out_specs=out_specs, check_vma=False)
```

```python
import functools

import jax
import jax.numpy as jnp
from jax import lax
from jax.experimental import pallas as pl
from jax.experimental.pallas import tpu as pltpu
from jax.sharding import PartitionSpec as P

HD = 64
P_LO = 197
P_HI = 577
SEQ = 640
SLOTS = 2


eps_norm = 1e-06
masked_score = -1e30
inv_sqrt_two = 0.7071067811865476
inv_sqrt_two_pi = 0.3989422804014327


F32=jnp.float32; BF=jnp.bfloat16
NT=(((1,),(1,)),((),()))
def head_mask(h, width):
    lane = lax.broadcasted_iota(jnp.int32, (1, width), 1)
    return ((lane >= h*HD) & (lane < (h+1)*HD)).astype(F32).astype(BF)


BB=32; UN=16
def scatter_run(idx_ref, g_ref, out, first, last, fresh):
    heads = g_ref.shape[0]; na = out.shape[1]; m = idx_ref.shape[1]
    if fresh:
        out[...] = jnp.zeros_like(out)
    ib = lax.broadcasted_iota(jnp.int32, (16, m), 0).astype(F32)
    def body(r, c):
        ms = []; os = []
        for u in range(UN):
            row = r*UN+u
            idx = jnp.broadcast_to(idx_ref[pl.ds(row,1), :], (16, m))
            ia = (idx >> 5).astype(F32).astype(BF); il = (idx & 31).astype(F32).astype(BF)
            g = [jnp.broadcast_to(g_ref[h, pl.ds(row,1), :], (16, m)).astype(BF) for h in range(heads)]
            hits = [il == (ib + 16.0*k).astype(BF) for k in range(BB//16)]
            ms.append(jnp.concatenate([jnp.where(hits[k], g[h], jnp.zeros_like(g[h])) for h in range(heads) for k in range(BB//16)], axis=0))
            os.append(jnp.concatenate([jnp.where(ia == (ib + 16.0*k).astype(BF), jnp.ones_like(ia), jnp.zeros_like(ia)) for k in range(na//16)], axis=0))
        out[...] += lax.dot_general(jnp.concatenate(ms, axis=1), jnp.concatenate(os, axis=1), NT, preferred_element_type=F32)
        return c
    lax.fori_loop(first, last, body, 0)

PACK=8191.0
MESH = pl.DeviceIdType.MESH

CHUNKS = 6
TN = (((0,), (0,)), ((), ()))

def row(ref):
    return ref[...].reshape(1, ref.shape[0])

def live_of(t, rows, res, counts):
    slot = t * rows // SEQ
    first = t * rows - slot * SEQ
    limit = jnp.where(res[slot] == 1, P_HI, P_LO)
    limit = jnp.where(slot < counts[0], limit, 0)
    place = lax.broadcasted_iota(jnp.int32, (rows, 1), 0) + first
    return jnp.where(place < limit, 1.0, 0.0).astype(F32)

def moments(values):
    center = jnp.mean(values, axis=1, keepdims=True)
    centered = values - center
    inverse = lax.rsqrt(jnp.mean(centered * centered, axis=1, keepdims=True) + eps_norm)
    return centered * inverse, inverse

def norm_back(grad, scaled, inverse, gain):
    inner = grad * gain
    mean_inner = jnp.mean(inner, axis=1, keepdims=True)
    mean_mixed = jnp.mean(inner * scaled, axis=1, keepdims=True)
    return inverse * (inner - mean_inner - scaled * mean_mixed)

def look_up(tab, idx, heads):
    nch = tab.shape[1]
    lane = idx & 127
    ch = idx >> 7
    shift = jnp.where(ch >= nch, 0, 16)
    ch = jnp.where(ch >= nch, ch - nch, ch)
    acc = [None] * heads
    for k in range(nch):
        hit = ch == k
        for h in range(heads):
            v = jnp.take_along_axis(tab[h, k], lane, axis=1)
            acc[h] = v if k == 0 else jnp.where(hit, v, acc[h])
    return [((acc[h] << shift) >> 16).astype(F32) * (1.0 / PACK) for h in range(heads)]

def bias_rows(res, tab_lo, tab_hi, idx_lo, idx_hi, out, first, last, both):
    slots, heads = out.shape[:2]
    def masked(vals, j, limit):
        if (j + 1) * 128 <= limit:
            return vals
        place = lax.broadcasted_iota(jnp.int32, (8, 128), 1) + j * 128
        return [jnp.where(place < limit, v, masked_score) for v in vals]
    def body(r, c):
        for j in range(idx_hi.shape[1] // 128):
            cols = pl.ds(j * 128, 128)
            high = []
            low = []
            for part in range(2):
                rows = pl.ds(pl.multiple_of(r * 16 + part * 8, 8), 8)
                high.append(masked(look_up(tab_hi, idx_hi[rows, cols], heads), j, P_HI))
                if both and j < idx_lo.shape[1] // 128:
                    low.append(masked(look_up(tab_lo, idx_lo[rows, cols], heads), j, P_LO))
                else:
                    low.append([jnp.full((8, 128), masked_score, F32)] * heads)
            for h in range(heads):
                hi = jnp.concatenate([high[0][h], high[1][h]], axis=0).astype(BF)
                lo = jnp.concatenate([low[0][h], low[1][h]], axis=0).astype(BF)
                for s in range(slots):
                    out[s, h, pl.ds(pl.multiple_of(r * 16, 16), 16), cols] = jnp.where(res[s] == 1, hi, lo)
        return c
    lax.fori_loop(first, last, body, 0)

def layer_kernel(scale, sums, res, counts, hidden, gain1, shift1, wq, bq, wk, wv, bv, wo, bo, scale1, gain2, shift2, we, be, wr, rbias, scale2, cot,
                 tab_lo, tab_hi, ilo, ihi,
                 o0, o1, o2, result, hidden_grad, wide, slim, tables,
                 g1, gm, gt, ga, q_buf, k_buf, v_buf, mix, dmix, pb, act, pgl, part, acc, attn, x0, x1, x2, ghi, glo, esum,
                 cbuf, ccore, xbuf, xin, acore, across, bcore, bcross, ybuf, zbuf,
                 tlo, thi, wmine, wmid, smine, tmine, wten, wdp, sdp, tdp,
                 h_s, h_r, m_s, m_r, t_s, t_r, a_s, a_r, o_s, o_r, n_s, n_r,
                 y_s, y_r, z_s, z_r, g_s, g_r, e_s, e_r, r_s, r_r, w_s, w_r, v_s, v_r):
    d = lax.axis_index("dp")
    t = lax.axis_index("tensor")
    col = d // 2
    side = lax.rem(d, 2)
    neighbour = d + 1 - 2 * side
    sibling = t + 1 - 2 * lax.rem(t, 2)
    cross = lax.rem(t + 2, 4)
    diag = 3 - t
    rows = hidden.shape[0]
    half = rows // 2
    slots, heads = pb.shape[:2]
    width = q_buf.shape[1]
    barrier = pltpu.get_barrier_semaphore()
    for k in range(1, 4):
        pl.semaphore_signal(barrier, inc=1, device_id=(d, lax.rem(t + k, 4)), device_id_type=MESH)
    if sums:
        for k in range(1, 8):
            pl.semaphore_signal(barrier, inc=1, device_id=(lax.rem(d + k, 8), t), device_id_type=MESH)

    def remote(src, dst, send, recv, device):
        return pltpu.make_async_remote_copy(src_ref=src, dst_ref=dst, send_sem=send, recv_sem=recv, device_id=device, device_id_type=MESH)
    def rows_at(who):
        return pl.ds(pl.multiple_of(who * rows, 16), rows)
    def span(who, h):
        return pl.ds(pl.multiple_of(who * rows + h * half, 16), half)
    def gather_x(buf, send, recv, h):
        here = buf.at[span(t, h)]
        return remote(here, here, send.at[h], recv.at[h], (d, cross))
    def gather_near(buf, send, recv, h):
        here = buf.at[span(t, h)]
        return remote(here, here, send.at[2 + h], recv.at[2 + h], (d, sibling))
    def gather_on(buf, send, recv, h):
        here = buf.at[span(cross, h)]
        return remote(here, here, send.at[4 + h], recv.at[4 + h], (d, sibling))
    def sum_far(j, send, recv, h):
        return remote(cbuf.at[j, 0, h], ccore.at[j, 0, h], send.at[h], recv.at[h], (d, sibling))
    def sum_near(j, send, recv, h):
        return remote(cbuf.at[j, 1, h], ccore.at[j, 1, h], send.at[2 + h], recv.at[2 + h], (d, sibling))
    def sum_x(j, send, recv, h):
        return remote(xbuf.at[j, h], xin.at[j, h], send.at[4 + h], recv.at[4 + h], (d, cross))
    arrays = (x0, x1, x2)
    outs = (o0, o1, o2)
    size = x0.shape[0] // 2
    part_y = size // 2
    part_z = part_y // 4
    def at(n, start, count):
        return pl.ds(pl.multiple_of((n % 2) * size + start, 16), count)
    def y_copy(n):
        return remote(arrays[n // 2].at[at(n, (1 - side) * part_y, part_y)], ybuf.at[n], y_s.at[n], y_r.at[n], (neighbour, t))
    def z_copy(n, k):
        to = lax.rem(col + k, 4)
        return remote(arrays[n // 2].at[at(n, side * part_y + to * part_z, part_z)], zbuf.at[n, k - 1], z_s.at[n, k], z_r.at[n, k], (to * 2 + side, t))
    def g_copy(n, k):
        to = lax.rem(col + k, 4)
        here = outs[n // 2].at[at(n, side * part_y + col * part_z, part_z)]
        return remote(here, here, g_s.at[n, k], g_r.at[n, k], (to * 2 + side, t))
    def e_copy(n):
        here = outs[n // 2].at[at(n, side * part_y, part_y)]
        return remote(here, here, e_s.at[n], e_r.at[n], (neighbour, t))
    def start_y(n):
        y_copy(n).start()
    def step_a(n):
        y_copy(n).wait()
        if n < 2:
            y_copy(n + 2).start()
        here = at(n, side * part_y, part_y)
        arrays[n // 2][here] = (arrays[n // 2][here].astype(F32) + ybuf[n].astype(F32)).astype(BF)
        for k in range(1, 4):
            z_copy(n, k).start()
    def step_b(n):
        for k in range(1, 4):
            z_copy(n, k).wait()
        here = at(n, side * part_y + col * part_z, part_z)
        total = arrays[n // 2][here].astype(F32)
        for k in range(3):
            total = total + zbuf[n, k].astype(F32)
        outs[n // 2][here] = total.astype(BF)
        for k in range(1, 4):
            g_copy(n, k).start()
    def step_d(n):
        for k in range(1, 4):
            g_copy(n, k).wait()
        e_copy(n).start()
    if not sums:
        start_y = step_a = step_b = step_d = lambda n: None

    scaled, inverse = moments(hidden[...].astype(F32))
    g1[rows_at(t)] = (scaled * row(gain1) + row(shift1)).astype(BF)
    pl.semaphore_wait(barrier, 10 if sums else 3)
    for h in range(2):
        gather_x(g1, h_s, h_r, h).start()
        gather_near(g1, h_s, h_r, h).start()
    alive = live_of(t, rows, res, counts)
    gm[rows_at(t)] = (cot[...].astype(F32) * alive * row(scale2)).astype(BF)
    look = functools.partial(bias_rows, res, tab_lo, tab_hi, ilo, ihi, pb)
    n_low = -(-P_LO // 16)
    n_high = -(-P_HI // 16)
    middle = (n_low + n_high) // 2
    look(0, n_low, True)
    look(n_low, middle, False)
    for h in range(2):
        gather_x(g1, h_s, h_r, h).wait()
        gather_on(g1, h_s, h_r, h).start()
        gather_x(gm, m_s, m_r, h).start()
        gather_near(gm, m_s, m_r, h).start()
    look(middle, n_high, False)
    pb[:, :, n_high * 16:, :] = jnp.zeros((slots, heads, SEQ - n_high * 16, SEQ), BF)
    for h in range(2):
        gather_near(g1, h_s, h_r, h).wait()
        gather_on(g1, h_s, h_r, h).wait()

    def project(i, c):
        here = rows_at(i)
        g = g1[here]
        q_buf[here] = ((lax.dot_general(g, wq[...], NT, preferred_element_type=F32) + row(bq)) * scale).astype(BF)
        k_buf[here] = lax.dot_general(g, wk[...], NT, preferred_element_type=F32).astype(BF)
        v_buf[here] = (lax.dot_general(g, wv[...], NT, preferred_element_type=F32) + row(bv)).astype(BF)
        return c
    lax.fori_loop(0, 4, project, 0)

    def attend_image(slot):
        here = pl.ds(pl.multiple_of(slot * SEQ, 16), SEQ)
        k = k_buf[here]
        v = v_buf[here]
        vm = [v * head_mask(h, width) for h in range(heads)]
        def piece(i, c):
            first = pl.multiple_of(i * rows, 16)
            there = pl.ds(pl.multiple_of(slot * SEQ + first, 16), rows)
            q = q_buf[there]
            out = jnp.zeros((rows, width), F32)
            for h in range(heads):
                s = lax.dot_general(q * head_mask(h, width), k, NT, preferred_element_type=F32)
                s = s + pb[slot, h, pl.ds(first, rows)].astype(F32)
                peak = jnp.max(s, axis=1, keepdims=True)
                e = jnp.exp(s - peak)
                total = jnp.sum(e, axis=1, keepdims=True)
                p = (e * (1.0 / total)).astype(BF)
                pb[slot, h, pl.ds(first, rows)] = p
                out = out + jnp.dot(p, vm[h], preferred_element_type=F32)
            mix[there] = out.astype(BF)
            return c
        lax.fori_loop(0, SEQ // rows, piece, 0)
    def output_of(who, h):
        return jnp.dot(mix[span(who, h)], wo[...], preferred_element_type=F32)

    mine = t * rows // SEQ
    attend_image(1 - mine)
    for h in range(2):
        cbuf[0, 0, h] = output_of(diag, h).astype(BF)
        sum_far(0, o_s, o_r, h).start()
    for h in range(2):
        total = output_of(cross, h)
        sum_far(0, o_s, o_r, h).wait()
        xbuf[0, h] = (total + ccore[0, 0, h].astype(F32)).astype(BF)
        sum_x(0, o_s, o_r, h).start()
    attend_image(mine)
    for h in range(2):
        cbuf[0, 1, h] = output_of(sibling, h).astype(BF)
        sum_near(0, o_s, o_r, h).start()
    for h in range(2):
        acc[pl.ds(h * half, half)] = output_of(t, h)
    for h in range(2):
        gather_x(gm, m_s, m_r, h).wait()
        gather_on(gm, m_s, m_r, h).start()
    for h in range(2):
        here = pl.ds(h * half, half)
        sum_near(0, o_s, o_r, h).wait()
        sum_x(0, o_s, o_r, h).wait()
        out = acc[here] + ccore[0, 1, h].astype(F32) + xin[0, h].astype(F32) + row(bo)
        attn[here] = out
        scaled, inverse = moments(hidden[here].astype(F32) + row(scale1) * out)
        gt[span(t, h)] = (scaled * row(gain2) + row(shift2)).astype(BF)
        gather_x(gt, t_s, t_r, h).start()
        gather_near(gt, t_s, t_r, h).start()

    esum[...] = jnp.zeros_like(esum)
    def feed(who, h):
        here = span(who, h)
        pre = jnp.dot(gt[here], we[...], preferred_element_type=F32) + row(be)
        grad = lax.dot_general(gm[here], wr[...], NT, preferred_element_type=F32)
        phi = 0.5 * (1.0 + lax.erf(pre * inv_sqrt_two))
        active = (pre * phi).astype(BF)
        act[here] = active
        grad = grad * (phi + pre * inv_sqrt_two_pi * jnp.exp(-0.5 * pre * pre))
        esum[...] += jnp.sum(grad, axis=0, keepdims=True)
        grad = grad.astype(BF)
        pgl[here] = grad
        part[here] = jnp.dot(active, wr[...], preferred_element_type=F32).astype(BF)
        return lax.dot_general(grad, we[...], NT, preferred_element_type=F32)
    def feed_own(h, c):
        acc[pl.ds(pl.multiple_of(h * half, 16), half)] = feed(t, h)
        return c
    lax.fori_loop(0, 2, feed_own, 0)
    for h in range(2):
        gather_near(gm, m_s, m_r, h).wait()
        gather_near(gt, t_s, t_r, h).wait()
    gather_x(gt, t_s, t_r, 0).wait()
    gather_on(gt, t_s, t_r, 0).start()
    def feed_near(h, c):
        cbuf[1, 1, h] = feed(sibling, h).astype(BF)
        return c
    lax.fori_loop(0, 2, feed_near, 0)
    for h in range(2):
        sum_near(1, n_s, n_r, h).start()
    gather_x(gt, t_s, t_r, 1).wait()
    gather_on(gt, t_s, t_r, 1).start()
    for h in range(2):
        gather_on(gm, m_s, m_r, h).wait()
        gather_on(gt, t_s, t_r, h).wait()
    def feed_far(h, c):
        cbuf[1, 0, h] = feed(diag, h).astype(BF)
        sum_far(1, n_s, n_r, h).start()
        total = feed(cross, h)
        sum_far(1, n_s, n_r, h).wait()
        xbuf[1, h] = (total + ccore[1, 0, h].astype(F32)).astype(BF)
        sum_x(1, n_s, n_r, h).start()
        return c
    lax.fori_loop(0, 2, feed_far, 0)

    tile = 128
    def reduce_grad(i, c):
        cols = pl.ds(pl.multiple_of(i * tile, tile), tile)
        x0[cols] = lax.dot_general(act[:, cols], gm[...], TN, preferred_element_type=F32).astype(BF)
        return c
    lax.fori_loop(0, act.shape[1] // tile, reduce_grad, 0)
    start_y(0)
    start_y(1)
    def expand_grad(i, c):
        cols = pl.ds(pl.multiple_of(i * tile, tile), tile)
        x1[cols] = lax.dot_general(gt[:, cols], pgl[...], TN, preferred_element_type=F32).astype(BF)
        return c
    lax.fori_loop(0, gt.shape[1] // tile, expand_grad, 0)

    wmine[...] = jnp.zeros_like(wmine)
    for h in range(2):
        here = pl.ds(h * half, half)
        sum_near(1, n_s, n_r, h).wait()
        sum_x(1, n_s, n_r, h).wait()
        grad = acc[here] + ccore[1, 1, h].astype(F32) + xin[1, h].astype(F32)
        out = attn[here]
        scaled, inverse = moments(hidden[here].astype(F32) + row(scale1) * out)
        after = cot[here].astype(F32) * alive[h * half:(h + 1) * half] + norm_back(grad, scaled, inverse, row(gain2))
        hidden_grad[here] = after
        agrad = after * row(scale1)
        ga[span(t, h)] = agrad.astype(BF)
        gather_x(ga, a_s, a_r, h).start()
        gather_near(ga, a_s, a_r, h).start()
        wmine[2:3, :] += jnp.sum(after * out, axis=0, keepdims=True)
        wmine[3:4, :] += jnp.sum(agrad, axis=0, keepdims=True)
        wmine[4:5, :] += jnp.sum(grad * scaled, axis=0, keepdims=True)
        wmine[5:6, :] += jnp.sum(grad, axis=0, keepdims=True)
    step_a(0)
    def mixture_of(who):
        here = rows_at(who)
        dmix[here] = lax.dot_general(ga[here], wo[...], NT, preferred_element_type=F32).astype(BF)
    mixture_of(t)
    gather_x(ga, a_s, a_r, 0).wait()
    gather_on(ga, a_s, a_r, 0).start()
    for h in range(2):
        gather_near(ga, a_s, a_r, h).wait()
    mixture_of(sibling)
    step_a(1)
    gather_x(ga, a_s, a_r, 1).wait()
    gather_on(ga, a_s, a_r, 1).start()
    mixture_of(cross)
    for h in range(2):
        gather_on(ga, a_s, a_r, h).wait()
    mixture_of(diag)

    smine[...] = jnp.zeros_like(smine)
    smine[2:3, :] = esum[...]
    def attention_back(slot):
        here = slice(slot * SEQ, (slot + 1) * SEQ)
        q = q_buf[here]
        k = k_buf[here]
        v = v_buf[here]
        dd = dmix[here]
        qt = q.T
        dt = dd.T
        is_high = jnp.where(res[slot] == 1, 1.0, 0.0).astype(F32)
        out = jnp.zeros((SEQ, width), F32)
        dks = []
        dvs = []
        nh = ghi.shape[1]
        nl, ml = glo.shape[1:]
        for h in range(heads):
            mask = head_mask(h, width)
            p = pb[slot, h]
            dp = lax.dot_general(dd * mask, v, NT, preferred_element_type=F32)
            pf = p.astype(F32)
            m = pf * dp
            ds = m - pf * jnp.sum(m, axis=1, keepdims=True)
            if slot == 0:
                ghi[h] = ds[:nh] * is_high
                glo[h] = ds[:nl, :ml] * (1.0 - is_high)
            else:
                ghi[h] += ds[:nh] * is_high
                glo[h] += ds[:nl, :ml] * (1.0 - is_high)
            low = ds.astype(BF)
            out = out + jnp.dot(low, k * mask, preferred_element_type=F32)
            dks.append(jnp.dot(qt[h*HD:(h+1)*HD], low, preferred_element_type=F32))
            dvs.append(jnp.dot(dt[h*HD:(h+1)*HD], p, preferred_element_type=F32))
        out = out * scale
        smine[0:1, 0:width] += jnp.sum(out, axis=0, keepdims=True)
        q_buf[here] = out.astype(BF)
        k_buf[here] = jnp.concatenate(dks, axis=0).T.astype(BF)
        out = jnp.concatenate(dvs, axis=0).T
        smine[1:2, 0:width] += jnp.sum(out, axis=0, keepdims=True)
        v_buf[here] = out.astype(BF)
    attention_back(0)
    step_a(2)
    attention_back(1)
    step_b(0)
    step_a(3)

    def back(who):
        here = rows_at(who)
        total = jnp.dot(q_buf[here], wq[...], preferred_element_type=F32)
        total = total + jnp.dot(k_buf[here], wk[...], preferred_element_type=F32)
        return total + jnp.dot(v_buf[here], wv[...], preferred_element_type=F32)
    def send(buf, value):
        for h in range(2):
            buf[h] = value[h * half:(h + 1) * half].astype(BF)
    def whole(ref):
        return jnp.concatenate([ref[0], ref[1]], axis=0).astype(F32)
    a_far = remote(cbuf.at[0, 0], acore.at[0], r_s.at[0], r_r.at[0], (d, sibling))
    a_near = remote(cbuf.at[0, 1], acore.at[1], r_s.at[1], r_r.at[1], (d, sibling))
    a_cross = remote(xbuf.at[0], across, r_s.at[2], r_r.at[2], (d, cross))
    b_far = remote(part.at[rows_at(diag)], bcore.at[0], r_s.at[3], r_r.at[3], (d, sibling))
    b_near = remote(part.at[rows_at(sibling)], bcore.at[1], r_s.at[4], r_r.at[4], (d, sibling))
    b_cross = remote(xbuf.at[1], bcross, r_s.at[5], r_r.at[5], (d, cross))
    send(cbuf.at[0, 0], back(diag))
    a_far.start()
    b_far.start()
    total = back(cross)
    a_far.wait()
    send(xbuf.at[0], total + whole(acore.at[0]))
    a_cross.start()
    for j, (left, right) in enumerate(((q_buf, g1), (k_buf, g1), (v_buf, g1), (mix, ga))):
        x2[j * width:(j + 1) * width, :] = lax.dot_general(left[...], right[...], TN, preferred_element_type=F32).astype(BF)
    start_y(4)
    start_y(5)
    step_b(1)
    send(cbuf.at[0, 1], back(sibling))
    a_near.start()
    b_near.start()
    acc[...] = back(t)
    b_far.wait()
    send(xbuf.at[1], part[rows_at(cross)].astype(F32) + bcore[0].astype(F32))
    segments = 7
    n_hi = (-(-P_HI // UN))
    def scatter_part(s):
        lo, hi = n_hi * s // segments, n_hi * (s + 1) // segments
        scatter_run(ihi, ghi, thi, lo, hi, s == 0)
    scatter_part(0)
    step_a(4)
    step_d(0)
    step_b(2)
    a_cross.wait()
    b_cross.start()
    a_near.wait()
    grad = acc[...] + whole(acore.at[1]) + whole(across)
    scaled, inverse = moments(hidden[...].astype(F32))
    wmine[0:1, :] = jnp.sum(grad * scaled, axis=0, keepdims=True)
    wmine[1:2, :] = jnp.sum(grad, axis=0, keepdims=True)
    hidden_grad[...] += norm_back(grad, scaled, inverse, row(gain1))
    scatter_part(1)
    step_a(5)
    step_d(1)
    step_b(3)
    scatter_part(2)
    b_near.wait()
    b_cross.wait()
    out = part[rows_at(t)].astype(F32) + bcore[1].astype(F32) + whole(bcross) + row(rbias)
    after = hidden[...].astype(F32) + row(scale1) * attn[...]
    result[...] = ((after + row(scale2) * out) * alive).astype(BF)
    up = cot[...].astype(F32) * alive
    wmine[6:7, :] = jnp.sum(up * out, axis=0, keepdims=True)
    wmine[7:8, :] = jnp.sum(up * row(scale2), axis=0, keepdims=True)
    def w_copy(k):
        return remote(wmine, wten.at[k], w_s.at[k], w_r.at[k], (d, lax.rem(t + k, 4)))
    def v_copy(j, k):
        src, dst = ((wmid, wdp), (smine, sdp), (tmine, tdp))[j]
        return remote(src, dst.at[k], v_s.at[j, k], v_r.at[j, k], (lax.rem(d + k, 8), t))
    if sums:
        for k in range(1, 4):
            w_copy(k).start()
        for k in range(1, 8):
            v_copy(1, k).start()
    step_d(2)
    step_b(4)
    scatter_part(3)
    total = wmine[...]
    if sums:
        for k in range(1, 4):
            w_copy(k).wait()
            total = total + wten[k]
    wmid[...] = total
    if sums:
        for k in range(1, 8):
            v_copy(0, k).start()
    step_b(5)
    step_d(3)
    scatter_part(4)
    step_d(4)
    scatter_part(5)
    scatter_part(6)
    scatter_run(ilo, glo, tlo, 0, -(-P_LO // UN), True)
    tables[...] = jnp.zeros_like(tables)
    n = tlo.shape[1]
    tables[:, 0:n] = tlo[...]
    tables[:, n:n + thi.shape[1]] = thi[...]
    wide[...] = wmid[...]
    slim[...] = smine[...]
    if not sums:
        o0[...] = x0[...]
        o1[...] = x1[...]
        o2[...] = x2[...]
        return
    tmine[...] = tables[...].astype(BF)
    tables[...] = tmine[...].astype(F32)
    for k in range(1, 8):
        v_copy(2, k).start()
    step_d(5)
    for k in range(1, 8):
        v_copy(0, k).wait()
        v_copy(1, k).wait()
        wide[...] += wdp[k]
        slim[...] += sdp[k]
    for k in range(1, 8):
        v_copy(2, k).wait()
        tables[...] += tdp[k].astype(F32)
    for n in range(CHUNKS):
        e_copy(n).wait()

def layer(scale, sums, res, counts, hidden, gain1, shift1, wq, bq, wk, wv, bv, wo, bo, scale1, gain2, shift2, we, be, wr, rbias, scale2, cot, table_low, table_high, ilo, ihi, n_lo, n_hi):
    rows, model = hidden.shape
    total = rows * 4
    width = wq.shape[0]
    inner = we.shape[1]
    heads = table_low.shape[1]
    def chunks(table):
        n = -(-table.shape[0] // 256) * 256
        w = jnp.round(jnp.pad(table.T, ((0, 0), (0, n - table.shape[0]))) * PACK).astype(jnp.int32)
        w = w.reshape(heads, 2, n // 256, 1, 128)
        w = (w[:, 1] << 16) | (w[:, 0] & 65535)
        return jnp.broadcast_to(w, (heads, n // 256, 8, 128))
    vm = pl.BlockSpec(memory_space=pltpu.VMEM)
    sm = pl.BlockSpec(memory_space=pltpu.SMEM)
    dma = pltpu.SemaphoreType.DMA
    V = pltpu.VMEM
    S = jax.ShapeDtypeStruct
    operands = (hidden, gain1, shift1, wq, bq, wk, wv, bv, wo, bo, scale1, gain2, shift2, we, be, wr, rbias, scale2, cot, chunks(table_low), chunks(table_high), ilo, ihi)
    tshape = (heads * BB, 128)
    half = rows // 2
    return pl.pallas_call(functools.partial(layer_kernel, scale, sums),
        out_shape=(S((inner, model), BF), S((model, inner), BF), S((4 * width, model), BF), S((rows, model), BF), S((rows, model), F32), S((8, model), F32), S((8, model), F32), S(tshape, F32)),
        in_specs=[sm, sm] + [vm] * len(operands), out_specs=(vm,) * 8,
        scratch_shapes=[V((total, model), BF)] * 4 + [V((total, width), BF)] * 5 + [V((SLOTS, heads, SEQ, SEQ), BF)]
            + [V((total, inner), BF)] * 2 + [V((total, model), BF)] + [V((rows, model), F32)] * 2
            + [V((inner, model), BF), V((model, inner), BF), V((4 * width, model), BF), V((heads,) + ihi.shape, F32), V((heads,) + ilo.shape, F32), V((1, inner), F32)]
            + [V((2, 2, 2, half, model), BF)] * 2 + [V((2, 2, half, model), BF)] * 2
            + [V((2, 2, half, model), BF), V((2, half, model), BF), V((2, rows, model), BF), V((2, half, model), BF)]
            + [V((CHUNKS, 192, model), BF), V((CHUNKS, 3, 48, model), BF)]
            + [V((heads * BB, n_lo), F32), V((heads * BB, n_hi), F32)]
            + [V((8, model), F32)] * 3 + [V(tshape, BF), V((4, 8, model), F32), V((8, 8, model), F32), V((8, 8, model), F32), V((8,) + tshape, BF)]
            + [dma((6,))] * 12
            + [dma((CHUNKS,)), dma((CHUNKS,)), dma((CHUNKS, 4)), dma((CHUNKS, 4)), dma((CHUNKS, 4)), dma((CHUNKS, 4)), dma((CHUNKS,)), dma((CHUNKS,)),
               dma((6,)), dma((6,)), dma((4,)), dma((4,)), dma((3, 8)), dma((3, 8))],
        name="layer", cost_estimate=pl.CostEstimate(flops=100 * 10**9, bytes_accessed=60 * 10**6, transcendentals=0),
        compiler_params=pltpu.CompilerParams(collective_id=0, has_side_effects=True, vmem_limit_bytes=63 << 20))(res, counts, *operands)


def local(
    hidden,
    first_gain,
    first_shift,
    query_weight,
    query_bias,
    key_weight,
    value_weight,
    value_bias,
    output_weight,
    output_bias,
    first_scale,
    second_gain,
    second_shift,
    expand_weight,
    expand_bias,
    reduce_weight,
    reduce_bias,
    second_scale,
    table_low,
    table_high,
    resolution,
    counts,
    index_low,
    index_high,
    cotangent,
):
    floating = jnp.float32
    heads_dev = table_low.shape[1]
    width = query_weight.shape[1]
    index_low_pad = jnp.pad(index_low, ((0, 256 - P_LO), (0, 256 - P_LO)))
    index_high_pad = jnp.pad(index_high, ((0, 592 - P_HI), (0, SEQ - P_HI)))
    n_low = -(-table_low.shape[0] // (BB * 16)) * 16
    n_high = -(-table_high.shape[0] // (BB * 16)) * 16
    known = lax.axis_size("dp") == 8
    reduce_grad, expand_grad, attn_grads, result, hidden_grad, wide, slim, tables = layer(
        HD ** (-0.5),
        known,
        resolution,
        counts,
        hidden,
        first_gain,
        first_shift,
        query_weight.T,
        query_bias,
        key_weight.T,
        value_weight.T,
        value_bias,
        output_weight,
        output_bias,
        first_scale,
        second_gain,
        second_shift,
        expand_weight,
        expand_bias,
        reduce_weight,
        reduce_bias,
        second_scale,
        cotangent,
        table_low,
        table_high,
        index_low_pad,
        index_high_pad,
        n_low,
        n_high,
    )
    reduce_grad = reduce_grad.astype(floating)
    expand_grad = expand_grad.astype(floating)
    attn_grads = attn_grads.astype(floating)
    if not known:
        reduce_grad, expand_grad, attn_grads, slim, tables = lax.psum(
            (reduce_grad, expand_grad, attn_grads, slim, tables), "dp"
        )
        wide = lax.psum(wide, ("dp", "tensor"))

    def unpack(block, count):
        block = block.reshape(heads_dev, BB, -1).transpose(2, 1, 0)
        return block.reshape(-1, heads_dev)[:count]

    return (
        result,
        hidden_grad,
        wide[0],
        wide[1],
        attn_grads[:width].T,
        slim[0, :width],
        attn_grads[width : 2 * width].T,
        attn_grads[2 * width : 3 * width].T,
        slim[1, :width],
        attn_grads[3 * width :],
        wide[3],
        wide[2],
        wide[4],
        wide[5],
        expand_grad,
        slim[2],
        reduce_grad,
        wide[7],
        wide[6],
        unpack(tables[:, :n_low], table_low.shape[0]),
        unpack(tables[:, n_low : n_low + n_high], table_high.shape[0]),
    )


def solution(mesh):
    in_specs = (
        P(("dp", "tensor"), None),
        P(),
        P(),
        P(None, "tensor"),
        P("tensor"),
        P(None, "tensor"),
        P(None, "tensor"),
        P("tensor"),
        P("tensor", None),
        P(),
        P(),
        P(),
        P(),
        P(None, "tensor"),
        P("tensor"),
        P("tensor", None),
        P(),
        P(),
        P(None, "tensor"),
        P(None, "tensor"),
        P("dp"),
        P("dp"),
        P(),
        P(),
        P(("dp", "tensor"), None),
    )
    out_specs = (
        P(("dp", "tensor"), None),
        P(("dp", "tensor"), None),
        P(),
        P(),
        P(None, "tensor"),
        P("tensor"),
        P(None, "tensor"),
        P(None, "tensor"),
        P("tensor"),
        P("tensor", None),
        P(),
        P(),
        P(),
        P(),
        P(None, "tensor"),
        P("tensor"),
        P("tensor", None),
        P(),
        P(),
        P(None, "tensor"),
        P(None, "tensor"),
    )
    return jax.shard_map(local, mesh=mesh, in_specs=in_specs, out_specs=out_specs, check_vma=False)
```

```python
import functools

import jax
import jax.numpy as jnp
from jax import lax
from jax.experimental import pallas as pl
from jax.experimental.pallas import tpu as pltpu
from jax.sharding import PartitionSpec as P

HD = 64
P_LO = 197
P_HI = 577
SEQ = 640
SLOTS = 2


eps_norm = 1e-06
masked_score = -1e30
inv_sqrt_two = 0.7071067811865476
inv_sqrt_two_pi = 0.3989422804014327


F32=jnp.float32; BF=jnp.bfloat16
NT=(((1,),(1,)),((),()))
def head_mask(h, width):
    lane = lax.broadcasted_iota(jnp.int32, (1, width), 1)
    return ((lane >= h*HD) & (lane < (h+1)*HD)).astype(F32).astype(BF)


BB=32; UN=16
def scatter_run(idx_ref, g_ref, out, first, last, fresh):
    heads = g_ref.shape[0]; na = out.shape[1]; m = idx_ref.shape[1]
    if fresh:
        out[...] = jnp.zeros_like(out)
    ib = lax.broadcasted_iota(jnp.int32, (16, m), 0).astype(F32)
    def body(r, c):
        ms = []; os = []
        for u in range(UN):
            row = r*UN+u
            idx = jnp.broadcast_to(idx_ref[pl.ds(row,1), :], (16, m))
            ia = (idx >> 5).astype(F32).astype(BF); il = (idx & 31).astype(F32).astype(BF)
            g = [jnp.broadcast_to(g_ref[h, pl.ds(row,1), :], (16, m)).astype(BF) for h in range(heads)]
            hits = [il == (ib + 16.0*k).astype(BF) for k in range(BB//16)]
            ms.append(jnp.concatenate([jnp.where(hits[k], g[h], jnp.zeros_like(g[h])) for h in range(heads) for k in range(BB//16)], axis=0))
            os.append(jnp.concatenate([jnp.where(ia == (ib + 16.0*k).astype(BF), jnp.ones_like(ia), jnp.zeros_like(ia)) for k in range(na//16)], axis=0))
        out[...] += lax.dot_general(jnp.concatenate(ms, axis=1), jnp.concatenate(os, axis=1), NT, preferred_element_type=F32)
        return c
    lax.fori_loop(first, last, body, 0)

PACK=8191.0
MESH = pl.DeviceIdType.MESH

CHUNKS = 6
TN = (((0,), (0,)), ((), ()))

def row(ref):
    return ref[...].reshape(1, ref.shape[0])

def live_of(t, rows, res, counts):
    slot = t * rows // SEQ
    first = t * rows - slot * SEQ
    limit = jnp.where(res[slot] == 1, P_HI, P_LO)
    limit = jnp.where(slot < counts[0], limit, 0)
    place = lax.broadcasted_iota(jnp.int32, (rows, 1), 0) + first
    return jnp.where(place < limit, 1.0, 0.0).astype(F32)

def moments(values):
    center = jnp.mean(values, axis=1, keepdims=True)
    centered = values - center
    inverse = lax.rsqrt(jnp.mean(centered * centered, axis=1, keepdims=True) + eps_norm)
    return centered * inverse, inverse

def norm_back(grad, scaled, inverse, gain):
    inner = grad * gain
    mean_inner = jnp.mean(inner, axis=1, keepdims=True)
    mean_mixed = jnp.mean(inner * scaled, axis=1, keepdims=True)
    return inverse * (inner - mean_inner - scaled * mean_mixed)

def look_up(tab, idx, heads):
    nch = tab.shape[1]
    lane = idx & 127
    ch = idx >> 7
    shift = jnp.where(ch >= nch, 0, 16)
    ch = jnp.where(ch >= nch, ch - nch, ch)
    acc = [None] * heads
    for k in range(nch):
        hit = ch == k
        for h in range(heads):
            v = jnp.take_along_axis(tab[h, k], lane, axis=1)
            acc[h] = v if k == 0 else jnp.where(hit, v, acc[h])
    return [((acc[h] << shift) >> 16).astype(F32) * (1.0 / PACK) for h in range(heads)]

def bias_rows(res, tab_lo, tab_hi, idx_lo, idx_hi, out, first, last, both):
    slots, heads = out.shape[:2]
    def masked(vals, j, limit):
        if (j + 1) * 128 <= limit:
            return vals
        place = lax.broadcasted_iota(jnp.int32, (8, 128), 1) + j * 128
        return [jnp.where(place < limit, v, masked_score) for v in vals]
    def body(r, c):
        for j in range(idx_hi.shape[1] // 128):
            cols = pl.ds(j * 128, 128)
            high = []
            low = []
            for part in range(2):
                rows = pl.ds(pl.multiple_of(r * 16 + part * 8, 8), 8)
                high.append(masked(look_up(tab_hi, idx_hi[rows, cols], heads), j, P_HI))
                if both and j < idx_lo.shape[1] // 128:
                    low.append(masked(look_up(tab_lo, idx_lo[rows, cols], heads), j, P_LO))
                else:
                    low.append([jnp.full((8, 128), masked_score, F32)] * heads)
            for h in range(heads):
                hi = jnp.concatenate([high[0][h], high[1][h]], axis=0).astype(BF)
                lo = jnp.concatenate([low[0][h], low[1][h]], axis=0).astype(BF)
                for s in range(slots):
                    out[s, h, pl.ds(pl.multiple_of(r * 16, 16), 16), cols] = jnp.where(res[s] == 1, hi, lo)
        return c
    lax.fori_loop(first, last, body, 0)

def layer_kernel(scale, sums, res, counts, hidden, gain1, shift1, wq, bq, wk, wv, bv, wo, bo, scale1, gain2, shift2, we, be, wr, rbias, scale2, cot,
                 table_lo, table_hi, ilo_in, ihi_in,
                 o0, o1, o2, result, hidden_grad, small, tlow, thigh,
                 tab_lo, tab_hi, raw, ilo, ihi, flip,
                 g1, gm, gt, ga, q_buf, k_buf, v_buf, mix, dmix, pb, act, pgl, part, acc, attn, x0, x1, x2, ghi, glo, esum,
                 cbuf, ccore, xbuf, xin, acore, across, bcore, bcross, ybuf, zbuf,
                 tlo, thi, wmine, smine, wten, vec, vland, vout, tbl, tland, tout,
                 h_s, h_r, m_s, m_r, t_s, t_r, a_s, a_r, o_s, o_r, n_s, n_r,
                 y_s, y_r, z_s, z_r, g_s, g_r, e_s, e_r, r_s, r_r, w_s, w_r, v_s, v_r):
    d = lax.axis_index("dp")
    t = lax.axis_index("tensor")
    col = d // 2
    side = lax.rem(d, 2)
    neighbour = d + 1 - 2 * side
    sibling = t + 1 - 2 * lax.rem(t, 2)
    cross = lax.rem(t + 2, 4)
    diag = 3 - t
    rows = hidden.shape[0]
    half = rows // 2
    slots, heads = pb.shape[:2]
    width = q_buf.shape[1]
    model = g1.shape[1]
    barrier = pltpu.get_barrier_semaphore()
    for k in range(1, 4):
        pl.semaphore_signal(barrier, inc=1, device_id=(d, lax.rem(t + k, 4)), device_id_type=MESH)
    if sums:
        for k in range(1, 8):
            pl.semaphore_signal(barrier, inc=1, device_id=(lax.rem(d + k, 8), t), device_id_type=MESH)

    def remote(src, dst, send, recv, device):
        return pltpu.make_async_remote_copy(src_ref=src, dst_ref=dst, send_sem=send, recv_sem=recv, device_id=device, device_id_type=MESH)
    def rows_at(who):
        return pl.ds(pl.multiple_of(who * rows, 16), rows)
    def span(who, h):
        return pl.ds(pl.multiple_of(who * rows + h * half, 16), half)
    def gather_x(buf, send, recv, h):
        here = buf.at[span(t, h)]
        return remote(here, here, send.at[h], recv.at[h], (d, cross))
    def gather_near(buf, send, recv, h):
        here = buf.at[span(t, h)]
        return remote(here, here, send.at[2 + h], recv.at[2 + h], (d, sibling))
    def gather_on(buf, send, recv, h):
        here = buf.at[span(cross, h)]
        return remote(here, here, send.at[4 + h], recv.at[4 + h], (d, sibling))
    def sum_far(j, send, recv, h):
        return remote(cbuf.at[j, 0, h], ccore.at[j, 0, h], send.at[h], recv.at[h], (d, sibling))
    def sum_near(j, send, recv, h):
        return remote(cbuf.at[j, 1, h], ccore.at[j, 1, h], send.at[2 + h], recv.at[2 + h], (d, sibling))
    def sum_x(j, send, recv, h):
        return remote(xbuf.at[j, h], xin.at[j, h], send.at[4 + h], recv.at[4 + h], (d, cross))
    arrays = (x0, x1, x2)
    outs = (o0, o1, o2)
    size = x0.shape[0] // 2
    part_y = size // 2
    part_z = part_y // 4
    def at(n, start, count):
        return pl.ds(pl.multiple_of((n % 2) * size + start, 16), count)
    def y_copy(n):
        return remote(arrays[n // 2].at[at(n, (1 - side) * part_y, part_y)], ybuf.at[n], y_s.at[n], y_r.at[n], (neighbour, t))
    def z_copy(n, k):
        to = lax.rem(col + k, 4)
        return remote(arrays[n // 2].at[at(n, side * part_y + to * part_z, part_z)], zbuf.at[n, k - 1], z_s.at[n, k], z_r.at[n, k], (to * 2 + side, t))
    def g_copy(n, k):
        to = lax.rem(col + k, 4)
        here = outs[n // 2].at[at(n, side * part_y + col * part_z, part_z)]
        return remote(here, here, g_s.at[n, k], g_r.at[n, k], (to * 2 + side, t))
    def e_copy(n):
        here = outs[n // 2].at[at(n, side * part_y, part_y)]
        return remote(here, here, e_s.at[n], e_r.at[n], (neighbour, t))
    def start_y(n):
        y_copy(n).start()
    def step_a(n):
        y_copy(n).wait()
        here = at(n, side * part_y, part_y)
        arrays[n // 2][here] = (arrays[n // 2][here].astype(F32) + ybuf[n].astype(F32)).astype(BF)
        for k in range(1, 4):
            z_copy(n, k).start()
    def step_b(n):
        for k in range(1, 4):
            z_copy(n, k).wait()
        here = at(n, side * part_y + col * part_z, part_z)
        total = arrays[n // 2][here].astype(F32)
        for k in range(3):
            total = total + zbuf[n, k].astype(F32)
        outs[n // 2][here] = total.astype(BF)
        for k in range(1, 4):
            g_copy(n, k).start()
    def step_d(n):
        for k in range(1, 4):
            g_copy(n, k).wait()
        e_copy(n).start()
    if not sums:
        start_y = step_a = step_b = step_d = lambda n: None

    scaled, inverse = moments(hidden[...].astype(F32))
    g1[rows_at(t)] = (scaled * row(gain1) + row(shift1)).astype(BF)
    pl.semaphore_wait(barrier, 10 if sums else 3)
    for h in range(2):
        gather_x(g1, h_s, h_r, h).start()
        gather_near(g1, h_s, h_r, h).start()
    alive = live_of(t, rows, res, counts)
    gm[rows_at(t)] = (cot[...].astype(F32) * alive * row(scale2)).astype(BF)
    ilo[...] = jnp.zeros_like(ilo)
    ilo[0:P_LO, 0:P_LO] = ilo_in[...]
    ihi[...] = jnp.zeros_like(ihi)
    ihi[0:P_HI, 0:P_HI] = ihi_in[...]
    for table, packed in ((table_lo, tab_lo), (table_hi, tab_hi)):
        nch = packed.shape[1]
        raw[...] = jnp.zeros_like(raw)
        raw[:, 0:table.shape[1]] = table[...]
        for k in range(nch):
            low = (raw[:, k * 128:(k + 1) * 128] * PACK + 32768.5).astype(jnp.int32) - 32768
            high = (raw[:, (k + nch) * 128:(k + nch + 1) * 128] * PACK + 32768.5).astype(jnp.int32) - 32768
            word = (high << 16) | (low & 65535)
            for h in range(heads):
                packed[h, k] = jnp.broadcast_to(word[h:h + 1, :], (8, 128))
    look = functools.partial(bias_rows, res, tab_lo, tab_hi, ilo, ihi, pb)
    n_low = -(-P_LO // 16)
    n_high = -(-P_HI // 16)
    middle = (n_low + n_high) // 2
    look(0, n_low, True)
    look(n_low, middle, False)
    for h in range(2):
        gather_x(g1, h_s, h_r, h).wait()
        gather_on(g1, h_s, h_r, h).start()
        gather_x(gm, m_s, m_r, h).start()
        gather_near(gm, m_s, m_r, h).start()
    look(middle, n_high, False)
    pb[:, :, n_high * 16:, :] = jnp.zeros((slots, heads, SEQ - n_high * 16, SEQ), BF)
    for h in range(2):
        gather_near(g1, h_s, h_r, h).wait()
        gather_on(g1, h_s, h_r, h).wait()

    def project(i, c):
        here = rows_at(i)
        g = g1[here]
        q_buf[here] = ((lax.dot_general(g, wq[...], NT, preferred_element_type=F32) + row(bq)) * scale).astype(BF)
        k_buf[here] = lax.dot_general(g, wk[...], NT, preferred_element_type=F32).astype(BF)
        v_buf[here] = (lax.dot_general(g, wv[...], NT, preferred_element_type=F32) + row(bv)).astype(BF)
        return c
    lax.fori_loop(0, 4, project, 0)

    def attend_image(slot):
        here = pl.ds(pl.multiple_of(slot * SEQ, 16), SEQ)
        k = k_buf[here]
        v = v_buf[here]
        vm = [v * head_mask(h, width) for h in range(heads)]
        def piece(i, c):
            first = pl.multiple_of(i * rows, 16)
            there = pl.ds(pl.multiple_of(slot * SEQ + first, 16), rows)
            q = q_buf[there]
            out = jnp.zeros((rows, width), F32)
            for h in range(heads):
                s = lax.dot_general(q * head_mask(h, width), k, NT, preferred_element_type=F32)
                s = s + pb[slot, h, pl.ds(first, rows)].astype(F32)
                peak = jnp.max(s, axis=1, keepdims=True)
                e = jnp.exp(s - peak)
                total = jnp.sum(e, axis=1, keepdims=True)
                p = (e * (1.0 / total)).astype(BF)
                pb[slot, h, pl.ds(first, rows)] = p
                out = out + jnp.dot(p, vm[h], preferred_element_type=F32)
            mix[there] = out.astype(BF)
            return c
        lax.fori_loop(0, SEQ // rows, piece, 0)
    def output_of(who, h):
        return jnp.dot(mix[span(who, h)], wo[...], preferred_element_type=F32)

    mine = t * rows // SEQ
    attend_image(1 - mine)
    for h in range(2):
        cbuf[0, 0, h] = output_of(diag, h).astype(BF)
        sum_far(0, o_s, o_r, h).start()
    for h in range(2):
        total = output_of(cross, h)
        sum_far(0, o_s, o_r, h).wait()
        xbuf[0, h] = (total + ccore[0, 0, h].astype(F32)).astype(BF)
        sum_x(0, o_s, o_r, h).start()
    attend_image(mine)
    for h in range(2):
        cbuf[0, 1, h] = output_of(sibling, h).astype(BF)
        sum_near(0, o_s, o_r, h).start()
    for h in range(2):
        acc[pl.ds(h * half, half)] = output_of(t, h)
    for h in range(2):
        gather_x(gm, m_s, m_r, h).wait()
        gather_on(gm, m_s, m_r, h).start()
    for h in range(2):
        here = pl.ds(h * half, half)
        sum_near(0, o_s, o_r, h).wait()
        sum_x(0, o_s, o_r, h).wait()
        out = acc[here] + ccore[0, 1, h].astype(F32) + xin[0, h].astype(F32) + row(bo)
        attn[here] = out
        scaled, inverse = moments(hidden[here].astype(F32) + row(scale1) * out)
        gt[span(t, h)] = (scaled * row(gain2) + row(shift2)).astype(BF)
        gather_x(gt, t_s, t_r, h).start()
        gather_near(gt, t_s, t_r, h).start()

    esum[...] = jnp.zeros_like(esum)
    def feed(who, h):
        here = span(who, h)
        pre = jnp.dot(gt[here], we[...], preferred_element_type=F32) + row(be)
        grad = lax.dot_general(gm[here], wr[...], NT, preferred_element_type=F32)
        phi = 0.5 * (1.0 + lax.erf(pre * inv_sqrt_two))
        active = (pre * phi).astype(BF)
        act[here] = active
        grad = grad * (phi + pre * inv_sqrt_two_pi * jnp.exp(-0.5 * pre * pre))
        esum[...] += jnp.sum(grad, axis=0, keepdims=True)
        grad = grad.astype(BF)
        pgl[here] = grad
        part[here] = jnp.dot(active, wr[...], preferred_element_type=F32).astype(BF)
        return lax.dot_general(grad, we[...], NT, preferred_element_type=F32)
    def feed_own(h, c):
        acc[pl.ds(pl.multiple_of(h * half, 16), half)] = feed(t, h)
        return c
    lax.fori_loop(0, 2, feed_own, 0)
    for h in range(2):
        gather_near(gm, m_s, m_r, h).wait()
        gather_near(gt, t_s, t_r, h).wait()
        gather_on(gm, m_s, m_r, h).wait()
    def feed_rest(h, c):
        gather_x(gt, t_s, t_r, h).wait()
        gather_on(gt, t_s, t_r, h).start()
        cbuf[1, 1, h] = feed(sibling, h).astype(BF)
        sum_near(1, n_s, n_r, h).start()
        gather_on(gt, t_s, t_r, h).wait()
        cbuf[1, 0, h] = feed(diag, h).astype(BF)
        sum_far(1, n_s, n_r, h).start()
        total = feed(cross, h)
        sum_far(1, n_s, n_r, h).wait()
        xbuf[1, h] = (total + ccore[1, 0, h].astype(F32)).astype(BF)
        sum_x(1, n_s, n_r, h).start()
        return c
    lax.fori_loop(0, 2, feed_rest, 0)

    tile = 128
    def reduce_grad(i, c):
        cols = pl.ds(pl.multiple_of(i * tile, tile), tile)
        x0[cols] = lax.dot_general(act[:, cols], gm[...], TN, preferred_element_type=F32).astype(BF)
        return c
    lax.fori_loop(0, act.shape[1] // tile, reduce_grad, 0)
    start_y(0)
    wmine[...] = jnp.zeros_like(wmine)
    def second_back(h):
        here = pl.ds(h * half, half)
        sum_near(1, n_s, n_r, h).wait()
        sum_x(1, n_s, n_r, h).wait()
        grad = acc[here] + ccore[1, 1, h].astype(F32) + xin[1, h].astype(F32)
        out = attn[here]
        scaled, inverse = moments(hidden[here].astype(F32) + row(scale1) * out)
        after = cot[here].astype(F32) * alive[h * half:(h + 1) * half] + norm_back(grad, scaled, inverse, row(gain2))
        hidden_grad[here] = after
        agrad = after * row(scale1)
        ga[span(t, h)] = agrad.astype(BF)
        gather_x(ga, a_s, a_r, h).start()
        gather_near(ga, a_s, a_r, h).start()
        wmine[2:3, :] += jnp.sum(after * out, axis=0, keepdims=True)
        wmine[3:4, :] += jnp.sum(agrad, axis=0, keepdims=True)
        wmine[4:5, :] += jnp.sum(grad * scaled, axis=0, keepdims=True)
        wmine[5:6, :] += jnp.sum(grad, axis=0, keepdims=True)
    second_back(0)
    def expand_grad(i, c):
        cols = pl.ds(pl.multiple_of(i * tile, tile), tile)
        x1[cols] = lax.dot_general(gt[:, cols], pgl[...], TN, preferred_element_type=F32).astype(BF)
        return c
    lax.fori_loop(0, gt.shape[1] // tile, expand_grad, 0)
    start_y(1)
    second_back(1)
    step_a(0)
    start_y(2)
    def mixture_of(who):
        here = rows_at(who)
        dmix[here] = lax.dot_general(ga[here], wo[...], NT, preferred_element_type=F32).astype(BF)
    mixture_of(t)
    step_a(1)
    start_y(3)
    gather_x(ga, a_s, a_r, 0).wait()
    gather_on(ga, a_s, a_r, 0).start()
    for h in range(2):
        gather_near(ga, a_s, a_r, h).wait()
    step_b(0)
    mixture_of(sibling)
    gather_x(ga, a_s, a_r, 1).wait()
    gather_on(ga, a_s, a_r, 1).start()
    mixture_of(cross)
    for h in range(2):
        gather_on(ga, a_s, a_r, h).wait()
    mixture_of(diag)

    smine[...] = jnp.zeros_like(smine)
    smine[1:2, :] = esum[...]
    def attention_back(slot):
        here = slice(slot * SEQ, (slot + 1) * SEQ)
        q = q_buf[here]
        k = k_buf[here]
        v = v_buf[here]
        dd = dmix[here]
        qt = q.T
        dt = dd.T
        is_high = jnp.where(res[slot] == 1, 1.0, 0.0).astype(F32)
        out = jnp.zeros((SEQ, width), F32)
        dks = []
        dvs = []
        nh = ghi.shape[1]
        nl, ml = glo.shape[1:]
        for h in range(heads):
            mask = head_mask(h, width)
            p = pb[slot, h]
            dp = lax.dot_general(dd * mask, v, NT, preferred_element_type=F32)
            pf = p.astype(F32)
            m = pf * dp
            ds = m - pf * jnp.sum(m, axis=1, keepdims=True)
            if slot == 0:
                ghi[h] = ds[:nh] * is_high
                glo[h] = ds[:nl, :ml] * (1.0 - is_high)
            else:
                ghi[h] += ds[:nh] * is_high
                glo[h] += ds[:nl, :ml] * (1.0 - is_high)
            low = ds.astype(BF)
            out = out + jnp.dot(low, k * mask, preferred_element_type=F32)
            dks.append(jnp.dot(qt[h*HD:(h+1)*HD], low, preferred_element_type=F32))
            dvs.append(jnp.dot(dt[h*HD:(h+1)*HD], p, preferred_element_type=F32))
        out = out * scale
        smine[0:1, 0:width] += jnp.sum(out, axis=0, keepdims=True)
        q_buf[here] = out.astype(BF)
        k_buf[here] = jnp.concatenate(dks, axis=0).T.astype(BF)
        out = jnp.concatenate(dvs, axis=0).T
        smine[0:1, 256:256 + width] += jnp.sum(out, axis=0, keepdims=True)
        v_buf[here] = out.astype(BF)
    attention_back(0)
    step_a(2)
    attention_back(1)

    def back(who):
        here = rows_at(who)
        total = jnp.dot(q_buf[here], wq[...], preferred_element_type=F32)
        total = total + jnp.dot(k_buf[here], wk[...], preferred_element_type=F32)
        return total + jnp.dot(v_buf[here], wv[...], preferred_element_type=F32)
    def send(buf, value):
        for h in range(2):
            buf[h] = value[h * half:(h + 1) * half].astype(BF)
    def whole(ref):
        return jnp.concatenate([ref[0], ref[1]], axis=0).astype(F32)
    a_far = remote(cbuf.at[0, 0], acore.at[0], r_s.at[0], r_r.at[0], (d, sibling))
    a_near = remote(cbuf.at[0, 1], acore.at[1], r_s.at[1], r_r.at[1], (d, sibling))
    a_cross = remote(xbuf.at[0], across, r_s.at[2], r_r.at[2], (d, cross))
    b_far = remote(part.at[rows_at(diag)], bcore.at[0], r_s.at[3], r_r.at[3], (d, sibling))
    b_near = remote(part.at[rows_at(sibling)], bcore.at[1], r_s.at[4], r_r.at[4], (d, sibling))
    b_cross = remote(xbuf.at[1], bcross, r_s.at[5], r_r.at[5], (d, cross))
    send(cbuf.at[0, 0], back(diag))
    a_far.start()
    b_far.start()
    step_a(3)
    total = back(cross)
    a_far.wait()
    send(xbuf.at[0], total + whole(acore.at[0]))
    a_cross.start()
    for j, (left, right) in enumerate(((q_buf, g1), (k_buf, g1), (v_buf, g1), (mix, ga))):
        x2[j * width:(j + 1) * width, :] = lax.dot_general(left[...], right[...], TN, preferred_element_type=F32).astype(BF)
    step_b(1)
    start_y(4)
    send(cbuf.at[0, 1], back(sibling))
    a_near.start()
    b_near.start()
    acc[...] = back(t)
    b_far.wait()
    send(xbuf.at[1], part[rows_at(cross)].astype(F32) + bcore[0].astype(F32))
    step_b(2)
    start_y(5)
    n_hi = -(-P_HI // UN)
    done = [0]
    def scatter_part(count):
        first, last = done[0], min(done[0] + count, n_hi)
        scatter_run(ihi, ghi, thi, first, last, first == 0)
        done[0] = last
    scatter_part(4)
    step_d(0)
    step_b(3)
    step_d(1)
    step_a(4)
    a_cross.wait()
    b_cross.start()
    a_near.wait()
    grad = acc[...] + whole(acore.at[1]) + whole(across)
    scaled, inverse = moments(hidden[...].astype(F32))
    wmine[0:1, :] = jnp.sum(grad * scaled, axis=0, keepdims=True)
    wmine[1:2, :] = jnp.sum(grad, axis=0, keepdims=True)
    hidden_grad[...] += norm_back(grad, scaled, inverse, row(gain1))
    scatter_part(8)
    step_a(5)
    step_d(2)
    scatter_part(4)
    b_near.wait()
    b_cross.wait()
    out = part[rows_at(t)].astype(F32) + bcore[1].astype(F32) + whole(bcross) + row(rbias)
    after = hidden[...].astype(F32) + row(scale1) * attn[...]
    result[...] = ((after + row(scale2) * out) * alive).astype(BF)
    up = cot[...].astype(F32) * alive
    wmine[6:7, :] = jnp.sum(up * out, axis=0, keepdims=True)
    wmine[7:8, :] = jnp.sum(up * row(scale2), axis=0, keepdims=True)
    def w_copy(k):
        return remote(wmine, wten.at[k], w_s.at[k], w_r.at[k], (d, lax.rem(t + k, 4)))
    def eighth(buf, who):
        count = buf.shape[0] // 8
        return buf.at[pl.ds(pl.multiple_of(who * count, 8), count)]
    def v_copy(j, k):
        buf, land = ((vec, vland), (tbl, tland))[j]
        to = lax.rem(d + k, 8)
        return remote(eighth(buf, to), land.at[k], v_s.at[j, k], v_r.at[j, k], (to, t))
    def u_copy(j, k):
        buf = (vout, tout)[j]
        return remote(eighth(buf, d), eighth(buf, d), v_s.at[2 + j, k], v_r.at[2 + j, k], (lax.rem(d + k, 8), t))
    def small_start(j):
        for k in range(1, 8):
            v_copy(j, k).start()
    def small_turn(j):
        buf, land = ((vec, vland), (tbl, tland))[j]
        total = eighth(buf, d)[...]
        for k in range(1, 8):
            v_copy(j, k).wait()
            total = total + land[k]
        eighth((vout, tout)[j], d)[...] = total
        for k in range(1, 8):
            u_copy(j, k).start()
    def small_end(j):
        for k in range(1, 8):
            u_copy(j, k).wait()
    if not sums:
        def small_turn(j):
            (vout, tout)[j][...] = (vec, tbl)[j][...]
        small_start = small_end = lambda j: None
    if sums:
        for k in range(1, 4):
            w_copy(k).start()
    step_d(3)
    scatter_part(4)
    step_b(4)
    total = wmine[...]
    if sums:
        for k in range(1, 4):
            w_copy(k).wait()
            total = total + wten[k]
    vec[...] = jnp.zeros_like(vec)
    lanes = model // 128
    for r in range(8):
        for j in range(lanes):
            vec[r * lanes + j:r * lanes + j + 1, :] = total[r:r + 1, j * 128:(j + 1) * 128]
    for r in range(2):
        for j in range(lanes):
            vec[(8 + r) * lanes + j:(8 + r) * lanes + j + 1, :] = smine[r:r + 1, j * 128:(j + 1) * 128]
    small_start(0)
    scatter_part(4)
    step_b(5)
    scatter_part(4)
    small_turn(0)
    step_d(4)
    scatter_part(n_hi)
    step_d(5)
    scatter_run(ilo, glo, tlo, 0, -(-P_LO // UN), True)
    per = (thi.shape[1] + tlo.shape[1]) // 4
    tbl[...] = jnp.zeros_like(tbl)
    def spread(src, base):
        count = src.shape[1] // 4
        for h in range(heads):
            flip[0:src.shape[1], :] = src[h * BB:(h + 1) * BB, :].T
            pieces = [flip[pl.ds(i, count, stride=4), :] for i in range(4)]
            start = h * per + base
            tbl[start:start + count, :] = jnp.concatenate(pieces, axis=1)
    spread(thi, 0)
    spread(tlo, thi.shape[1] // 4)
    if not sums:
        o0[...] = x0[...]
        o1[...] = x1[...]
        o2[...] = x2[...]
    small_start(1)
    small_end(0)
    for r in range(10):
        for j in range(lanes):
            small[r:r + 1, j * 128:(j + 1) * 128] = vout[r * lanes + j:r * lanes + j + 1, :]
    small_turn(1)
    small_end(1)
    for src, base, count in ((thigh, 0, thi.shape[1] // 4), (tlow, thi.shape[1] // 4, tlo.shape[1] // 4)):
        for h in range(heads):
            for r in range(count):
                at_row = h * per + base + r
                src[h:h + 1, r * 128:(r + 1) * 128] = tout[at_row:at_row + 1, :]
    if sums:
        for n in range(CHUNKS):
            e_copy(n).wait()

def layer(scale, sums, res, counts, hidden, gain1, shift1, wq, bq, wk, wv, bv, wo, bo, scale1, gain2, shift2, we, be, wr, rbias, scale2, cot, table_low, table_high, ilo, ihi, n_lo, n_hi):
    rows, model = hidden.shape
    total = rows * 4
    width = wq.shape[0]
    inner = we.shape[1]
    heads, e_lo = table_low.shape
    e_hi = table_high.shape[1]
    vm = pl.BlockSpec(memory_space=pltpu.VMEM)
    sm = pl.BlockSpec(memory_space=pltpu.SMEM)
    dma = pltpu.SemaphoreType.DMA
    V = pltpu.VMEM
    S = jax.ShapeDtypeStruct
    operands = (hidden, gain1, shift1, wq, bq, wk, wv, bv, wo, bo, scale1, gain2, shift2, we, be, wr, rbias, scale2, cot, table_low, table_high, ilo, ihi)
    half = rows // 2
    return pl.pallas_call(functools.partial(layer_kernel, scale, sums),
        out_shape=(S((inner, model), BF), S((model, inner), BF), S((4 * width, model), BF), S((rows, model), BF), S((rows, model), F32), S((16, model), F32), S((heads, n_lo * 32), F32), S((heads, n_hi * 32), F32)),
        in_specs=[sm, sm] + [vm] * len(operands), out_specs=(vm,) * 8,
        scratch_shapes=[V((heads, -(-e_lo // 256), 8, 128), jnp.int32), V((heads, -(-e_hi // 256), 8, 128), jnp.int32), V((heads, -(-e_hi // 256) * 256), F32), V((208, 256), jnp.int32), V((592, SEQ), jnp.int32), V((n_hi, BB), F32)]
            + [V((total, model), BF)] * 4 + [V((total, width), BF)] * 5 + [V((SLOTS, heads, SEQ, SEQ), BF)]
            + [V((total, inner), BF)] * 2 + [V((total, model), BF)] + [V((rows, model), F32)] * 2
            + [V((inner, model), BF), V((model, inner), BF), V((4 * width, model), BF), V((heads, 592, SEQ), F32), V((heads, 208, 256), F32), V((1, inner), F32)]
            + [V((2, 2, 2, half, model), BF)] * 2 + [V((2, 2, half, model), BF)] * 2
            + [V((2, 2, half, model), BF), V((2, half, model), BF), V((2, rows, model), BF), V((2, half, model), BF)]
            + [V((CHUNKS, 192, model), BF), V((CHUNKS, 3, 48, model), BF)]
            + [V((heads * BB, n_lo), F32), V((heads * BB, n_hi), F32)]
            + [V((8, model), F32)] * 2 + [V((4, 8, model), F32), V((64, 128), F32), V((8, 8, 128), F32), V((64, 128), F32), V((128, 128), F32), V((8, 16, 128), F32), V((128, 128), F32)]
            + [dma((6,))] * 12
            + [dma((CHUNKS,)), dma((CHUNKS,)), dma((CHUNKS, 4)), dma((CHUNKS, 4)), dma((CHUNKS, 4)), dma((CHUNKS, 4)), dma((CHUNKS,)), dma((CHUNKS,)),
               dma((6,)), dma((6,)), dma((4,)), dma((4,)), dma((4, 8)), dma((4, 8))],
        name="layer", cost_estimate=pl.CostEstimate(flops=100 * 10**9, bytes_accessed=60 * 10**6, transcendentals=0),
        compiler_params=pltpu.CompilerParams(collective_id=0, has_side_effects=True, vmem_limit_bytes=63 << 20))(res, counts, *operands)


def local(
    hidden,
    first_gain,
    first_shift,
    query_weight,
    query_bias,
    key_weight,
    value_weight,
    value_bias,
    output_weight,
    output_bias,
    first_scale,
    second_gain,
    second_shift,
    expand_weight,
    expand_bias,
    reduce_weight,
    reduce_bias,
    second_scale,
    table_low,
    table_high,
    resolution,
    counts,
    index_low,
    index_high,
    cotangent,
):
    floating = jnp.float32
    width = query_weight.shape[1]
    n_low = -(-table_low.shape[0] // (BB * 16)) * 16
    n_high = -(-table_high.shape[0] // (BB * 16)) * 16
    known = lax.axis_size("dp") == 8
    reduce_grad, expand_grad, attn_grads, result, hidden_grad, small, low_grad, high_grad = layer(
        HD ** (-0.5),
        known,
        resolution,
        counts,
        hidden,
        first_gain,
        first_shift,
        query_weight.T,
        query_bias,
        key_weight.T,
        value_weight.T,
        value_bias,
        output_weight,
        output_bias,
        first_scale,
        second_gain,
        second_shift,
        expand_weight,
        expand_bias,
        reduce_weight,
        reduce_bias,
        second_scale,
        cotangent,
        table_low.T,
        table_high.T,
        index_low,
        index_high,
        n_low,
        n_high,
    )
    if not known:
        reduce_grad, expand_grad, attn_grads, tail, low_grad, high_grad = lax.psum(
            (
                reduce_grad.astype(floating),
                expand_grad.astype(floating),
                attn_grads.astype(floating),
                small[8:],
                low_grad,
                high_grad,
            ),
            "dp",
        )
        small = jnp.concatenate((lax.psum(small[:8], ("dp", "tensor")), tail), axis=0)
    return (
        result,
        hidden_grad,
        small[0],
        small[1],
        attn_grads[:width].astype(floating).T,
        small[8, :width],
        attn_grads[width : 2 * width].astype(floating).T,
        attn_grads[2 * width : 3 * width].astype(floating).T,
        small[8, 256 : 256 + width],
        attn_grads[3 * width :].astype(floating),
        small[3],
        small[2],
        small[4],
        small[5],
        expand_grad.astype(floating),
        small[9],
        reduce_grad.astype(floating),
        small[7],
        small[6],
        low_grad[:, : table_low.shape[0]].T,
        high_grad[:, : table_high.shape[0]].T,
    )


def solution(mesh):
    in_specs = (
        P(("dp", "tensor"), None),
        P(),
        P(),
        P(None, "tensor"),
        P("tensor"),
        P(None, "tensor"),
        P(None, "tensor"),
        P("tensor"),
        P("tensor", None),
        P(),
        P(),
        P(),
        P(),
        P(None, "tensor"),
        P("tensor"),
        P("tensor", None),
        P(),
        P(),
        P(None, "tensor"),
        P(None, "tensor"),
        P("dp"),
        P("dp"),
        P(),
        P(),
        P(("dp", "tensor"), None),
    )
    out_specs = (
        P(("dp", "tensor"), None),
        P(("dp", "tensor"), None),
        P(),
        P(),
        P(None, "tensor"),
        P("tensor"),
        P(None, "tensor"),
        P(None, "tensor"),
        P("tensor"),
        P("tensor", None),
        P(),
        P(),
        P(),
        P(),
        P(None, "tensor"),
        P("tensor"),
        P("tensor", None),
        P(),
        P(),
        P(None, "tensor"),
        P(None, "tensor"),
    )
    return jax.shard_map(local, mesh=mesh, in_specs=in_specs, out_specs=out_specs, check_vma=False)
```

```python
import functools

import jax
import jax.numpy as jnp
from jax import lax
from jax.experimental import pallas as pl
from jax.experimental.pallas import tpu as pltpu
from jax.sharding import PartitionSpec as P

HD = 64
P_LO = 197
P_HI = 577
SEQ = 640
SLOTS = 2


eps_norm = 1e-06
masked_score = -1e30
inv_sqrt_two = 0.7071067811865476
inv_sqrt_two_pi = 0.3989422804014327


F32=jnp.float32; BF=jnp.bfloat16
NT=(((1,),(1,)),((),()))
def head_mask(h, width):
    lane = lax.broadcasted_iota(jnp.int32, (1, width), 1)
    return ((lane >= h*HD) & (lane < (h+1)*HD)).astype(F32).astype(BF)


BB=32; UN=16
def scatter_run(idx_ref, g_ref, out, first, last, fresh):
    heads = g_ref.shape[0]; na = out.shape[1]; m = idx_ref.shape[1]
    if fresh:
        out[...] = jnp.zeros_like(out)
    ib = lax.broadcasted_iota(jnp.int32, (16, m), 0).astype(F32)
    def body(r, c):
        ms = []; os = []
        for u in range(UN):
            row = r*UN+u
            idx = jnp.broadcast_to(idx_ref[pl.ds(row,1), :], (16, m))
            ia = (idx >> 5).astype(F32).astype(BF); il = (idx & 31).astype(F32).astype(BF)
            g = [jnp.broadcast_to(g_ref[h, pl.ds(row,1), :], (16, m)).astype(BF) for h in range(heads)]
            hits = [il == (ib + 16.0*k).astype(BF) for k in range(BB//16)]
            ms.append(jnp.concatenate([jnp.where(hits[k], g[h], jnp.zeros_like(g[h])) for h in range(heads) for k in range(BB//16)], axis=0))
            os.append(jnp.concatenate([jnp.where(ia == (ib + 16.0*k).astype(BF), jnp.ones_like(ia), jnp.zeros_like(ia)) for k in range(na//16)], axis=0))
        out[...] += lax.dot_general(jnp.concatenate(ms, axis=1), jnp.concatenate(os, axis=1), NT, preferred_element_type=F32)
        return c
    lax.fori_loop(first, last, body, 0)

PACK=8191.0
MESH = pl.DeviceIdType.MESH

CHUNKS = 6
TN = (((0,), (0,)), ((), ()))

def row(ref):
    return ref[...].reshape(1, ref.shape[0])

def live_of(t, rows, res, counts):
    slot = t * rows // SEQ
    first = t * rows - slot * SEQ
    limit = jnp.where(res[slot] == 1, P_HI, P_LO)
    limit = jnp.where(slot < counts[0], limit, 0)
    place = lax.broadcasted_iota(jnp.int32, (rows, 1), 0) + first
    return jnp.where(place < limit, 1.0, 0.0).astype(F32)

def moments(values):
    center = jnp.mean(values, axis=1, keepdims=True)
    centered = values - center
    inverse = lax.rsqrt(jnp.mean(centered * centered, axis=1, keepdims=True) + eps_norm)
    return centered * inverse, inverse

def norm_back(grad, scaled, inverse, gain):
    inner = grad * gain
    mean_inner = jnp.mean(inner, axis=1, keepdims=True)
    mean_mixed = jnp.mean(inner * scaled, axis=1, keepdims=True)
    return inverse * (inner - mean_inner - scaled * mean_mixed)

def look_up(tab, idx, heads):
    nch = tab.shape[1]
    lane = idx & 127
    ch = idx >> 7
    shift = jnp.where(ch >= nch, 0, 16)
    ch = jnp.where(ch >= nch, ch - nch, ch)
    acc = [None] * heads
    for k in range(nch):
        hit = ch == k
        for h in range(heads):
            v = jnp.take_along_axis(tab[h, k], lane, axis=1)
            acc[h] = v if k == 0 else jnp.where(hit, v, acc[h])
    return [((acc[h] << shift) >> 16).astype(F32) * (1.0 / PACK) for h in range(heads)]

def bias_rows(res, tab_lo, tab_hi, idx_lo, idx_hi, out, first, last, both):
    slots, heads = out.shape[:2]
    def masked(vals, j, limit):
        if (j + 1) * 128 <= limit:
            return vals
        place = lax.broadcasted_iota(jnp.int32, (8, 128), 1) + j * 128
        return [jnp.where(place < limit, v, masked_score) for v in vals]
    def body(r, c):
        for j in range(idx_hi.shape[1] // 128):
            cols = pl.ds(j * 128, 128)
            high = []
            low = []
            for part in range(2):
                rows = pl.ds(pl.multiple_of(r * 16 + part * 8, 8), 8)
                high.append(masked(look_up(tab_hi, idx_hi[rows, cols], heads), j, P_HI))
                if both and j < idx_lo.shape[1] // 128:
                    low.append(masked(look_up(tab_lo, idx_lo[rows, cols], heads), j, P_LO))
                else:
                    low.append([jnp.full((8, 128), masked_score, F32)] * heads)
            for h in range(heads):
                hi = jnp.concatenate([high[0][h], high[1][h]], axis=0).astype(BF)
                lo = jnp.concatenate([low[0][h], low[1][h]], axis=0).astype(BF)
                for s in range(slots):
                    out[s, h, pl.ds(pl.multiple_of(r * 16, 16), 16), cols] = jnp.where(res[s] == 1, hi, lo)
        return c
    lax.fori_loop(first, last, body, 0)

def layer_kernel(scale, sums, res, counts, hidden, gain1, shift1, wq, bq, wk, wv, bv, wo, bo, scale1, gain2, shift2, we, be, wr, rbias, scale2, cot,
                 table_lo, table_hi, ilo_in, ihi_in,
                 o0, o1, o2, result, hidden_grad, small, tlow, thigh,
                 tab_lo, tab_hi, raw, ilo, ihi, flip,
                 g1, gm, gt, ga, q_buf, k_buf, v_buf, mix, dmix, pb, act, pgl, part, acc, attn, x0, x1, x2, ghi, glo, esum,
                 cbuf, ccore, xbuf, xin, acore, across, bcore, bcross, ybuf, zbuf,
                 tlo, thi, wmine, smine, wten, vec, vland, vout, tbl, tland, tout,
                 h_s, h_r, m_s, m_r, t_s, t_r, a_s, a_r, o_s, o_r, n_s, n_r,
                 y_s, y_r, z_s, z_r, g_s, g_r, e_s, e_r, r_s, r_r, w_s, w_r, v_s, v_r):
    d = lax.axis_index("dp")
    t = lax.axis_index("tensor")
    col = d // 2
    side = lax.rem(d, 2)
    neighbour = d + 1 - 2 * side
    sibling = t + 1 - 2 * lax.rem(t, 2)
    cross = lax.rem(t + 2, 4)
    diag = 3 - t
    rows = hidden.shape[0]
    half = rows // 2
    slots, heads = pb.shape[:2]
    width = q_buf.shape[1]
    model = g1.shape[1]
    barrier = pltpu.get_barrier_semaphore()
    for k in range(1, 4):
        pl.semaphore_signal(barrier, inc=1, device_id=(d, lax.rem(t + k, 4)), device_id_type=MESH)
    if sums:
        for k in range(1, 8):
            pl.semaphore_signal(barrier, inc=1, device_id=(lax.rem(d + k, 8), t), device_id_type=MESH)

    def remote(src, dst, send, recv, device):
        return pltpu.make_async_remote_copy(src_ref=src, dst_ref=dst, send_sem=send, recv_sem=recv, device_id=device, device_id_type=MESH)
    def rows_at(who):
        return pl.ds(pl.multiple_of(who * rows, 16), rows)
    def span(who, h):
        return pl.ds(pl.multiple_of(who * rows + h * half, 16), half)
    def gather_x(buf, send, recv, h):
        here = buf.at[span(t, h)]
        return remote(here, here, send.at[h], recv.at[h], (d, cross))
    def gather_near(buf, send, recv, h):
        here = buf.at[span(t, h)]
        return remote(here, here, send.at[2 + h], recv.at[2 + h], (d, sibling))
    def gather_on(buf, send, recv, h):
        here = buf.at[span(cross, h)]
        return remote(here, here, send.at[4 + h], recv.at[4 + h], (d, sibling))
    def sum_far(j, send, recv, h):
        return remote(cbuf.at[0, h], ccore.at[j, 0, h], send.at[h], recv.at[h], (d, sibling))
    def sum_near(j, send, recv, h):
        return remote(cbuf.at[1, h], ccore.at[j, 1, h], send.at[2 + h], recv.at[2 + h], (d, sibling))
    def sum_x(j, send, recv, h):
        return remote(xbuf.at[j, h], xin.at[j, h], send.at[4 + h], recv.at[4 + h], (d, cross))
    arrays = (x0, x1, x2)
    outs = (o0, o1, o2)
    size = x0.shape[0] // 2
    part_y = size // 2
    part_z = part_y // 4
    def at(n, start, count):
        return pl.ds(pl.multiple_of((n % 2) * size + start, 16), count)
    def y_copy(n):
        return remote(arrays[n // 2].at[at(n, (1 - side) * part_y, part_y)], ybuf.at[n], y_s.at[n], y_r.at[n], (neighbour, t))
    def z_copy(n, k):
        to = lax.rem(col + k, 4)
        return remote(arrays[n // 2].at[at(n, side * part_y + to * part_z, part_z)], zbuf.at[n, k - 1], z_s.at[n, k], z_r.at[n, k], (to * 2 + side, t))
    def g_copy(n, k):
        to = lax.rem(col + k, 4)
        here = outs[n // 2].at[at(n, side * part_y + col * part_z, part_z)]
        return remote(here, here, g_s.at[n, k], g_r.at[n, k], (to * 2 + side, t))
    def e_copy(n):
        here = outs[n // 2].at[at(n, side * part_y, part_y)]
        return remote(here, here, e_s.at[n], e_r.at[n], (neighbour, t))
    def start_y(n):
        y_copy(n).start()
    def step_a(n):
        y_copy(n).wait()
        here = at(n, side * part_y, part_y)
        arrays[n // 2][here] = (arrays[n // 2][here].astype(F32) + ybuf[n].astype(F32)).astype(BF)
        for k in range(1, 4):
            z_copy(n, k).start()
    def step_b(n):
        for k in range(1, 4):
            z_copy(n, k).wait()
        here = at(n, side * part_y + col * part_z, part_z)
        total = arrays[n // 2][here].astype(F32)
        for k in range(3):
            total = total + zbuf[n, k].astype(F32)
        outs[n // 2][here] = total.astype(BF)
        for k in range(1, 4):
            g_copy(n, k).start()
    def step_d(n):
        for k in range(1, 4):
            g_copy(n, k).wait()
        e_copy(n).start()
    if not sums:
        start_y = step_a = step_b = step_d = lambda n: None

    scaled, inverse = moments(hidden[...].astype(F32))
    g1[rows_at(t)] = (scaled * row(gain1) + row(shift1)).astype(BF)
    pl.semaphore_wait(barrier, 10 if sums else 3)
    for h in range(2):
        gather_x(g1, h_s, h_r, h).start()
        gather_near(g1, h_s, h_r, h).start()
    alive = live_of(t, rows, res, counts)
    gm[rows_at(t)] = (cot[...].astype(F32) * alive * row(scale2)).astype(BF)
    ilo[...] = jnp.zeros_like(ilo)
    ilo[0:P_LO, 0:P_LO] = ilo_in[...]
    ihi[...] = jnp.zeros_like(ihi)
    ihi[0:P_HI, 0:P_HI] = ihi_in[...]
    for table, packed in ((table_lo, tab_lo), (table_hi, tab_hi)):
        nch = packed.shape[1]
        raw[...] = jnp.zeros_like(raw)
        raw[:, 0:table.shape[1]] = table[...]
        for k in range(nch):
            low = (raw[:, k * 128:(k + 1) * 128] * PACK + 32768.5).astype(jnp.int32) - 32768
            high = (raw[:, (k + nch) * 128:(k + nch + 1) * 128] * PACK + 32768.5).astype(jnp.int32) - 32768
            word = (high << 16) | (low & 65535)
            for h in range(heads):
                packed[h, k] = jnp.broadcast_to(word[h:h + 1, :], (8, 128))
    look = functools.partial(bias_rows, res, tab_lo, tab_hi, ilo, ihi, pb)
    n_low = -(-P_LO // 16)
    n_high = -(-P_HI // 16)
    middle = (n_low + n_high) // 2
    look(0, n_low, True)
    look(n_low, middle, False)
    for h in range(2):
        gather_x(g1, h_s, h_r, h).wait()
        gather_on(g1, h_s, h_r, h).start()
        gather_x(gm, m_s, m_r, h).start()
        gather_near(gm, m_s, m_r, h).start()
    look(middle, n_high, False)
    pb[:, :, n_high * 16:, :] = jnp.zeros((slots, heads, SEQ - n_high * 16, SEQ), BF)
    for h in range(2):
        gather_near(g1, h_s, h_r, h).wait()
        gather_on(g1, h_s, h_r, h).wait()

    def project(i, c):
        here = rows_at(i)
        g = g1[here]
        q_buf[here] = ((lax.dot_general(g, wq[...], NT, preferred_element_type=F32) + row(bq)) * scale).astype(BF)
        k_buf[here] = lax.dot_general(g, wk[...], NT, preferred_element_type=F32).astype(BF)
        v_buf[here] = (lax.dot_general(g, wv[...], NT, preferred_element_type=F32) + row(bv)).astype(BF)
        return c
    lax.fori_loop(0, 4, project, 0)

    def attend_image(slot):
        here = pl.ds(pl.multiple_of(slot * SEQ, 16), SEQ)
        k = k_buf[here]
        v = v_buf[here]
        vm = [v * head_mask(h, width) for h in range(heads)]
        def piece(i, c):
            first = pl.multiple_of(i * rows, 16)
            there = pl.ds(pl.multiple_of(slot * SEQ + first, 16), rows)
            q = q_buf[there]
            out = jnp.zeros((rows, width), F32)
            for h in range(heads):
                s = lax.dot_general(q * head_mask(h, width), k, NT, preferred_element_type=F32)
                s = s + pb[slot, h, pl.ds(first, rows)].astype(F32)
                peak = jnp.max(s, axis=1, keepdims=True)
                e = jnp.exp(s - peak)
                total = jnp.sum(e, axis=1, keepdims=True)
                p = (e * (1.0 / total)).astype(BF)
                pb[slot, h, pl.ds(first, rows)] = p
                out = out + jnp.dot(p, vm[h], preferred_element_type=F32)
            mix[there] = out.astype(BF)
            return c
        lax.fori_loop(0, SEQ // rows, piece, 0)
    def output_of(who, h):
        return jnp.dot(mix[span(who, h)], wo[...], preferred_element_type=F32)

    mine = t * rows // SEQ
    attend_image(1 - mine)
    for h in range(2):
        cbuf[0, h] = output_of(diag, h).astype(BF)
        sum_far(0, o_s, o_r, h).start()
    for h in range(2):
        total = output_of(cross, h)
        sum_far(0, o_s, o_r, h).wait()
        xbuf[0, h] = (total + ccore[0, 0, h].astype(F32)).astype(BF)
        sum_x(0, o_s, o_r, h).start()
    attend_image(mine)
    for h in range(2):
        cbuf[1, h] = output_of(sibling, h).astype(BF)
        sum_near(0, o_s, o_r, h).start()
    for h in range(2):
        acc[pl.ds(h * half, half)] = output_of(t, h)
    for h in range(2):
        gather_x(gm, m_s, m_r, h).wait()
        gather_on(gm, m_s, m_r, h).start()
    for h in range(2):
        here = pl.ds(h * half, half)
        sum_near(0, o_s, o_r, h).wait()
        sum_x(0, o_s, o_r, h).wait()
        out = acc[here] + ccore[0, 1, h].astype(F32) + xin[0, h].astype(F32) + row(bo)
        attn[here] = out
        scaled, inverse = moments(hidden[here].astype(F32) + row(scale1) * out)
        gt[span(t, h)] = (scaled * row(gain2) + row(shift2)).astype(BF)
        gather_x(gt, t_s, t_r, h).start()
        gather_near(gt, t_s, t_r, h).start()

    esum[...] = jnp.zeros_like(esum)
    def feed(who, h):
        here = span(who, h)
        pre = jnp.dot(gt[here], we[...], preferred_element_type=F32) + row(be)
        grad = lax.dot_general(gm[here], wr[...], NT, preferred_element_type=F32)
        phi = 0.5 * (1.0 + lax.erf(pre * inv_sqrt_two))
        active = (pre * phi).astype(BF)
        act[here] = active
        grad = grad * (phi + pre * inv_sqrt_two_pi * jnp.exp(-0.5 * pre * pre))
        esum[...] += jnp.sum(grad, axis=0, keepdims=True)
        grad = grad.astype(BF)
        pgl[here] = grad
        part[here] = jnp.dot(active, wr[...], preferred_element_type=F32).astype(BF)
        return lax.dot_general(grad, we[...], NT, preferred_element_type=F32)
    def feed_own(h, c):
        acc[pl.ds(pl.multiple_of(h * half, 16), half)] = feed(t, h)
        return c
    lax.fori_loop(0, 2, feed_own, 0)
    for h in range(2):
        gather_near(gm, m_s, m_r, h).wait()
        gather_near(gt, t_s, t_r, h).wait()
        gather_on(gm, m_s, m_r, h).wait()
    def feed_near(h, c):
        cbuf[1, h] = feed(sibling, h).astype(BF)
        sum_near(1, n_s, n_r, h).start()
        return c
    lax.fori_loop(0, 2, feed_near, 0)
    def feed_far(h, c):
        gather_x(gt, t_s, t_r, h).wait()
        gather_on(gt, t_s, t_r, h).start()
        total = feed(cross, h)
        gather_on(gt, t_s, t_r, h).wait()
        cbuf[0, h] = feed(diag, h).astype(BF)
        sum_far(1, n_s, n_r, h).start()
        sum_far(1, n_s, n_r, h).wait()
        xbuf[1, h] = (total + ccore[1, 0, h].astype(F32)).astype(BF)
        sum_x(1, n_s, n_r, h).start()
        return c
    lax.fori_loop(0, 2, feed_far, 0)

    tile = 128
    def reduce_grad(i, c):
        cols = pl.ds(pl.multiple_of(i * tile, tile), tile)
        x0[cols] = lax.dot_general(act[:, cols], gm[...], TN, preferred_element_type=F32).astype(BF)
        return c
    count = act.shape[1] // tile
    lax.fori_loop(0, count // 2, reduce_grad, 0)
    start_y(0)
    lax.fori_loop(count // 2, count, reduce_grad, 0)
    wmine[...] = jnp.zeros_like(wmine)
    def second_back(h):
        here = pl.ds(h * half, half)
        sum_near(1, n_s, n_r, h).wait()
        sum_x(1, n_s, n_r, h).wait()
        grad = acc[here] + ccore[1, 1, h].astype(F32) + xin[1, h].astype(F32)
        out = attn[here]
        scaled, inverse = moments(hidden[here].astype(F32) + row(scale1) * out)
        after = cot[here].astype(F32) * alive[h * half:(h + 1) * half] + norm_back(grad, scaled, inverse, row(gain2))
        hidden_grad[here] = after
        agrad = after * row(scale1)
        ga[span(t, h)] = agrad.astype(BF)
        gather_x(ga, a_s, a_r, h).start()
        gather_near(ga, a_s, a_r, h).start()
        wmine[2:3, :] += jnp.sum(after * out, axis=0, keepdims=True)
        wmine[3:4, :] += jnp.sum(agrad, axis=0, keepdims=True)
        wmine[4:5, :] += jnp.sum(grad * scaled, axis=0, keepdims=True)
        wmine[5:6, :] += jnp.sum(grad, axis=0, keepdims=True)
    start_y(1)
    second_back(0)
    def expand_grad(i, c):
        cols = pl.ds(pl.multiple_of(i * tile, tile), tile)
        x1[cols] = lax.dot_general(gt[:, cols], pgl[...], TN, preferred_element_type=F32).astype(BF)
        return c
    lax.fori_loop(0, gt.shape[1] // tile, expand_grad, 0)
    step_a(0)
    start_y(2)
    second_back(1)
    step_a(1)
    def mixture_of(who):
        here = rows_at(who)
        dmix[here] = lax.dot_general(ga[here], wo[...], NT, preferred_element_type=F32).astype(BF)
    mixture_of(t)
    gather_x(ga, a_s, a_r, 0).wait()
    gather_on(ga, a_s, a_r, 0).start()
    start_y(3)
    for h in range(2):
        gather_near(ga, a_s, a_r, h).wait()
    mixture_of(sibling)
    step_b(0)
    gather_x(ga, a_s, a_r, 1).wait()
    gather_on(ga, a_s, a_r, 1).start()
    mixture_of(cross)
    step_b(1)
    for h in range(2):
        gather_on(ga, a_s, a_r, h).wait()
    mixture_of(diag)

    smine[...] = jnp.zeros_like(smine)
    smine[1:2, :] = esum[...]
    def attention_back(slot):
        here = slice(slot * SEQ, (slot + 1) * SEQ)
        q = q_buf[here]
        k = k_buf[here]
        v = v_buf[here]
        dd = dmix[here]
        qt = q.T
        dt = dd.T
        is_high = jnp.where(res[slot] == 1, 1.0, 0.0).astype(F32)
        out = jnp.zeros((SEQ, width), F32)
        dks = []
        dvs = []
        nh = ghi.shape[1]
        nl, ml = glo.shape[1:]
        for h in range(heads):
            mask = head_mask(h, width)
            p = pb[slot, h]
            dp = lax.dot_general(dd * mask, v, NT, preferred_element_type=F32)
            pf = p.astype(F32)
            m = pf * dp
            ds = m - pf * jnp.sum(m, axis=1, keepdims=True)
            if slot == 0:
                ghi[h] = ds[:nh] * is_high
                glo[h] = ds[:nl, :ml] * (1.0 - is_high)
            else:
                ghi[h] += ds[:nh] * is_high
                glo[h] += ds[:nl, :ml] * (1.0 - is_high)
            low = ds.astype(BF)
            out = out + jnp.dot(low, k * mask, preferred_element_type=F32)
            dks.append(jnp.dot(qt[h*HD:(h+1)*HD], low, preferred_element_type=F32))
            dvs.append(jnp.dot(dt[h*HD:(h+1)*HD], p, preferred_element_type=F32))
        out = out * scale
        smine[0:1, 0:width] += jnp.sum(out, axis=0, keepdims=True)
        q_buf[here] = out.astype(BF)
        k_buf[here] = jnp.concatenate(dks, axis=0).T.astype(BF)
        out = jnp.concatenate(dvs, axis=0).T
        smine[0:1, 256:256 + width] += jnp.sum(out, axis=0, keepdims=True)
        v_buf[here] = out.astype(BF)
    attention_back(0)
    step_a(2)
    step_d(0)
    attention_back(1)

    def back(who):
        here = rows_at(who)
        total = jnp.dot(q_buf[here], wq[...], preferred_element_type=F32)
        total = total + jnp.dot(k_buf[here], wk[...], preferred_element_type=F32)
        return total + jnp.dot(v_buf[here], wv[...], preferred_element_type=F32)
    def send(buf, value):
        for h in range(2):
            buf[h] = value[h * half:(h + 1) * half].astype(BF)
    def whole(ref):
        return jnp.concatenate([ref[0], ref[1]], axis=0).astype(F32)
    a_far = remote(cbuf.at[0], acore.at[0], r_s.at[0], r_r.at[0], (d, sibling))
    a_near = remote(cbuf.at[1], acore.at[1], r_s.at[1], r_r.at[1], (d, sibling))
    a_cross = remote(xbuf.at[0], across, r_s.at[2], r_r.at[2], (d, cross))
    b_far = remote(part.at[rows_at(diag)], bcore.at[0], r_s.at[3], r_r.at[3], (d, sibling))
    b_near = remote(part.at[rows_at(sibling)], bcore.at[1], r_s.at[4], r_r.at[4], (d, sibling))
    b_cross = remote(xbuf.at[1], bcross, r_s.at[5], r_r.at[5], (d, cross))
    send(cbuf.at[0], back(diag))
    a_far.start()
    b_far.start()
    step_d(1)
    total = back(cross)
    step_a(3)
    a_far.wait()
    send(xbuf.at[0], total + whole(acore.at[0]))
    a_cross.start()
    for j, (left, right) in enumerate(((q_buf, g1), (k_buf, g1), (v_buf, g1), (mix, ga))):
        x2[j * width:(j + 1) * width, :] = lax.dot_general(left[...], right[...], TN, preferred_element_type=F32).astype(BF)
        if j == 1:
            start_y(4)
    start_y(5)
    send(cbuf.at[1], back(sibling))
    a_near.start()
    b_near.start()
    acc[...] = back(t)
    step_b(2)
    b_far.wait()
    send(xbuf.at[1], part[rows_at(cross)].astype(F32) + bcore[0].astype(F32))
    n_hi = -(-P_HI // UN)
    done = [0]
    def scatter_part(count):
        first, last = done[0], min(done[0] + count, n_hi)
        scatter_run(ihi, ghi, thi, first, last, first == 0)
        done[0] = last
    scatter_part(5)
    a_cross.wait()
    b_cross.start()
    a_near.wait()
    step_a(4)
    grad = acc[...] + whole(acore.at[1]) + whole(across)
    scaled, inverse = moments(hidden[...].astype(F32))
    wmine[0:1, :] = jnp.sum(grad * scaled, axis=0, keepdims=True)
    wmine[1:2, :] = jnp.sum(grad, axis=0, keepdims=True)
    hidden_grad[...] += norm_back(grad, scaled, inverse, row(gain1))
    scatter_part(6)
    step_a(5)
    scatter_part(4)
    step_d(2)
    scatter_part(2)
    b_near.wait()
    b_cross.wait()
    out = part[rows_at(t)].astype(F32) + bcore[1].astype(F32) + whole(bcross) + row(rbias)
    after = hidden[...].astype(F32) + row(scale1) * attn[...]
    result[...] = ((after + row(scale2) * out) * alive).astype(BF)
    up = cot[...].astype(F32) * alive
    wmine[6:7, :] = jnp.sum(up * out, axis=0, keepdims=True)
    wmine[7:8, :] = jnp.sum(up * row(scale2), axis=0, keepdims=True)
    step_b(3)
    def w_copy(k):
        return remote(wmine, wten.at[k], w_s.at[k], w_r.at[k], (d, lax.rem(t + k, 4)))
    def eighth(buf, who):
        count = buf.shape[0] // 8
        return buf.at[pl.ds(pl.multiple_of(who * count, 8), count)]
    def v_copy(j, k):
        buf, land = ((vec, vland), (tbl, tland))[j]
        to = lax.rem(d + k, 8)
        return remote(eighth(buf, to), land.at[k], v_s.at[j, k], v_r.at[j, k], (to, t))
    def u_copy(j, k):
        buf = (vout, tout)[j]
        return remote(eighth(buf, d), eighth(buf, d), v_s.at[2 + j, k], v_r.at[2 + j, k], (lax.rem(d + k, 8), t))
    def small_start(j):
        for k in range(1, 8):
            v_copy(j, k).start()
    def small_turn(j):
        buf, land = ((vec, vland), (tbl, tland))[j]
        total = eighth(buf, d)[...]
        for k in range(1, 8):
            v_copy(j, k).wait()
            total = total + land[k]
        eighth((vout, tout)[j], d)[...] = total
        for k in range(1, 8):
            u_copy(j, k).start()
    def small_end(j):
        for k in range(1, 8):
            u_copy(j, k).wait()
    if not sums:
        def small_turn(j):
            (vout, tout)[j][...] = (vec, tbl)[j][...]
        small_start = small_end = lambda j: None
    if sums:
        for k in range(1, 4):
            w_copy(k).start()
    step_b(4)
    scatter_part(4)
    step_b(5)
    total = wmine[...]
    if sums:
        for k in range(1, 4):
            w_copy(k).wait()
            total = total + wten[k]
    vec[...] = jnp.zeros_like(vec)
    lanes = model // 128
    for r in range(8):
        for j in range(lanes):
            vec[r * lanes + j:r * lanes + j + 1, :] = total[r:r + 1, j * 128:(j + 1) * 128]
    for r in range(2):
        for j in range(lanes):
            vec[(8 + r) * lanes + j:(8 + r) * lanes + j + 1, :] = smine[r:r + 1, j * 128:(j + 1) * 128]
    small_start(0)
    scatter_part(7)
    step_d(3)
    scatter_part(4)
    step_d(4)
    scatter_part(n_hi)
    step_d(5)
    small_turn(0)
    scatter_run(ilo, glo, tlo, 0, -(-P_LO // UN), True)
    per = (thi.shape[1] + tlo.shape[1]) // 4
    tbl[...] = jnp.zeros_like(tbl)
    def spread(src, base):
        count = src.shape[1] // 4
        for h in range(heads):
            flip[0:src.shape[1], :] = src[h * BB:(h + 1) * BB, :].T
            pieces = [flip[pl.ds(i, count, stride=4), :] for i in range(4)]
            start = h * per + base
            tbl[start:start + count, :] = jnp.concatenate(pieces, axis=1)
    spread(thi, 0)
    spread(tlo, thi.shape[1] // 4)
    if not sums:
        o0[...] = x0[...]
        o1[...] = x1[...]
        o2[...] = x2[...]
    small_start(1)
    small_end(0)
    for r in range(10):
        for j in range(lanes):
            small[r:r + 1, j * 128:(j + 1) * 128] = vout[r * lanes + j:r * lanes + j + 1, :]
    small_turn(1)
    small_end(1)
    for src, base, count in ((thigh, 0, thi.shape[1] // 4), (tlow, thi.shape[1] // 4, tlo.shape[1] // 4)):
        for h in range(heads):
            for r in range(count):
                at_row = h * per + base + r
                src[h:h + 1, r * 128:(r + 1) * 128] = tout[at_row:at_row + 1, :]
    if sums:
        for n in range(CHUNKS):
            e_copy(n).wait()

def layer(scale, sums, res, counts, hidden, gain1, shift1, wq, bq, wk, wv, bv, wo, bo, scale1, gain2, shift2, we, be, wr, rbias, scale2, cot, table_low, table_high, ilo, ihi, n_lo, n_hi):
    rows, model = hidden.shape
    total = rows * 4
    width = wq.shape[0]
    inner = we.shape[1]
    heads, e_lo = table_low.shape
    e_hi = table_high.shape[1]
    vm = pl.BlockSpec(memory_space=pltpu.VMEM)
    sm = pl.BlockSpec(memory_space=pltpu.SMEM)
    dma = pltpu.SemaphoreType.DMA
    V = pltpu.VMEM
    S = jax.ShapeDtypeStruct
    operands = (hidden, gain1, shift1, wq, bq, wk, wv, bv, wo, bo, scale1, gain2, shift2, we, be, wr, rbias, scale2, cot, table_low, table_high, ilo, ihi)
    half = rows // 2
    return pl.pallas_call(functools.partial(layer_kernel, scale, sums),
        out_shape=(S((inner, model), BF), S((model, inner), BF), S((4 * width, model), BF), S((rows, model), BF), S((rows, model), F32), S((16, model), F32), S((heads, n_lo * 32), F32), S((heads, n_hi * 32), F32)),
        in_specs=[sm, sm] + [vm] * len(operands), out_specs=(vm,) * 8,
        scratch_shapes=[V((heads, -(-e_lo // 256), 8, 128), jnp.int32), V((heads, -(-e_hi // 256), 8, 128), jnp.int32), V((heads, -(-e_hi // 256) * 256), F32), V((208, 256), jnp.int32), V((592, SEQ), jnp.int32), V((n_hi, BB), F32)]
            + [V((total, model), BF)] * 4 + [V((total, width), BF)] * 5 + [V((SLOTS, heads, SEQ, SEQ), BF)]
            + [V((total, inner), BF)] * 2 + [V((total, model), BF)] + [V((rows, model), F32)] * 2
            + [V((inner, model), BF), V((model, inner), BF), V((4 * width, model), BF), V((heads, 592, SEQ), F32), V((heads, 208, 256), F32), V((1, inner), F32)]
            + [V((2, 2, half, model), BF), V((2, 2, 2, half, model), BF)] + [V((2, 2, half, model), BF)] * 2
            + [V((2, 2, half, model), BF), V((2, half, model), BF), V((2, rows, model), BF), V((2, half, model), BF)]
            + [V((CHUNKS, 192, model), BF), V((CHUNKS, 3, 48, model), BF)]
            + [V((heads * BB, n_lo), F32), V((heads * BB, n_hi), F32)]
            + [V((8, model), F32)] * 2 + [V((4, 8, model), F32), V((64, 128), F32), V((8, 8, 128), F32), V((64, 128), F32), V((128, 128), F32), V((8, 16, 128), F32), V((128, 128), F32)]
            + [dma((6,))] * 12
            + [dma((CHUNKS,)), dma((CHUNKS,)), dma((CHUNKS, 4)), dma((CHUNKS, 4)), dma((CHUNKS, 4)), dma((CHUNKS, 4)), dma((CHUNKS,)), dma((CHUNKS,)),
               dma((6,)), dma((6,)), dma((4,)), dma((4,)), dma((4, 8)), dma((4, 8))],
        name="layer", cost_estimate=pl.CostEstimate(flops=100 * 10**9, bytes_accessed=60 * 10**6, transcendentals=0),
        compiler_params=pltpu.CompilerParams(collective_id=0, has_side_effects=True, vmem_limit_bytes=63 << 20))(res, counts, *operands)


def finish_kernel(pieces, i0, i1, i2, small, tlow, thigh, res_in, hid_in, *refs):
    r_out, e_out, q_out, k_out, v_out, o_out = refs[:6]
    vectors = refs[6:14]
    qb, vb, eb, tl, th, res_out, hid_out, low, wide, s_in, s_out, s_x = refs[14:]
    copies = [pltpu.make_async_copy(res_in, res_out, s_x.at[0]), pltpu.make_async_copy(hid_in, hid_out, s_x.at[1])]
    rows = low.shape[1]
    places = []
    for src, out in ((i0, r_out), (i1, e_out)):
        for n in range(pieces):
            here = pl.ds(n * rows, rows)
            places.append((src.at[here], out.at[here]))
    for n, out in enumerate((q_out, k_out, v_out, o_out)):
        places.append((i2.at[pl.ds(n * rows, rows)], out))
    loads = [pltpu.make_async_copy(src, low.at[n], s_in.at[n]) for n, (src, _) in enumerate(places)]
    stores = [pltpu.make_async_copy(wide.at[n], out, s_out.at[n]) for n, (_, out) in enumerate(places)]
    for copy in loads:
        copy.start()
    for copy in copies:
        copy.start()
    for n in range(len(places)):
        loads[n].wait()
        wide[n] = low[n].astype(F32)
        stores[n].start()
    for r, out in enumerate(vectors):
        out[...] = small[r:r + 1, :].reshape(out.shape)
    qb[...] = small[8:9, 0:qb.shape[0]].reshape(qb.shape)
    vb[...] = small[8:9, 256:256 + vb.shape[0]].reshape(vb.shape)
    eb[...] = small[9:10, :].reshape(eb.shape)
    tl[...] = tlow[:, 0:tl.shape[1]]
    th[...] = thigh[:, 0:th.shape[1]]
    for copy in stores + copies:
        copy.wait()

def finish(reduce_grad, expand_grad, attn_grads, small, low_grad, high_grad, result, hidden_grad, width, e_lo, e_hi):
    S = jax.ShapeDtypeStruct
    vm = pl.BlockSpec(memory_space=pltpu.VMEM)
    anywhere = pl.BlockSpec(memory_space=pl.ANY)
    model = reduce_grad.shape[1]
    pieces = reduce_grad.shape[0] // width
    count = 2 * pieces + 4
    shapes = (S(reduce_grad.shape, F32), S(expand_grad.shape, F32)) + (S((width, model), F32),) * 4 + (S((model,), F32),) * 8 + (
        S((width,), F32), S((width,), F32), S((model,), F32), S((low_grad.shape[0], e_lo), F32), S((high_grad.shape[0], e_hi), F32),
        S(result.shape, result.dtype), S(hidden_grad.shape, F32))
    dma = pltpu.SemaphoreType.DMA
    return pl.pallas_call(functools.partial(finish_kernel, pieces), out_shape=shapes,
        in_specs=[anywhere] * 3 + [vm] * 3 + [anywhere] * 2, out_specs=(anywhere,) * 6 + (vm,) * 13 + (anywhere,) * 2,
        scratch_shapes=[pltpu.VMEM((count, width, model), BF), pltpu.VMEM((count, width, model), F32), dma((count,)), dma((count,)), dma((2,))],
        name="finish", compiler_params=pltpu.CompilerParams(vmem_limit_bytes=63 << 20))(reduce_grad, expand_grad, attn_grads, small, low_grad, high_grad, result, hidden_grad)


def local(
    hidden,
    first_gain,
    first_shift,
    query_weight,
    query_bias,
    key_weight,
    value_weight,
    value_bias,
    output_weight,
    output_bias,
    first_scale,
    second_gain,
    second_shift,
    expand_weight,
    expand_bias,
    reduce_weight,
    reduce_bias,
    second_scale,
    table_low,
    table_high,
    resolution,
    counts,
    index_low,
    index_high,
    cotangent,
):
    floating = jnp.float32
    width = query_weight.shape[1]
    n_low = -(-table_low.shape[0] // (BB * 16)) * 16
    n_high = -(-table_high.shape[0] // (BB * 16)) * 16
    known = lax.axis_size("dp") == 8
    reduce_grad, expand_grad, attn_grads, result, hidden_grad, small, low_grad, high_grad = layer(
        HD ** (-0.5),
        known,
        resolution,
        counts,
        hidden,
        first_gain,
        first_shift,
        query_weight.T,
        query_bias,
        key_weight.T,
        value_weight.T,
        value_bias,
        output_weight,
        output_bias,
        first_scale,
        second_gain,
        second_shift,
        expand_weight,
        expand_bias,
        reduce_weight,
        reduce_bias,
        second_scale,
        cotangent,
        table_low.T,
        table_high.T,
        index_low,
        index_high,
        n_low,
        n_high,
    )
    if known:
        reduce_grad, expand_grad, *rest, low_grad, high_grad, result, hidden_grad = finish(
            reduce_grad,
            expand_grad,
            attn_grads,
            small,
            low_grad,
            high_grad,
            result,
            hidden_grad,
            width,
            table_low.shape[0],
            table_high.shape[0],
        )
        query_grad, key_grad, value_grad, output_grad, *norms, query_row, value_row, expand_row = rest
        return (
            result,
            hidden_grad,
            norms[0],
            norms[1],
            query_grad.T,
            query_row,
            key_grad.T,
            value_grad.T,
            value_row,
            output_grad,
            norms[3],
            norms[2],
            norms[4],
            norms[5],
            expand_grad,
            expand_row,
            reduce_grad,
            norms[7],
            norms[6],
            low_grad.T,
            high_grad.T,
        )
    if not known:
        reduce_grad, expand_grad, attn_grads, tail, low_grad, high_grad = lax.psum(
            (
                reduce_grad.astype(floating),
                expand_grad.astype(floating),
                attn_grads.astype(floating),
                small[8:],
                low_grad,
                high_grad,
            ),
            "dp",
        )
        small = jnp.concatenate((lax.psum(small[:8], ("dp", "tensor")), tail), axis=0)
    return (
        result,
        hidden_grad,
        small[0],
        small[1],
        attn_grads[:width].astype(floating).T,
        small[8, :width],
        attn_grads[width : 2 * width].astype(floating).T,
        attn_grads[2 * width : 3 * width].astype(floating).T,
        small[8, 256 : 256 + width],
        attn_grads[3 * width :].astype(floating),
        small[3],
        small[2],
        small[4],
        small[5],
        expand_grad.astype(floating),
        small[9],
        reduce_grad.astype(floating),
        small[7],
        small[6],
        low_grad[:, : table_low.shape[0]].T,
        high_grad[:, : table_high.shape[0]].T,
    )


def solution(mesh):
    in_specs = (
        P(("dp", "tensor"), None),
        P(),
        P(),
        P(None, "tensor"),
        P("tensor"),
        P(None, "tensor"),
        P(None, "tensor"),
        P("tensor"),
        P("tensor", None),
        P(),
        P(),
        P(),
        P(),
        P(None, "tensor"),
        P("tensor"),
        P("tensor", None),
        P(),
        P(),
        P(None, "tensor"),
        P(None, "tensor"),
        P("dp"),
        P("dp"),
        P(),
        P(),
        P(("dp", "tensor"), None),
    )
    out_specs = (
        P(("dp", "tensor"), None),
        P(("dp", "tensor"), None),
        P(),
        P(),
        P(None, "tensor"),
        P("tensor"),
        P(None, "tensor"),
        P(None, "tensor"),
        P("tensor"),
        P("tensor", None),
        P(),
        P(),
        P(),
        P(),
        P(None, "tensor"),
        P("tensor"),
        P("tensor", None),
        P(),
        P(),
        P(None, "tensor"),
        P(None, "tensor"),
    )
    return jax.shard_map(local, mesh=mesh, in_specs=in_specs, out_specs=out_specs, check_vma=False)
```

```python
import functools

import jax
import jax.numpy as jnp
from jax import lax
from jax.experimental import pallas as pl
from jax.experimental.pallas import tpu as pltpu
from jax.sharding import PartitionSpec as P

HD = 64
P_LO = 197
P_HI = 577
SEQ = 640
SLOTS = 2


eps_norm = 1e-06
masked_score = -1e30
inv_sqrt_two = 0.7071067811865476
inv_sqrt_two_pi = 0.3989422804014327


F32=jnp.float32; BF=jnp.bfloat16
NT=(((1,),(1,)),((),()))
def head_mask(h, width):
    lane = lax.broadcasted_iota(jnp.int32, (1, width), 1)
    return ((lane >= h*HD) & (lane < (h+1)*HD)).astype(F32).astype(BF)


BB=32; UN=16
def scatter_run(idx_ref, g_ref, out, first, last, fresh):
    heads = g_ref.shape[0]; na = out.shape[1]; m = idx_ref.shape[1]
    if fresh:
        out[...] = jnp.zeros_like(out)
    ib = lax.broadcasted_iota(jnp.int32, (16, m), 0).astype(F32)
    def body(r, c):
        ms = []; os = []
        for u in range(UN):
            row = r*UN+u
            idx = jnp.broadcast_to(idx_ref[pl.ds(row,1), :], (16, m))
            ia = (idx >> 5).astype(F32).astype(BF); il = (idx & 31).astype(F32).astype(BF)
            g = [jnp.broadcast_to(g_ref[h, pl.ds(row,1), :], (16, m)).astype(BF) for h in range(heads)]
            hits = [il == (ib + 16.0*k).astype(BF) for k in range(BB//16)]
            ms.append(jnp.concatenate([jnp.where(hits[k], g[h], jnp.zeros_like(g[h])) for h in range(heads) for k in range(BB//16)], axis=0))
            os.append(jnp.concatenate([jnp.where(ia == (ib + 16.0*k).astype(BF), jnp.ones_like(ia), jnp.zeros_like(ia)) for k in range(na//16)], axis=0))
        out[...] += lax.dot_general(jnp.concatenate(ms, axis=1), jnp.concatenate(os, axis=1), NT, preferred_element_type=F32)
        return c
    lax.fori_loop(first, last, body, 0)

PACK=8191.0
MESH = pl.DeviceIdType.MESH

CHUNKS = 6
TN = (((0,), (0,)), ((), ()))

def row(ref):
    return ref[...].reshape(1, ref.shape[0])

def live_of(t, rows, res, counts):
    slot = t * rows // SEQ
    first = t * rows - slot * SEQ
    limit = jnp.where(res[slot] == 1, P_HI, P_LO)
    limit = jnp.where(slot < counts[0], limit, 0)
    place = lax.broadcasted_iota(jnp.int32, (rows, 1), 0) + first
    return jnp.where(place < limit, 1.0, 0.0).astype(F32)

def moments(values):
    center = jnp.mean(values, axis=1, keepdims=True)
    centered = values - center
    inverse = lax.rsqrt(jnp.mean(centered * centered, axis=1, keepdims=True) + eps_norm)
    return centered * inverse, inverse

def norm_back(grad, scaled, inverse, gain):
    inner = grad * gain
    mean_inner = jnp.mean(inner, axis=1, keepdims=True)
    mean_mixed = jnp.mean(inner * scaled, axis=1, keepdims=True)
    return inverse * (inner - mean_inner - scaled * mean_mixed)

def look_up(tab, idx, heads):
    nch = tab.shape[1]
    lane = idx & 127
    ch = idx >> 7
    shift = jnp.where(ch >= nch, 0, 16)
    ch = jnp.where(ch >= nch, ch - nch, ch)
    acc = [None] * heads
    for k in range(nch):
        hit = ch == k
        for h in range(heads):
            v = jnp.take_along_axis(tab[h, k], lane, axis=1)
            acc[h] = v if k == 0 else jnp.where(hit, v, acc[h])
    return [((acc[h] << shift) >> 16).astype(F32) * (1.0 / PACK) for h in range(heads)]

def bias_rows(res, tab_lo, tab_hi, idx_lo, idx_hi, out, first, last, both):
    slots, heads = out.shape[:2]
    def masked(vals, j, limit):
        if (j + 1) * 128 <= limit:
            return vals
        place = lax.broadcasted_iota(jnp.int32, (8, 128), 1) + j * 128
        return [jnp.where(place < limit, v, masked_score) for v in vals]
    def body(r, c):
        for j in range(idx_hi.shape[1] // 128):
            cols = pl.ds(j * 128, 128)
            high = []
            low = []
            for part in range(2):
                rows = pl.ds(pl.multiple_of(r * 16 + part * 8, 8), 8)
                high.append(masked(look_up(tab_hi, idx_hi[rows, cols], heads), j, P_HI))
                if both and j < idx_lo.shape[1] // 128:
                    low.append(masked(look_up(tab_lo, idx_lo[rows, cols], heads), j, P_LO))
                else:
                    low.append([jnp.full((8, 128), masked_score, F32)] * heads)
            for h in range(heads):
                hi = jnp.concatenate([high[0][h], high[1][h]], axis=0).astype(BF)
                lo = jnp.concatenate([low[0][h], low[1][h]], axis=0).astype(BF)
                for s in range(slots):
                    out[s, h, pl.ds(pl.multiple_of(r * 16, 16), 16), cols] = jnp.where(res[s] == 1, hi, lo)
        return c
    lax.fori_loop(first, last, body, 0)

def layer_kernel(scale, sums, res, counts, hidden, gain1, shift1, wq, bq, wk, wv, bv, wo, bo, scale1, gain2, shift2, we, be, wr, rbias, scale2, cot,
                 table_lo, table_hi, ilo_in, ihi_in,
                 o0, o1, o2, result, hidden_grad, small, tlow, thigh,
                 tab_lo, tab_hi, raw, ilo, ihi, flip,
                 g1, gm, gt, ga, q_buf, k_buf, v_buf, mix, dmix, pb, act, pgl, part, acc, attn, x0, x1, x2, ghi, glo, esum,
                 cbuf, ccore, xbuf, xin, acore, across, bcore, bcross, ybuf, zbuf,
                 tlo, thi, wmine, smine, wten, vec, vland, vout, tbl, tland, tout,
                 h_s, h_r, m_s, m_r, t_s, t_r, a_s, a_r, o_s, o_r, n_s, n_r,
                 y_s, y_r, z_s, z_r, g_s, g_r, e_s, e_r, r_s, r_r, w_s, w_r, v_s, v_r):
    d = lax.axis_index("dp")
    t = lax.axis_index("tensor")
    col = d // 2
    side = lax.rem(d, 2)
    neighbour = d + 1 - 2 * side
    sibling = t + 1 - 2 * lax.rem(t, 2)
    cross = lax.rem(t + 2, 4)
    diag = 3 - t
    rows = hidden.shape[0]
    half = rows // 2
    slots, heads = pb.shape[:2]
    width = q_buf.shape[1]
    model = g1.shape[1]
    barrier = pltpu.get_barrier_semaphore()
    for k in range(1, 4):
        pl.semaphore_signal(barrier, inc=1, device_id=(d, lax.rem(t + k, 4)), device_id_type=MESH)
    if sums:
        for k in range(1, 8):
            pl.semaphore_signal(barrier, inc=1, device_id=(lax.rem(d + k, 8), t), device_id_type=MESH)

    def remote(src, dst, send, recv, device):
        return pltpu.make_async_remote_copy(src_ref=src, dst_ref=dst, send_sem=send, recv_sem=recv, device_id=device, device_id_type=MESH)
    def rows_at(who):
        return pl.ds(pl.multiple_of(who * rows, 16), rows)
    def span(who, h):
        return pl.ds(pl.multiple_of(who * rows + h * half, 16), half)
    def gather_x(buf, send, recv, h):
        here = buf.at[span(t, h)]
        return remote(here, here, send.at[h], recv.at[h], (d, cross))
    def gather_near(buf, send, recv, h):
        here = buf.at[span(t, h)]
        return remote(here, here, send.at[2 + h], recv.at[2 + h], (d, sibling))
    def gather_on(buf, send, recv, h):
        here = buf.at[span(cross, h)]
        return remote(here, here, send.at[4 + h], recv.at[4 + h], (d, sibling))
    def sum_far(j, send, recv, h):
        return remote(cbuf.at[0, h], ccore.at[j, 0, h], send.at[h], recv.at[h], (d, sibling))
    def sum_near(j, send, recv, h):
        return remote(cbuf.at[1, h], ccore.at[j, 1, h], send.at[2 + h], recv.at[2 + h], (d, sibling))
    def sum_x(j, send, recv, h):
        return remote(xbuf.at[j, h], xin.at[j, h], send.at[4 + h], recv.at[4 + h], (d, cross))
    arrays = (x0, x1, x2)
    outs = (o0, o1, o2)
    size = x0.shape[0] // 2
    part_y = size // 2
    part_z = part_y // 4
    def at(n, start, count):
        return pl.ds(pl.multiple_of((n % 2) * size + start, 16), count)
    def y_copy(n):
        return remote(arrays[n // 2].at[at(n, (1 - side) * part_y, part_y)], ybuf.at[n], y_s.at[n], y_r.at[n], (neighbour, t))
    def z_copy(n, k):
        to = lax.rem(col + k, 4)
        return remote(arrays[n // 2].at[at(n, side * part_y + to * part_z, part_z)], zbuf.at[n, k - 1], z_s.at[n, k], z_r.at[n, k], (to * 2 + side, t))
    def g_copy(n, k):
        to = lax.rem(col + k, 4)
        here = outs[n // 2].at[at(n, side * part_y + col * part_z, part_z)]
        return remote(here, here, g_s.at[n, k], g_r.at[n, k], (to * 2 + side, t))
    def e_copy(n):
        here = outs[n // 2].at[at(n, side * part_y, part_y)]
        return remote(here, here, e_s.at[n], e_r.at[n], (neighbour, t))
    def start_y(n):
        y_copy(n).start()
    def step_a(n):
        y_copy(n).wait()
        here = at(n, side * part_y, part_y)
        arrays[n // 2][here] = (arrays[n // 2][here].astype(F32) + ybuf[n].astype(F32)).astype(BF)
        for k in range(1, 4):
            z_copy(n, k).start()
    def step_b(n):
        for k in range(1, 4):
            z_copy(n, k).wait()
        here = at(n, side * part_y + col * part_z, part_z)
        total = arrays[n // 2][here].astype(F32)
        for k in range(3):
            total = total + zbuf[n, k].astype(F32)
        outs[n // 2][here] = total.astype(BF)
        for k in range(1, 4):
            g_copy(n, k).start()
    def step_d(n):
        for k in range(1, 4):
            g_copy(n, k).wait()
        e_copy(n).start()
    if not sums:
        start_y = step_a = step_b = step_d = lambda n: None

    scaled, inverse = moments(hidden[...].astype(F32))
    g1[rows_at(t)] = (scaled * row(gain1) + row(shift1)).astype(BF)
    pl.semaphore_wait(barrier, 10 if sums else 3)
    for h in range(2):
        gather_x(g1, h_s, h_r, h).start()
        gather_near(g1, h_s, h_r, h).start()
    alive = live_of(t, rows, res, counts)
    gm[rows_at(t)] = (cot[...].astype(F32) * alive * row(scale2)).astype(BF)
    ilo[...] = jnp.zeros_like(ilo)
    ilo[0:P_LO, 0:P_LO] = ilo_in[...]
    ihi[...] = jnp.zeros_like(ihi)
    ihi[0:P_HI, 0:P_HI] = ihi_in[...]
    for table, packed in ((table_lo, tab_lo), (table_hi, tab_hi)):
        nch = packed.shape[1]
        raw[...] = jnp.zeros_like(raw)
        raw[:, 0:table.shape[1]] = table[...]
        for k in range(nch):
            low = (raw[:, k * 128:(k + 1) * 128] * PACK + 32768.5).astype(jnp.int32) - 32768
            high = (raw[:, (k + nch) * 128:(k + nch + 1) * 128] * PACK + 32768.5).astype(jnp.int32) - 32768
            word = (high << 16) | (low & 65535)
            for h in range(heads):
                packed[h, k] = jnp.broadcast_to(word[h:h + 1, :], (8, 128))
    look = functools.partial(bias_rows, res, tab_lo, tab_hi, ilo, ihi, pb)
    n_low = -(-P_LO // 16)
    n_high = -(-P_HI // 16)
    middle = (n_low + n_high) // 2
    look(0, n_low, True)
    look(n_low, middle, False)
    for h in range(2):
        gather_x(g1, h_s, h_r, h).wait()
        gather_on(g1, h_s, h_r, h).start()
        gather_x(gm, m_s, m_r, h).start()
        gather_near(gm, m_s, m_r, h).start()
    look(middle, n_high, False)
    pb[:, :, n_high * 16:, :] = jnp.zeros((slots, heads, SEQ - n_high * 16, SEQ), BF)
    for h in range(2):
        gather_near(g1, h_s, h_r, h).wait()
        gather_on(g1, h_s, h_r, h).wait()

    def project(i, c):
        here = rows_at(i)
        g = g1[here]
        q_buf[here] = ((lax.dot_general(g, wq[...], NT, preferred_element_type=F32) + row(bq)) * scale).astype(BF)
        k_buf[here] = lax.dot_general(g, wk[...], NT, preferred_element_type=F32).astype(BF)
        v_buf[here] = (lax.dot_general(g, wv[...], NT, preferred_element_type=F32) + row(bv)).astype(BF)
        return c
    lax.fori_loop(0, 4, project, 0)

    def attend_image(slot):
        here = pl.ds(pl.multiple_of(slot * SEQ, 16), SEQ)
        k = k_buf[here]
        v = v_buf[here]
        vm = [v * head_mask(h, width) for h in range(heads)]
        def piece(i, c):
            first = pl.multiple_of(i * rows, 16)
            there = pl.ds(pl.multiple_of(slot * SEQ + first, 16), rows)
            q = q_buf[there]
            out = jnp.zeros((rows, width), F32)
            for h in range(heads):
                s = lax.dot_general(q * head_mask(h, width), k, NT, preferred_element_type=F32)
                s = s + pb[slot, h, pl.ds(first, rows)].astype(F32)
                peak = jnp.max(s, axis=1, keepdims=True)
                e = jnp.exp(s - peak)
                total = jnp.sum(e, axis=1, keepdims=True)
                p = (e * (1.0 / total)).astype(BF)
                pb[slot, h, pl.ds(first, rows)] = p
                out = out + jnp.dot(p, vm[h], preferred_element_type=F32)
            mix[there] = out.astype(BF)
            return c
        lax.fori_loop(0, SEQ // rows, piece, 0)
    def output_of(who, h):
        return jnp.dot(mix[span(who, h)], wo[...], preferred_element_type=F32)

    mine = t * rows // SEQ
    attend_image(1 - mine)
    for h in range(2):
        cbuf[0, h] = output_of(diag, h).astype(BF)
        sum_far(0, o_s, o_r, h).start()
    for h in range(2):
        total = output_of(cross, h)
        sum_far(0, o_s, o_r, h).wait()
        xbuf[0, h] = (total + ccore[0, 0, h].astype(F32)).astype(BF)
        sum_x(0, o_s, o_r, h).start()
    attend_image(mine)
    for h in range(2):
        cbuf[1, h] = output_of(sibling, h).astype(BF)
        sum_near(0, o_s, o_r, h).start()
    for h in range(2):
        acc[pl.ds(h * half, half)] = output_of(t, h)
    for h in range(2):
        gather_x(gm, m_s, m_r, h).wait()
        gather_on(gm, m_s, m_r, h).start()
    for h in range(2):
        here = pl.ds(h * half, half)
        sum_near(0, o_s, o_r, h).wait()
        sum_x(0, o_s, o_r, h).wait()
        out = acc[here] + ccore[0, 1, h].astype(F32) + xin[0, h].astype(F32) + row(bo)
        attn[here] = out
        scaled, inverse = moments(hidden[here].astype(F32) + row(scale1) * out)
        gt[span(t, h)] = (scaled * row(gain2) + row(shift2)).astype(BF)
        gather_x(gt, t_s, t_r, h).start()
        gather_near(gt, t_s, t_r, h).start()

    esum[...] = jnp.zeros_like(esum)
    def feed(who, h):
        here = span(who, h)
        pre = jnp.dot(gt[here], we[...], preferred_element_type=F32) + row(be)
        grad = lax.dot_general(gm[here], wr[...], NT, preferred_element_type=F32)
        phi = 0.5 * (1.0 + lax.erf(pre * inv_sqrt_two))
        active = (pre * phi).astype(BF)
        act[here] = active
        grad = grad * (phi + pre * inv_sqrt_two_pi * jnp.exp(-0.5 * pre * pre))
        esum[...] += jnp.sum(grad, axis=0, keepdims=True)
        grad = grad.astype(BF)
        pgl[here] = grad
        part[here] = jnp.dot(active, wr[...], preferred_element_type=F32).astype(BF)
        return lax.dot_general(grad, we[...], NT, preferred_element_type=F32)
    def feed_own(h, c):
        acc[pl.ds(pl.multiple_of(h * half, 16), half)] = feed(t, h)
        return c
    lax.fori_loop(0, 2, feed_own, 0)
    for h in range(2):
        gather_near(gm, m_s, m_r, h).wait()
        gather_near(gt, t_s, t_r, h).wait()
        gather_on(gm, m_s, m_r, h).wait()
    def feed_near(h, c):
        cbuf[1, h] = feed(sibling, h).astype(BF)
        sum_near(1, n_s, n_r, h).start()
        return c
    lax.fori_loop(0, 2, feed_near, 0)
    def feed_far(h, c):
        gather_x(gt, t_s, t_r, h).wait()
        gather_on(gt, t_s, t_r, h).start()
        total = feed(cross, h)
        gather_on(gt, t_s, t_r, h).wait()
        cbuf[0, h] = feed(diag, h).astype(BF)
        sum_far(1, n_s, n_r, h).start()
        sum_far(1, n_s, n_r, h).wait()
        xbuf[1, h] = (total + ccore[1, 0, h].astype(F32)).astype(BF)
        sum_x(1, n_s, n_r, h).start()
        return c
    lax.fori_loop(0, 2, feed_far, 0)

    tile = 128
    def reduce_grad(i, c):
        cols = pl.ds(pl.multiple_of(i * tile, tile), tile)
        x0[cols] = lax.dot_general(act[:, cols], gm[...], TN, preferred_element_type=F32).astype(BF)
        return c
    count = act.shape[1] // tile
    lax.fori_loop(0, count // 2, reduce_grad, 0)
    start_y(0)
    lax.fori_loop(count // 2, count, reduce_grad, 0)
    wmine[...] = jnp.zeros_like(wmine)
    def second_back(h):
        here = pl.ds(h * half, half)
        sum_near(1, n_s, n_r, h).wait()
        sum_x(1, n_s, n_r, h).wait()
        grad = acc[here] + ccore[1, 1, h].astype(F32) + xin[1, h].astype(F32)
        out = attn[here]
        scaled, inverse = moments(hidden[here].astype(F32) + row(scale1) * out)
        after = cot[here].astype(F32) * alive[h * half:(h + 1) * half] + norm_back(grad, scaled, inverse, row(gain2))
        hidden_grad[here] = after
        agrad = after * row(scale1)
        ga[span(t, h)] = agrad.astype(BF)
        gather_x(ga, a_s, a_r, h).start()
        gather_near(ga, a_s, a_r, h).start()
        wmine[2:3, :] += jnp.sum(after * out, axis=0, keepdims=True)
        wmine[3:4, :] += jnp.sum(agrad, axis=0, keepdims=True)
        wmine[4:5, :] += jnp.sum(grad * scaled, axis=0, keepdims=True)
        wmine[5:6, :] += jnp.sum(grad, axis=0, keepdims=True)
    start_y(1)
    second_back(0)
    def expand_grad(i, c):
        cols = pl.ds(pl.multiple_of(i * tile, tile), tile)
        x1[cols] = lax.dot_general(gt[:, cols], pgl[...], TN, preferred_element_type=F32).astype(BF)
        return c
    lax.fori_loop(0, gt.shape[1] // tile, expand_grad, 0)
    step_a(0)
    start_y(2)
    second_back(1)
    step_a(1)
    def mixture_of(who):
        here = rows_at(who)
        dmix[here] = lax.dot_general(ga[here], wo[...], NT, preferred_element_type=F32).astype(BF)
    mixture_of(t)
    gather_x(ga, a_s, a_r, 0).wait()
    gather_on(ga, a_s, a_r, 0).start()
    start_y(3)
    for h in range(2):
        gather_near(ga, a_s, a_r, h).wait()
    mixture_of(sibling)
    step_b(0)
    gather_x(ga, a_s, a_r, 1).wait()
    gather_on(ga, a_s, a_r, 1).start()
    mixture_of(cross)
    step_b(1)
    for h in range(2):
        gather_on(ga, a_s, a_r, h).wait()
    mixture_of(diag)

    smine[...] = jnp.zeros_like(smine)
    smine[1:2, :] = esum[...]
    def attention_back(slot):
        here = slice(slot * SEQ, (slot + 1) * SEQ)
        q = q_buf[here]
        k = k_buf[here]
        v = v_buf[here]
        dd = dmix[here]
        qt = q.T
        dt = dd.T
        is_high = jnp.where(res[slot] == 1, 1.0, 0.0).astype(F32)
        out = jnp.zeros((SEQ, width), F32)
        dks = []
        dvs = []
        nh = ghi.shape[1]
        nl, ml = glo.shape[1:]
        for h in range(heads):
            mask = head_mask(h, width)
            p = pb[slot, h]
            dp = lax.dot_general(dd * mask, v, NT, preferred_element_type=F32)
            pf = p.astype(F32)
            m = pf * dp
            ds = m - pf * jnp.sum(m, axis=1, keepdims=True)
            if slot == 0:
                ghi[h] = ds[:nh] * is_high
                glo[h] = ds[:nl, :ml] * (1.0 - is_high)
            else:
                ghi[h] += ds[:nh] * is_high
                glo[h] += ds[:nl, :ml] * (1.0 - is_high)
            low = ds.astype(BF)
            out = out + jnp.dot(low, k * mask, preferred_element_type=F32)
            dks.append(jnp.dot(qt[h*HD:(h+1)*HD], low, preferred_element_type=F32))
            dvs.append(jnp.dot(dt[h*HD:(h+1)*HD], p, preferred_element_type=F32))
        out = out * scale
        smine[0:1, 0:width] += jnp.sum(out, axis=0, keepdims=True)
        q_buf[here] = out.astype(BF)
        k_buf[here] = jnp.concatenate(dks, axis=0).T.astype(BF)
        out = jnp.concatenate(dvs, axis=0).T
        smine[0:1, 256:256 + width] += jnp.sum(out, axis=0, keepdims=True)
        v_buf[here] = out.astype(BF)
    attention_back(0)
    step_a(2)
    step_d(0)
    attention_back(1)

    def back(who):
        here = rows_at(who)
        total = jnp.dot(q_buf[here], wq[...], preferred_element_type=F32)
        total = total + jnp.dot(k_buf[here], wk[...], preferred_element_type=F32)
        return total + jnp.dot(v_buf[here], wv[...], preferred_element_type=F32)
    def send(buf, value):
        for h in range(2):
            buf[h] = value[h * half:(h + 1) * half].astype(BF)
    def whole(ref):
        return jnp.concatenate([ref[0], ref[1]], axis=0).astype(F32)
    a_far = remote(cbuf.at[0], acore.at[0], r_s.at[0], r_r.at[0], (d, sibling))
    a_near = remote(cbuf.at[1], acore.at[1], r_s.at[1], r_r.at[1], (d, sibling))
    a_cross = remote(xbuf.at[0], across, r_s.at[2], r_r.at[2], (d, cross))
    b_far = remote(part.at[rows_at(diag)], bcore.at[0], r_s.at[3], r_r.at[3], (d, sibling))
    b_near = remote(part.at[rows_at(sibling)], bcore.at[1], r_s.at[4], r_r.at[4], (d, sibling))
    b_cross = remote(xbuf.at[1], bcross, r_s.at[5], r_r.at[5], (d, cross))
    send(cbuf.at[0], back(diag))
    a_far.start()
    b_far.start()
    step_d(1)
    total = back(cross)
    step_a(3)
    a_far.wait()
    send(xbuf.at[0], total + whole(acore.at[0]))
    a_cross.start()
    for j, (left, right) in enumerate(((q_buf, g1), (k_buf, g1), (v_buf, g1), (mix, ga))):
        x2[j * width:(j + 1) * width, :] = lax.dot_general(left[...], right[...], TN, preferred_element_type=F32).astype(BF)
        if j == 1:
            start_y(4)
    start_y(5)
    send(cbuf.at[1], back(sibling))
    a_near.start()
    b_near.start()
    acc[...] = back(t)
    step_b(2)
    b_far.wait()
    send(xbuf.at[1], part[rows_at(cross)].astype(F32) + bcore[0].astype(F32))
    n_hi = -(-P_HI // UN)
    done = [0]
    def scatter_part(count):
        first, last = done[0], min(done[0] + count, n_hi)
        scatter_run(ihi, ghi, thi, first, last, first == 0)
        done[0] = last
    scatter_part(5)
    a_cross.wait()
    b_cross.start()
    a_near.wait()
    step_a(4)
    grad = acc[...] + whole(acore.at[1]) + whole(across)
    scaled, inverse = moments(hidden[...].astype(F32))
    wmine[0:1, :] = jnp.sum(grad * scaled, axis=0, keepdims=True)
    wmine[1:2, :] = jnp.sum(grad, axis=0, keepdims=True)
    hidden_grad[...] += norm_back(grad, scaled, inverse, row(gain1))
    scatter_part(6)
    step_a(5)
    scatter_part(4)
    step_d(2)
    scatter_part(2)
    b_near.wait()
    b_cross.wait()
    out = part[rows_at(t)].astype(F32) + bcore[1].astype(F32) + whole(bcross) + row(rbias)
    after = hidden[...].astype(F32) + row(scale1) * attn[...]
    result[...] = ((after + row(scale2) * out) * alive).astype(BF)
    up = cot[...].astype(F32) * alive
    wmine[6:7, :] = jnp.sum(up * out, axis=0, keepdims=True)
    wmine[7:8, :] = jnp.sum(up * row(scale2), axis=0, keepdims=True)
    step_b(3)
    def w_copy(k):
        return remote(wmine, wten.at[k], w_s.at[k], w_r.at[k], (d, lax.rem(t + k, 4)))
    def eighth(buf, who):
        count = buf.shape[0] // 8
        return buf.at[pl.ds(pl.multiple_of(who * count, 8), count)]
    def v_copy(j, k):
        buf, land = ((vec, vland), (tbl, tland))[j]
        to = lax.rem(d + k, 8)
        return remote(eighth(buf, to), land.at[k], v_s.at[j, k], v_r.at[j, k], (to, t))
    def u_copy(j, k):
        buf = (vout, tout)[j]
        return remote(eighth(buf, d), eighth(buf, d), v_s.at[2 + j, k], v_r.at[2 + j, k], (lax.rem(d + k, 8), t))
    def small_start(j):
        for k in range(1, 8):
            v_copy(j, k).start()
    def small_turn(j):
        buf, land = ((vec, vland), (tbl, tland))[j]
        total = eighth(buf, d)[...]
        for k in range(1, 8):
            v_copy(j, k).wait()
            total = total + land[k]
        eighth((vout, tout)[j], d)[...] = total
        for k in range(1, 8):
            u_copy(j, k).start()
    def small_end(j):
        for k in range(1, 8):
            u_copy(j, k).wait()
    if not sums:
        def small_turn(j):
            (vout, tout)[j][...] = (vec, tbl)[j][...]
        small_start = small_end = lambda j: None
    if sums:
        for k in range(1, 4):
            w_copy(k).start()
    step_b(4)
    scatter_part(4)
    step_b(5)
    total = wmine[...]
    if sums:
        for k in range(1, 4):
            w_copy(k).wait()
            total = total + wten[k]
    vec[...] = jnp.zeros_like(vec)
    lanes = model // 128
    for r in range(8):
        for j in range(lanes):
            vec[r * lanes + j:r * lanes + j + 1, :] = total[r:r + 1, j * 128:(j + 1) * 128]
    for r in range(2):
        for j in range(lanes):
            vec[(8 + r) * lanes + j:(8 + r) * lanes + j + 1, :] = smine[r:r + 1, j * 128:(j + 1) * 128]
    small_start(0)
    scatter_part(7)
    step_d(3)
    scatter_part(4)
    scatter_run(ilo, glo, tlo, 0, -(-P_LO // UN), True)
    step_d(4)
    scatter_part(n_hi)
    small_turn(0)
    per = (thi.shape[1] + tlo.shape[1]) // 4
    tbl[...] = jnp.zeros_like(tbl)
    def spread(src, base):
        count = src.shape[1] // 4
        for h in range(heads):
            flip[0:src.shape[1], :] = src[h * BB:(h + 1) * BB, :].T
            pieces = [flip[pl.ds(i, count, stride=4), :] for i in range(4)]
            start = h * per + base
            tbl[start:start + count, :] = jnp.concatenate(pieces, axis=1)
    spread(thi, 0)
    spread(tlo, thi.shape[1] // 4)
    if not sums:
        o0[...] = x0[...]
        o1[...] = x1[...]
        o2[...] = x2[...]
    small_start(1)
    step_d(5)
    small_end(0)
    for r in range(10):
        for j in range(lanes):
            small[r:r + 1, j * 128:(j + 1) * 128] = vout[r * lanes + j:r * lanes + j + 1, :]
    small_turn(1)
    small_end(1)
    for src, base, count in ((thigh, 0, thi.shape[1] // 4), (tlow, thi.shape[1] // 4, tlo.shape[1] // 4)):
        for h in range(heads):
            for r in range(count):
                at_row = h * per + base + r
                src[h:h + 1, r * 128:(r + 1) * 128] = tout[at_row:at_row + 1, :]
    if sums:
        for n in range(CHUNKS):
            e_copy(n).wait()

def layer(scale, sums, res, counts, hidden, gain1, shift1, wq, bq, wk, wv, bv, wo, bo, scale1, gain2, shift2, we, be, wr, rbias, scale2, cot, table_low, table_high, ilo, ihi, n_lo, n_hi):
    rows, model = hidden.shape
    total = rows * 4
    width = wq.shape[0]
    inner = we.shape[1]
    heads, e_lo = table_low.shape
    e_hi = table_high.shape[1]
    vm = pl.BlockSpec(memory_space=pltpu.VMEM)
    sm = pl.BlockSpec(memory_space=pltpu.SMEM)
    dma = pltpu.SemaphoreType.DMA
    V = pltpu.VMEM
    S = jax.ShapeDtypeStruct
    operands = (hidden, gain1, shift1, wq, bq, wk, wv, bv, wo, bo, scale1, gain2, shift2, we, be, wr, rbias, scale2, cot, table_low, table_high, ilo, ihi)
    half = rows // 2
    return pl.pallas_call(functools.partial(layer_kernel, scale, sums),
        out_shape=(S((inner, model), BF), S((model, inner), BF), S((4 * width, model), BF), S((rows, model), BF), S((rows, model), F32), S((16, model), F32), S((heads, n_lo * 32), F32), S((heads, n_hi * 32), F32)),
        in_specs=[sm, sm] + [vm] * len(operands), out_specs=(vm,) * 8,
        scratch_shapes=[V((heads, -(-e_lo // 256), 8, 128), jnp.int32), V((heads, -(-e_hi // 256), 8, 128), jnp.int32), V((heads, -(-e_hi // 256) * 256), F32), V((208, 256), jnp.int32), V((592, SEQ), jnp.int32), V((n_hi, BB), F32)]
            + [V((total, model), BF)] * 4 + [V((total, width), BF)] * 5 + [V((SLOTS, heads, SEQ, SEQ), BF)]
            + [V((total, inner), BF)] * 2 + [V((total, model), BF)] + [V((rows, model), F32)] * 2
            + [V((inner, model), BF), V((model, inner), BF), V((4 * width, model), BF), V((heads, 592, SEQ), F32), V((heads, 208, 256), F32), V((1, inner), F32)]
            + [V((2, 2, half, model), BF), V((2, 2, 2, half, model), BF)] + [V((2, 2, half, model), BF)] * 2
            + [V((2, 2, half, model), BF), V((2, half, model), BF), V((2, rows, model), BF), V((2, half, model), BF)]
            + [V((CHUNKS, 192, model), BF), V((CHUNKS, 3, 48, model), BF)]
            + [V((heads * BB, n_lo), F32), V((heads * BB, n_hi), F32)]
            + [V((8, model), F32)] * 2 + [V((4, 8, model), F32), V((64, 128), F32), V((8, 8, 128), F32), V((64, 128), F32), V((128, 128), F32), V((8, 16, 128), F32), V((128, 128), F32)]
            + [dma((6,))] * 12
            + [dma((CHUNKS,)), dma((CHUNKS,)), dma((CHUNKS, 4)), dma((CHUNKS, 4)), dma((CHUNKS, 4)), dma((CHUNKS, 4)), dma((CHUNKS,)), dma((CHUNKS,)),
               dma((6,)), dma((6,)), dma((4,)), dma((4,)), dma((4, 8)), dma((4, 8))],
        name="layer", cost_estimate=pl.CostEstimate(flops=100 * 10**9, bytes_accessed=60 * 10**6, transcendentals=0),
        compiler_params=pltpu.CompilerParams(collective_id=0, has_side_effects=True, vmem_limit_bytes=63 << 20))(res, counts, *operands)


def finish_kernel(pieces, i0, i1, i2, small, tlow, thigh, res_in, hid_in, *refs):
    r_out, e_out, q_out, k_out, v_out, o_out = refs[:6]
    vectors = refs[6:14]
    qb, vb, eb, tl, th, res_out, hid_out, low, wide, res, hid, s_in, s_out, s_x = refs[14:]
    first = [pltpu.make_async_copy(hid_in, hid, s_x.at[0]), pltpu.make_async_copy(res_in, res, s_x.at[1])]
    second = [pltpu.make_async_copy(hid, hid_out, s_x.at[2]), pltpu.make_async_copy(res, res_out, s_x.at[3])]
    rows = low.shape[1]
    places = []
    for src, out in ((i0, r_out), (i1, e_out)):
        for n in range(pieces):
            here = pl.ds(n * rows, rows)
            places.append((src.at[here], out.at[here]))
    for n, out in enumerate((q_out, k_out, v_out, o_out)):
        places.append((i2.at[pl.ds(n * rows, rows)], out))
    loads = [pltpu.make_async_copy(src, low.at[n], s_in.at[n]) for n, (src, _) in enumerate(places)]
    stores = [pltpu.make_async_copy(wide.at[n], out, s_out.at[n]) for n, (_, out) in enumerate(places)]
    for copy in first + loads:
        copy.start()
    for before, after in zip(first, second):
        before.wait()
        after.start()
    for n in range(len(places)):
        loads[n].wait()
        wide[n] = low[n].astype(F32)
        stores[n].start()
    for r, out in enumerate(vectors):
        out[...] = small[r:r + 1, :].reshape(out.shape)
    qb[...] = small[8:9, 0:qb.shape[0]].reshape(qb.shape)
    vb[...] = small[8:9, 256:256 + vb.shape[0]].reshape(vb.shape)
    eb[...] = small[9:10, :].reshape(eb.shape)
    tl[...] = tlow[:, 0:tl.shape[1]]
    th[...] = thigh[:, 0:th.shape[1]]
    for copy in stores + second:
        copy.wait()

def finish(reduce_grad, expand_grad, attn_grads, small, low_grad, high_grad, result, hidden_grad, width, e_lo, e_hi):
    S = jax.ShapeDtypeStruct
    vm = pl.BlockSpec(memory_space=pltpu.VMEM)
    anywhere = pl.BlockSpec(memory_space=pl.ANY)
    model = reduce_grad.shape[1]
    pieces = reduce_grad.shape[0] // width
    count = 2 * pieces + 4
    shapes = (S(reduce_grad.shape, F32), S(expand_grad.shape, F32)) + (S((width, model), F32),) * 4 + (S((model,), F32),) * 8 + (
        S((width,), F32), S((width,), F32), S((model,), F32), S((low_grad.shape[0], e_lo), F32), S((high_grad.shape[0], e_hi), F32),
        S(result.shape, result.dtype), S(hidden_grad.shape, F32))
    dma = pltpu.SemaphoreType.DMA
    return pl.pallas_call(functools.partial(finish_kernel, pieces), out_shape=shapes,
        in_specs=[anywhere] * 3 + [vm] * 3 + [anywhere] * 2, out_specs=(anywhere,) * 6 + (vm,) * 13 + (anywhere,) * 2,
        scratch_shapes=[pltpu.VMEM((count, width, model), BF), pltpu.VMEM((count, width, model), F32), pltpu.VMEM(result.shape, result.dtype), pltpu.VMEM(hidden_grad.shape, F32), dma((count,)), dma((count,)), dma((4,))],
        name="finish", compiler_params=pltpu.CompilerParams(vmem_limit_bytes=63 << 20))(reduce_grad, expand_grad, attn_grads, small, low_grad, high_grad, result, hidden_grad)


def local(
    hidden,
    first_gain,
    first_shift,
    query_weight,
    query_bias,
    key_weight,
    value_weight,
    value_bias,
    output_weight,
    output_bias,
    first_scale,
    second_gain,
    second_shift,
    expand_weight,
    expand_bias,
    reduce_weight,
    reduce_bias,
    second_scale,
    table_low,
    table_high,
    resolution,
    counts,
    index_low,
    index_high,
    cotangent,
):
    floating = jnp.float32
    width = query_weight.shape[1]
    n_low = -(-table_low.shape[0] // (BB * 16)) * 16
    n_high = -(-table_high.shape[0] // (BB * 16)) * 16
    known = lax.axis_size("dp") == 8
    reduce_grad, expand_grad, attn_grads, result, hidden_grad, small, low_grad, high_grad = layer(
        HD ** (-0.5),
        known,
        resolution,
        counts,
        hidden,
        first_gain,
        first_shift,
        query_weight.T,
        query_bias,
        key_weight.T,
        value_weight.T,
        value_bias,
        output_weight,
        output_bias,
        first_scale,
        second_gain,
        second_shift,
        expand_weight,
        expand_bias,
        reduce_weight,
        reduce_bias,
        second_scale,
        cotangent,
        table_low.T,
        table_high.T,
        index_low,
        index_high,
        n_low,
        n_high,
    )
    if known:
        reduce_grad, expand_grad, *rest, low_grad, high_grad, result, hidden_grad = finish(
            reduce_grad,
            expand_grad,
            attn_grads,
            small,
            low_grad,
            high_grad,
            result,
            hidden_grad,
            width,
            table_low.shape[0],
            table_high.shape[0],
        )
        query_grad, key_grad, value_grad, output_grad, *norms, query_row, value_row, expand_row = rest
        return (
            result,
            hidden_grad,
            norms[0],
            norms[1],
            query_grad.T,
            query_row,
            key_grad.T,
            value_grad.T,
            value_row,
            output_grad,
            norms[3],
            norms[2],
            norms[4],
            norms[5],
            expand_grad,
            expand_row,
            reduce_grad,
            norms[7],
            norms[6],
            low_grad.T,
            high_grad.T,
        )
    if not known:
        reduce_grad, expand_grad, attn_grads, tail, low_grad, high_grad = lax.psum(
            (
                reduce_grad.astype(floating),
                expand_grad.astype(floating),
                attn_grads.astype(floating),
                small[8:],
                low_grad,
                high_grad,
            ),
            "dp",
        )
        small = jnp.concatenate((lax.psum(small[:8], ("dp", "tensor")), tail), axis=0)
    return (
        result,
        hidden_grad,
        small[0],
        small[1],
        attn_grads[:width].astype(floating).T,
        small[8, :width],
        attn_grads[width : 2 * width].astype(floating).T,
        attn_grads[2 * width : 3 * width].astype(floating).T,
        small[8, 256 : 256 + width],
        attn_grads[3 * width :].astype(floating),
        small[3],
        small[2],
        small[4],
        small[5],
        expand_grad.astype(floating),
        small[9],
        reduce_grad.astype(floating),
        small[7],
        small[6],
        low_grad[:, : table_low.shape[0]].T,
        high_grad[:, : table_high.shape[0]].T,
    )


def solution(mesh):
    in_specs = (
        P(("dp", "tensor"), None),
        P(),
        P(),
        P(None, "tensor"),
        P("tensor"),
        P(None, "tensor"),
        P(None, "tensor"),
        P("tensor"),
        P("tensor", None),
        P(),
        P(),
        P(),
        P(),
        P(None, "tensor"),
        P("tensor"),
        P("tensor", None),
        P(),
        P(),
        P(None, "tensor"),
        P(None, "tensor"),
        P("dp"),
        P("dp"),
        P(),
        P(),
        P(("dp", "tensor"), None),
    )
    out_specs = (
        P(("dp", "tensor"), None),
        P(("dp", "tensor"), None),
        P(),
        P(),
        P(None, "tensor"),
        P("tensor"),
        P(None, "tensor"),
        P(None, "tensor"),
        P("tensor"),
        P("tensor", None),
        P(),
        P(),
        P(),
        P(),
        P(None, "tensor"),
        P("tensor"),
        P("tensor", None),
        P(),
        P(),
        P(None, "tensor"),
        P(None, "tensor"),
    )
    return jax.shard_map(local, mesh=mesh, in_specs=in_specs, out_specs=out_specs, check_vma=False)
```

```python
import functools

import jax
import jax.numpy as jnp
from jax import lax
from jax.experimental import pallas as pl
from jax.experimental.pallas import tpu as pltpu
from jax.sharding import PartitionSpec as P

HD = 64
P_LO = 197
P_HI = 577
SEQ = 640
SLOTS = 2


eps_norm = 1e-06
masked_score = -1e30
inv_sqrt_two = 0.7071067811865476
inv_sqrt_two_pi = 0.3989422804014327


F32=jnp.float32; BF=jnp.bfloat16
NT=(((1,),(1,)),((),()))
def head_mask(h, width):
    lane = lax.broadcasted_iota(jnp.int32, (1, width), 1)
    return ((lane >= h*HD) & (lane < (h+1)*HD)).astype(F32).astype(BF)


BB=32; UN=16
def scatter_run(idx_ref, g_ref, out, first, last, fresh):
    heads = g_ref.shape[0]; na = out.shape[1]; m = idx_ref.shape[1]
    if fresh:
        out[...] = jnp.zeros_like(out)
    ib = lax.broadcasted_iota(jnp.int32, (16, m), 0).astype(F32)
    def body(r, c):
        ms = []; os = []
        for u in range(UN):
            row = r*UN+u
            idx = jnp.broadcast_to(idx_ref[pl.ds(row,1), :], (16, m))
            ia = (idx >> 5).astype(F32).astype(BF); il = (idx & 31).astype(F32).astype(BF)
            g = [jnp.broadcast_to(g_ref[h, pl.ds(row,1), :], (16, m)).astype(BF) for h in range(heads)]
            hits = [il == (ib + 16.0*k).astype(BF) for k in range(BB//16)]
            ms.append(jnp.concatenate([jnp.where(hits[k], g[h], jnp.zeros_like(g[h])) for h in range(heads) for k in range(BB//16)], axis=0))
            os.append(jnp.concatenate([jnp.where(ia == (ib + 16.0*k).astype(BF), jnp.ones_like(ia), jnp.zeros_like(ia)) for k in range(na//16)], axis=0))
        out[...] += lax.dot_general(jnp.concatenate(ms, axis=1), jnp.concatenate(os, axis=1), NT, preferred_element_type=F32)
        return c
    lax.fori_loop(first, last, body, 0)

PACK=8191.0
MESH = pl.DeviceIdType.MESH

CHUNKS = 9
TN = (((0,), (0,)), ((), ()))

def row(ref):
    return ref[...].reshape(1, ref.shape[0])

def live_of(t, rows, res, counts):
    slot = t * rows // SEQ
    first = t * rows - slot * SEQ
    limit = jnp.where(res[slot] == 1, P_HI, P_LO)
    limit = jnp.where(slot < counts[0], limit, 0)
    place = lax.broadcasted_iota(jnp.int32, (rows, 1), 0) + first
    return jnp.where(place < limit, 1.0, 0.0).astype(F32)

def moments(values):
    center = jnp.mean(values, axis=1, keepdims=True)
    centered = values - center
    inverse = lax.rsqrt(jnp.mean(centered * centered, axis=1, keepdims=True) + eps_norm)
    return centered * inverse, inverse

def norm_back(grad, scaled, inverse, gain):
    inner = grad * gain
    mean_inner = jnp.mean(inner, axis=1, keepdims=True)
    mean_mixed = jnp.mean(inner * scaled, axis=1, keepdims=True)
    return inverse * (inner - mean_inner - scaled * mean_mixed)

def look_up(tab, idx, heads):
    nch = tab.shape[1]
    lane = idx & 127
    ch = idx >> 7
    shift = jnp.where(ch >= nch, 0, 16)
    ch = jnp.where(ch >= nch, ch - nch, ch)
    acc = [None] * heads
    for k in range(nch):
        hit = ch == k
        for h in range(heads):
            v = jnp.take_along_axis(tab[h, k], lane, axis=1)
            acc[h] = v if k == 0 else jnp.where(hit, v, acc[h])
    return [((acc[h] << shift) >> 16).astype(F32) * (1.0 / PACK) for h in range(heads)]

def bias_rows(res, tab_lo, tab_hi, idx_lo, idx_hi, out, first, last, both):
    slots, heads = out.shape[:2]
    def masked(vals, j, limit):
        if (j + 1) * 128 <= limit:
            return vals
        place = lax.broadcasted_iota(jnp.int32, (8, 128), 1) + j * 128
        return [jnp.where(place < limit, v, masked_score) for v in vals]
    def body(r, c):
        for j in range(idx_hi.shape[1] // 128):
            cols = pl.ds(j * 128, 128)
            high = []
            low = []
            for part in range(2):
                rows = pl.ds(pl.multiple_of(r * 16 + part * 8, 8), 8)
                high.append(masked(look_up(tab_hi, idx_hi[rows, cols], heads), j, P_HI))
                if both and j < idx_lo.shape[1] // 128:
                    low.append(masked(look_up(tab_lo, idx_lo[rows, cols], heads), j, P_LO))
                else:
                    low.append([jnp.full((8, 128), masked_score, F32)] * heads)
            for h in range(heads):
                hi = jnp.concatenate([high[0][h], high[1][h]], axis=0).astype(BF)
                lo = jnp.concatenate([low[0][h], low[1][h]], axis=0).astype(BF)
                for s in range(slots):
                    out[s, h, pl.ds(pl.multiple_of(r * 16, 16), 16), cols] = jnp.where(res[s] == 1, hi, lo)
        return c
    lax.fori_loop(first, last, body, 0)

def layer_kernel(scale, sums, res, counts, hidden, gain1, shift1, wq, bq, wk, wv, bv, wo, bo, scale1, gain2, shift2, we, be, wr, rbias, scale2, cot,
                 table_lo, table_hi, ilo_in, ihi_in,
                 o0, o1, o2, result, hidden_grad, small, tlow, thigh,
                 tab_lo, tab_hi, raw, ilo, ihi, flip,
                 g1, gm, gt, ga, q_buf, k_buf, v_buf, mix, dmix, pb, act, pgl, part, acc, attn, x0, x1, x2, ghi, glo, esum,
                 cbuf, ccore, xbuf, xin, acore, across, bcore, bcross, ybuf, zbuf,
                 tlo, thi, wmine, smine, wten, vec, vland, vout, tbl, tland, tout,
                 h_s, h_r, m_s, m_r, t_s, t_r, a_s, a_r, o_s, o_r, n_s, n_r,
                 y_s, y_r, z_s, z_r, g_s, g_r, e_s, e_r, r_s, r_r, w_s, w_r, v_s, v_r):
    d = lax.axis_index("dp")
    t = lax.axis_index("tensor")
    col = d // 2
    side = lax.rem(d, 2)
    neighbour = d + 1 - 2 * side
    sibling = t + 1 - 2 * lax.rem(t, 2)
    cross = lax.rem(t + 2, 4)
    diag = 3 - t
    rows = hidden.shape[0]
    half = rows // 2
    slots, heads = pb.shape[:2]
    width = q_buf.shape[1]
    model = g1.shape[1]
    barrier = pltpu.get_barrier_semaphore()
    for k in range(1, 4):
        pl.semaphore_signal(barrier, inc=1, device_id=(d, lax.rem(t + k, 4)), device_id_type=MESH)
    if sums:
        for k in range(1, 8):
            pl.semaphore_signal(barrier, inc=1, device_id=(lax.rem(d + k, 8), t), device_id_type=MESH)

    def remote(src, dst, send, recv, device):
        return pltpu.make_async_remote_copy(src_ref=src, dst_ref=dst, send_sem=send, recv_sem=recv, device_id=device, device_id_type=MESH)
    def rows_at(who):
        return pl.ds(pl.multiple_of(who * rows, 16), rows)
    def span(who, h):
        return pl.ds(pl.multiple_of(who * rows + h * half, 16), half)
    def gather_x(buf, send, recv, h):
        here = buf.at[span(t, h)]
        return remote(here, here, send.at[h], recv.at[h], (d, cross))
    def gather_near(buf, send, recv, h):
        here = buf.at[span(t, h)]
        return remote(here, here, send.at[2 + h], recv.at[2 + h], (d, sibling))
    def gather_on(buf, send, recv, h):
        here = buf.at[span(cross, h)]
        return remote(here, here, send.at[4 + h], recv.at[4 + h], (d, sibling))
    def sum_far(j, send, recv, h):
        return remote(cbuf.at[0, h], ccore.at[j, 0, h], send.at[h], recv.at[h], (d, sibling))
    def sum_near(j, send, recv, h):
        return remote(cbuf.at[1, h], ccore.at[j, 1, h], send.at[2 + h], recv.at[2 + h], (d, sibling))
    def sum_x(j, send, recv, h):
        return remote(xbuf.at[h], xin.at[j, h], send.at[4 + h], recv.at[4 + h], (d, cross))
    arrays = (x0, x1, x2)
    outs = (o0, o1, o2)
    size = x0.shape[0] // 3
    part_y = size // 2
    part_z = part_y // 4
    def at(n, start, count):
        return pl.ds(pl.multiple_of((n % 3) * size + start, 16), count)
    def y_copy(n):
        return remote(arrays[n // 3].at[at(n, (1 - side) * part_y, part_y)], ybuf.at[n], y_s.at[n], y_r.at[n], (neighbour, t))
    def z_copy(n, k):
        to = lax.rem(col + k, 4)
        return remote(arrays[n // 3].at[at(n, side * part_y + to * part_z, part_z)], zbuf.at[n, k - 1], z_s.at[n, k], z_r.at[n, k], (to * 2 + side, t))
    def g_copy(n, k):
        to = lax.rem(col + k, 4)
        here = outs[n // 3].at[at(n, side * part_y + col * part_z, part_z)]
        return remote(here, here, g_s.at[n, k], g_r.at[n, k], (to * 2 + side, t))
    def e_copy(n):
        here = outs[n // 3].at[at(n, side * part_y, part_y)]
        return remote(here, here, e_s.at[n], e_r.at[n], (neighbour, t))
    def start_y(n):
        y_copy(n).start()
    def step_a(n):
        y_copy(n).wait()
        here = at(n, side * part_y, part_y)
        arrays[n // 3][here] = (arrays[n // 3][here].astype(F32) + ybuf[n].astype(F32)).astype(BF)
        for k in range(1, 4):
            z_copy(n, k).start()
    def step_b(n):
        for k in range(1, 4):
            z_copy(n, k).wait()
        here = at(n, side * part_y + col * part_z, part_z)
        total = arrays[n // 3][here].astype(F32)
        for k in range(3):
            total = total + zbuf[n, k].astype(F32)
        outs[n // 3][here] = total.astype(BF)
        for k in range(1, 4):
            g_copy(n, k).start()
    def step_d(n):
        for k in range(1, 4):
            g_copy(n, k).wait()
        e_copy(n).start()
    if not sums:
        start_y = step_a = step_b = step_d = lambda n: None

    scaled, inverse = moments(hidden[...].astype(F32))
    g1[rows_at(t)] = (scaled * row(gain1) + row(shift1)).astype(BF)
    pl.semaphore_wait(barrier, 10 if sums else 3)
    for h in range(2):
        gather_x(g1, h_s, h_r, h).start()
        gather_near(g1, h_s, h_r, h).start()
    alive = live_of(t, rows, res, counts)
    gm[rows_at(t)] = (cot[...].astype(F32) * alive * row(scale2)).astype(BF)
    ilo[...] = jnp.zeros_like(ilo)
    ilo[0:P_LO, 0:P_LO] = ilo_in[...]
    ihi[...] = jnp.zeros_like(ihi)
    ihi[0:P_HI, 0:P_HI] = ihi_in[...]
    for table, packed in ((table_lo, tab_lo), (table_hi, tab_hi)):
        nch = packed.shape[1]
        raw[...] = jnp.zeros_like(raw)
        raw[:, 0:table.shape[1]] = table[...]
        for k in range(nch):
            low = (raw[:, k * 128:(k + 1) * 128] * PACK + 32768.5).astype(jnp.int32) - 32768
            high = (raw[:, (k + nch) * 128:(k + nch + 1) * 128] * PACK + 32768.5).astype(jnp.int32) - 32768
            word = (high << 16) | (low & 65535)
            for h in range(heads):
                packed[h, k] = jnp.broadcast_to(word[h:h + 1, :], (8, 128))
    look = functools.partial(bias_rows, res, tab_lo, tab_hi, ilo, ihi, pb)
    n_low = -(-P_LO // 16)
    n_high = -(-P_HI // 16)
    middle = (n_low + n_high) // 2
    look(0, n_low, True)
    look(n_low, middle, False)
    for h in range(2):
        gather_x(g1, h_s, h_r, h).wait()
        gather_on(g1, h_s, h_r, h).start()
        gather_x(gm, m_s, m_r, h).start()
        gather_near(gm, m_s, m_r, h).start()
    look(middle, n_high, False)
    pb[:, :, n_high * 16:, :] = jnp.zeros((slots, heads, SEQ - n_high * 16, SEQ), BF)
    for h in range(2):
        gather_near(g1, h_s, h_r, h).wait()
        gather_on(g1, h_s, h_r, h).wait()

    def project(i, c):
        here = rows_at(i)
        g = g1[here]
        q_buf[here] = ((lax.dot_general(g, wq[...], NT, preferred_element_type=F32) + row(bq)) * scale).astype(BF)
        k_buf[here] = lax.dot_general(g, wk[...], NT, preferred_element_type=F32).astype(BF)
        v_buf[here] = (lax.dot_general(g, wv[...], NT, preferred_element_type=F32) + row(bv)).astype(BF)
        return c
    lax.fori_loop(0, 4, project, 0)

    def attend_image(slot):
        here = pl.ds(pl.multiple_of(slot * SEQ, 16), SEQ)
        k = k_buf[here]
        v = v_buf[here]
        vm = [v * head_mask(h, width) for h in range(heads)]
        def piece(i, c):
            first = pl.multiple_of(i * rows, 16)
            there = pl.ds(pl.multiple_of(slot * SEQ + first, 16), rows)
            q = q_buf[there]
            out = jnp.zeros((rows, width), F32)
            for h in range(heads):
                s = lax.dot_general(q * head_mask(h, width), k, NT, preferred_element_type=F32)
                s = s + pb[slot, h, pl.ds(first, rows)].astype(F32)
                peak = jnp.max(s, axis=1, keepdims=True)
                e = jnp.exp(s - peak)
                total = jnp.sum(e, axis=1, keepdims=True)
                p = (e * (1.0 / total)).astype(BF)
                pb[slot, h, pl.ds(first, rows)] = p
                out = out + jnp.dot(p, vm[h], preferred_element_type=F32)
            mix[there] = out.astype(BF)
            return c
        lax.fori_loop(0, SEQ // rows, piece, 0)
    def output_of(who, h):
        return jnp.dot(mix[span(who, h)], wo[...], preferred_element_type=F32)

    mine = t * rows // SEQ
    attend_image(1 - mine)
    for h in range(2):
        cbuf[0, h] = output_of(diag, h).astype(BF)
        sum_far(0, o_s, o_r, h).start()
    for h in range(2):
        total = output_of(cross, h)
        sum_far(0, o_s, o_r, h).wait()
        xbuf[h] = (total + ccore[0, 0, h].astype(F32)).astype(BF)
        sum_x(0, o_s, o_r, h).start()
    attend_image(mine)
    for h in range(2):
        cbuf[1, h] = output_of(sibling, h).astype(BF)
        sum_near(0, o_s, o_r, h).start()
    for h in range(2):
        acc[pl.ds(h * half, half)] = output_of(t, h)
    for h in range(2):
        gather_x(gm, m_s, m_r, h).wait()
        gather_on(gm, m_s, m_r, h).start()
    for h in range(2):
        here = pl.ds(h * half, half)
        sum_near(0, o_s, o_r, h).wait()
        sum_x(0, o_s, o_r, h).wait()
        out = acc[here] + ccore[0, 1, h].astype(F32) + xin[0, h].astype(F32) + row(bo)
        attn[here] = out
        scaled, inverse = moments(hidden[here].astype(F32) + row(scale1) * out)
        gt[span(t, h)] = (scaled * row(gain2) + row(shift2)).astype(BF)
        gather_x(gt, t_s, t_r, h).start()
        gather_near(gt, t_s, t_r, h).start()

    esum[...] = jnp.zeros_like(esum)
    def feed(who, h):
        here = span(who, h)
        pre = jnp.dot(gt[here], we[...], preferred_element_type=F32) + row(be)
        grad = lax.dot_general(gm[here], wr[...], NT, preferred_element_type=F32)
        phi = 0.5 * (1.0 + lax.erf(pre * inv_sqrt_two))
        active = (pre * phi).astype(BF)
        act[here] = active
        grad = grad * (phi + pre * inv_sqrt_two_pi * jnp.exp(-0.5 * pre * pre))
        esum[...] += jnp.sum(grad, axis=0, keepdims=True)
        grad = grad.astype(BF)
        pgl[here] = grad
        part[here] = jnp.dot(active, wr[...], preferred_element_type=F32).astype(BF)
        return lax.dot_general(grad, we[...], NT, preferred_element_type=F32)
    def feed_own(h, c):
        acc[pl.ds(pl.multiple_of(h * half, 16), half)] = feed(t, h)
        return c
    lax.fori_loop(0, 2, feed_own, 0)
    for h in range(2):
        gather_near(gm, m_s, m_r, h).wait()
        gather_near(gt, t_s, t_r, h).wait()
        gather_on(gm, m_s, m_r, h).wait()
    def feed_near(h, c):
        cbuf[1, h] = feed(sibling, h).astype(BF)
        sum_near(1, n_s, n_r, h).start()
        return c
    lax.fori_loop(0, 2, feed_near, 0)
    def feed_far(h, c):
        gather_x(gt, t_s, t_r, h).wait()
        gather_on(gt, t_s, t_r, h).start()
        total = feed(cross, h)
        gather_on(gt, t_s, t_r, h).wait()
        cbuf[0, h] = feed(diag, h).astype(BF)
        sum_far(1, n_s, n_r, h).start()
        sum_far(1, n_s, n_r, h).wait()
        xbuf[h] = (total + ccore[1, 0, h].astype(F32)).astype(BF)
        sum_x(1, n_s, n_r, h).start()
        return c
    lax.fori_loop(0, 2, feed_far, 0)

    tile = 128
    def reduce_grad(i, c):
        cols = pl.ds(pl.multiple_of(i * tile, tile), tile)
        x0[cols] = lax.dot_general(act[:, cols], gm[...], TN, preferred_element_type=F32).astype(BF)
        return c
    third = act.shape[1] // tile // 3
    lax.fori_loop(0, third, reduce_grad, 0)
    start_y(0)
    lax.fori_loop(third, 2 * third, reduce_grad, 0)
    start_y(1)
    lax.fori_loop(2 * third, 3 * third, reduce_grad, 0)
    start_y(2)
    wmine[...] = jnp.zeros_like(wmine)
    def second_back(h):
        here = pl.ds(h * half, half)
        sum_near(1, n_s, n_r, h).wait()
        sum_x(1, n_s, n_r, h).wait()
        grad = acc[here] + ccore[1, 1, h].astype(F32) + xin[1, h].astype(F32)
        out = attn[here]
        scaled, inverse = moments(hidden[here].astype(F32) + row(scale1) * out)
        after = cot[here].astype(F32) * alive[h * half:(h + 1) * half] + norm_back(grad, scaled, inverse, row(gain2))
        hidden_grad[here] = after
        agrad = after * row(scale1)
        ga[span(t, h)] = agrad.astype(BF)
        gather_x(ga, a_s, a_r, h).start()
        gather_near(ga, a_s, a_r, h).start()
        wmine[2:3, :] += jnp.sum(after * out, axis=0, keepdims=True)
        wmine[3:4, :] += jnp.sum(agrad, axis=0, keepdims=True)
        wmine[4:5, :] += jnp.sum(grad * scaled, axis=0, keepdims=True)
        wmine[5:6, :] += jnp.sum(grad, axis=0, keepdims=True)
    second_back(0)
    step_a(0)
    def expand_grad(i, c):
        cols = pl.ds(pl.multiple_of(i * tile, tile), tile)
        x1[cols] = lax.dot_general(gt[:, cols], pgl[...], TN, preferred_element_type=F32).astype(BF)
        return c
    lax.fori_loop(0, third, expand_grad, 0)
    lax.fori_loop(third, 2 * third, expand_grad, 0)
    start_y(3)
    start_y(4)
    lax.fori_loop(2 * third, 3 * third, expand_grad, 0)
    step_a(1)
    second_back(1)
    step_b(0)
    step_a(2)
    start_y(5)
    def mixture_of(who):
        here = rows_at(who)
        dmix[here] = lax.dot_general(ga[here], wo[...], NT, preferred_element_type=F32).astype(BF)
    mixture_of(t)
    gather_x(ga, a_s, a_r, 0).wait()
    gather_on(ga, a_s, a_r, 0).start()
    for h in range(2):
        gather_near(ga, a_s, a_r, h).wait()
    mixture_of(sibling)
    step_b(1)
    gather_x(ga, a_s, a_r, 1).wait()
    gather_on(ga, a_s, a_r, 1).start()
    mixture_of(cross)
    step_a(3)
    step_a(4)
    for h in range(2):
        gather_on(ga, a_s, a_r, h).wait()
    mixture_of(diag)
    smine[...] = jnp.zeros_like(smine)
    smine[1:2, :] = esum[...]
    def attention_back(slot):
        here = slice(slot * SEQ, (slot + 1) * SEQ)
        q = q_buf[here]
        k = k_buf[here]
        v = v_buf[here]
        dd = dmix[here]
        qt = q.T
        dt = dd.T
        is_high = jnp.where(res[slot] == 1, 1.0, 0.0).astype(F32)
        out = jnp.zeros((SEQ, width), F32)
        dks = []
        dvs = []
        nh = ghi.shape[1]
        nl, ml = glo.shape[1:]
        for h in range(heads):
            mask = head_mask(h, width)
            p = pb[slot, h]
            dp = lax.dot_general(dd * mask, v, NT, preferred_element_type=F32)
            pf = p.astype(F32)
            m = pf * dp
            ds = m - pf * jnp.sum(m, axis=1, keepdims=True)
            if slot == 0:
                ghi[h] = ds[:nh] * is_high
                glo[h] = ds[:nl, :ml] * (1.0 - is_high)
            else:
                ghi[h] += ds[:nh] * is_high
                glo[h] += ds[:nl, :ml] * (1.0 - is_high)
            low = ds.astype(BF)
            out = out + jnp.dot(low, k * mask, preferred_element_type=F32)
            dks.append(jnp.dot(qt[h*HD:(h+1)*HD], low, preferred_element_type=F32))
            dvs.append(jnp.dot(dt[h*HD:(h+1)*HD], p, preferred_element_type=F32))
        out = out * scale
        smine[0:1, 0:width] += jnp.sum(out, axis=0, keepdims=True)
        q_buf[here] = out.astype(BF)
        k_buf[here] = jnp.concatenate(dks, axis=0).T.astype(BF)
        out = jnp.concatenate(dvs, axis=0).T
        smine[0:1, 256:256 + width] += jnp.sum(out, axis=0, keepdims=True)
        v_buf[here] = out.astype(BF)
    attention_back(0)
    attention_back(1)
    def back(who):
        here = rows_at(who)
        total = jnp.dot(q_buf[here], wq[...], preferred_element_type=F32)
        total = total + jnp.dot(k_buf[here], wk[...], preferred_element_type=F32)
        return total + jnp.dot(v_buf[here], wv[...], preferred_element_type=F32)
    def send(buf, value):
        for h in range(2):
            buf[h] = value[h * half:(h + 1) * half].astype(BF)
    def whole(ref):
        return jnp.concatenate([ref[0], ref[1]], axis=0).astype(F32)
    a_far = remote(cbuf.at[0], acore.at[0], r_s.at[0], r_r.at[0], (d, sibling))
    a_near = remote(cbuf.at[1], acore.at[1], r_s.at[1], r_r.at[1], (d, sibling))
    a_cross = remote(xbuf, across, r_s.at[2], r_r.at[2], (d, cross))
    b_far = remote(part.at[rows_at(diag)], bcore.at[0], r_s.at[3], r_r.at[3], (d, sibling))
    b_near = remote(part.at[rows_at(sibling)], bcore.at[1], r_s.at[4], r_r.at[4], (d, sibling))
    b_cross = remote(xbuf, bcross, r_s.at[5], r_r.at[5], (d, cross))
    send(cbuf.at[0], back(diag))
    a_far.start()
    b_far.start()
    total = back(cross)
    a_far.wait()
    send(xbuf, total + whole(acore.at[0]))
    a_cross.start()
    step_d(1)
    step_b(3)
    for j, (left, right) in list(enumerate(((q_buf, g1), (k_buf, g1), (v_buf, g1), (mix, ga))))[0:2]:
        x2[j * width:(j + 1) * width, :] = lax.dot_general(left[...], right[...], TN, preferred_element_type=F32).astype(BF)
    step_d(0)
    step_b(2)
    start_y(6)
    for j, (left, right) in list(enumerate(((q_buf, g1), (k_buf, g1), (v_buf, g1), (mix, ga))))[2:3]:
        x2[j * width:(j + 1) * width, :] = lax.dot_general(left[...], right[...], TN, preferred_element_type=F32).astype(BF)
    for j, (left, right) in list(enumerate(((q_buf, g1), (k_buf, g1), (v_buf, g1), (mix, ga))))[3:4]:
        x2[j * width:(j + 1) * width, :] = lax.dot_general(left[...], right[...], TN, preferred_element_type=F32).astype(BF)
    step_a(5)
    start_y(7)
    send(cbuf.at[1], back(sibling))
    a_near.start()
    b_near.start()
    acc[...] = back(t)
    b_far.wait()
    n_hi = -(-P_HI // UN)
    done = [0]
    def scatter_part(count):
        first, last = done[0], min(done[0] + count, n_hi)
        scatter_run(ihi, ghi, thi, first, last, first == 0)
        done[0] = last
    scatter_part(3)
    scatter_part(3)
    step_b(4)
    start_y(8)
    a_cross.wait()
    send(xbuf, part[rows_at(cross)].astype(F32) + bcore[0].astype(F32))
    b_cross.start()
    a_near.wait()
    grad = acc[...] + whole(acore.at[1]) + whole(across)
    scaled, inverse = moments(hidden[...].astype(F32))
    wmine[0:1, :] = jnp.sum(grad * scaled, axis=0, keepdims=True)
    wmine[1:2, :] = jnp.sum(grad, axis=0, keepdims=True)
    hidden_grad[...] += norm_back(grad, scaled, inverse, row(gain1))
    scatter_part(3)
    step_b(5)
    scatter_part(3)
    step_a(6)
    scatter_part(3)
    scatter_part(3)
    step_d(5)
    b_near.wait()
    b_cross.wait()
    out = part[rows_at(t)].astype(F32) + bcore[1].astype(F32) + whole(bcross) + row(rbias)
    after = hidden[...].astype(F32) + row(scale1) * attn[...]
    result[...] = ((after + row(scale2) * out) * alive).astype(BF)
    up = cot[...].astype(F32) * alive
    wmine[6:7, :] = jnp.sum(up * out, axis=0, keepdims=True)
    wmine[7:8, :] = jnp.sum(up * row(scale2), axis=0, keepdims=True)
    step_d(4)
    step_a(8)
    def w_copy(k):
        return remote(wmine, wten.at[k], w_s.at[k], w_r.at[k], (d, lax.rem(t + k, 4)))
    def eighth(buf, who):
        count = buf.shape[0] // 8
        return buf.at[pl.ds(pl.multiple_of(who * count, 8), count)]
    def v_copy(j, k):
        buf, land = ((vec, vland), (tbl, tland))[j]
        to = lax.rem(d + k, 8)
        return remote(eighth(buf, to), land.at[k], v_s.at[j, k], v_r.at[j, k], (to, t))
    def u_copy(j, k):
        buf = (vout, tout)[j]
        return remote(eighth(buf, d), eighth(buf, d), v_s.at[2 + j, k], v_r.at[2 + j, k], (lax.rem(d + k, 8), t))
    def small_start(j):
        for k in range(1, 8):
            v_copy(j, k).start()
    def small_turn(j):
        buf, land = ((vec, vland), (tbl, tland))[j]
        total = eighth(buf, d)[...]
        for k in range(1, 8):
            v_copy(j, k).wait()
            total = total + land[k]
        eighth((vout, tout)[j], d)[...] = total
        for k in range(1, 8):
            u_copy(j, k).start()
    def small_end(j):
        for k in range(1, 8):
            u_copy(j, k).wait()
    if not sums:
        def small_turn(j):
            (vout, tout)[j][...] = (vec, tbl)[j][...]
        small_start = small_end = lambda j: None
    if sums:
        for k in range(1, 4):
            w_copy(k).start()
    step_a(7)
    scatter_part(3)
    scatter_part(3)
    step_d(2)
    total = wmine[...]
    if sums:
        for k in range(1, 4):
            w_copy(k).wait()
            total = total + wten[k]
    vec[...] = jnp.zeros_like(vec)
    lanes = model // 128
    for r in range(8):
        for j in range(lanes):
            vec[r * lanes + j:r * lanes + j + 1, :] = total[r:r + 1, j * 128:(j + 1) * 128]
    for r in range(2):
        for j in range(lanes):
            vec[(8 + r) * lanes + j:(8 + r) * lanes + j + 1, :] = smine[r:r + 1, j * 128:(j + 1) * 128]
    small_start(0)
    scatter_part(3)
    step_d(3)
    step_b(6)
    scatter_part(3)
    step_b(8)
    scatter_part(3)
    step_b(7)
    scatter_part(n_hi)
    small_turn(0)
    step_d(6)
    scatter_run(ilo, glo, tlo, 0, -(-P_LO // UN), True)
    step_d(8)
    per = (thi.shape[1] + tlo.shape[1]) // 4
    tbl[...] = jnp.zeros_like(tbl)
    def spread(src, base):
        count = src.shape[1] // 4
        for h in range(heads):
            flip[0:src.shape[1], :] = src[h * BB:(h + 1) * BB, :].T
            pieces = [flip[pl.ds(i, count, stride=4), :] for i in range(4)]
            start = h * per + base
            tbl[start:start + count, :] = jnp.concatenate(pieces, axis=1)
    spread(thi, 0)
    spread(tlo, thi.shape[1] // 4)
    if not sums:
        o0[...] = x0[...]
        o1[...] = x1[...]
        o2[...] = x2[...]
    small_start(1)
    step_d(7)
    small_end(0)
    for r in range(10):
        for j in range(lanes):
            small[r:r + 1, j * 128:(j + 1) * 128] = vout[r * lanes + j:r * lanes + j + 1, :]
    small_turn(1)
    small_end(1)
    for src, base, count in ((thigh, 0, thi.shape[1] // 4), (tlow, thi.shape[1] // 4, tlo.shape[1] // 4)):
        for h in range(heads):
            for r in range(count):
                at_row = h * per + base + r
                src[h:h + 1, r * 128:(r + 1) * 128] = tout[at_row:at_row + 1, :]
    if sums:
        for n in range(CHUNKS):
            e_copy(n).wait()

def layer(scale, sums, res, counts, hidden, gain1, shift1, wq, bq, wk, wv, bv, wo, bo, scale1, gain2, shift2, we, be, wr, rbias, scale2, cot, table_low, table_high, ilo, ihi, n_lo, n_hi):
    rows, model = hidden.shape
    total = rows * 4
    width = wq.shape[0]
    inner = we.shape[1]
    heads, e_lo = table_low.shape
    e_hi = table_high.shape[1]
    vm = pl.BlockSpec(memory_space=pltpu.VMEM)
    sm = pl.BlockSpec(memory_space=pltpu.SMEM)
    dma = pltpu.SemaphoreType.DMA
    V = pltpu.VMEM
    S = jax.ShapeDtypeStruct
    operands = (hidden, gain1, shift1, wq, bq, wk, wv, bv, wo, bo, scale1, gain2, shift2, we, be, wr, rbias, scale2, cot, table_low, table_high, ilo, ihi)
    half = rows // 2
    return pl.pallas_call(functools.partial(layer_kernel, scale, sums),
        out_shape=(S((inner, model), BF), S((model, inner), BF), S((4 * width, model), BF), S((rows, model), BF), S((rows, model), F32), S((16, model), F32), S((heads, n_lo * 32), F32), S((heads, n_hi * 32), F32)),
        in_specs=[sm, sm] + [vm] * len(operands), out_specs=(vm,) * 8,
        scratch_shapes=[V((heads, -(-e_lo // 256), 8, 128), jnp.int32), V((heads, -(-e_hi // 256), 8, 128), jnp.int32), V((heads, -(-e_hi // 256) * 256), F32), V((208, 256), jnp.int32), V((592, SEQ), jnp.int32), V((n_hi, BB), F32)]
            + [V((total, model), BF)] * 4 + [V((total, width), BF)] * 5 + [V((SLOTS, heads, SEQ, SEQ), BF)]
            + [V((total, inner), BF)] * 2 + [V((total, model), BF)] + [V((rows, model), F32)] * 2
            + [V((inner, model), BF), V((model, inner), BF), V((4 * width, model), BF), V((heads, 592, SEQ), F32), V((heads, 208, 256), F32), V((1, inner), F32)]
            + [V((2, 2, half, model), BF), V((2, 2, 2, half, model), BF)] + [V((2, half, model), BF), V((2, 2, half, model), BF)]
            + [V((2, 2, half, model), BF), V((2, half, model), BF), V((2, rows, model), BF), V((2, half, model), BF)]
            + [V((CHUNKS, 128, model), BF), V((CHUNKS, 3, 32, model), BF)]
            + [V((heads * BB, n_lo), F32), V((heads * BB, n_hi), F32)]
            + [V((8, model), F32)] * 2 + [V((4, 8, model), F32), V((64, 128), F32), V((8, 8, 128), F32), V((64, 128), F32), V((128, 128), F32), V((8, 16, 128), F32), V((128, 128), F32)]
            + [dma((6,))] * 12
            + [dma((CHUNKS,)), dma((CHUNKS,)), dma((CHUNKS, 4)), dma((CHUNKS, 4)), dma((CHUNKS, 4)), dma((CHUNKS, 4)), dma((CHUNKS,)), dma((CHUNKS,)),
               dma((6,)), dma((6,)), dma((4,)), dma((4,)), dma((4, 8)), dma((4, 8))],
        name="layer", cost_estimate=pl.CostEstimate(flops=100 * 10**9, bytes_accessed=60 * 10**6, transcendentals=0),
        compiler_params=pltpu.CompilerParams(collective_id=0, has_side_effects=True, vmem_limit_bytes=127 << 19))(res, counts, *operands)


def finish_kernel(pieces, i0, i1, i2, small, tlow, thigh, res_in, hid_in, *refs):
    r_out, e_out, q_out, k_out, v_out, o_out = refs[:6]
    vectors = refs[6:14]
    qb, vb, eb, tl, th, res_out, hid_out, low, wide, res, hid, s_in, s_out, s_x = refs[14:]
    first = [pltpu.make_async_copy(hid_in, hid, s_x.at[0]), pltpu.make_async_copy(res_in, res, s_x.at[1])]
    second = [pltpu.make_async_copy(hid, hid_out, s_x.at[2]), pltpu.make_async_copy(res, res_out, s_x.at[3])]
    rows = low.shape[1]
    places = []
    for src, out in ((i0, r_out), (i1, e_out)):
        for n in range(pieces):
            here = pl.ds(n * rows, rows)
            places.append((src.at[here], out.at[here]))
    for n, out in enumerate((q_out, k_out, v_out, o_out)):
        places.append((i2.at[pl.ds(n * rows, rows)], out))
    loads = [pltpu.make_async_copy(src, low.at[n], s_in.at[n]) for n, (src, _) in enumerate(places)]
    stores = [pltpu.make_async_copy(wide.at[n], out, s_out.at[n]) for n, (_, out) in enumerate(places)]
    for copy in first + loads:
        copy.start()
    for before, after in zip(first, second):
        before.wait()
        after.start()
    for n in range(len(places)):
        loads[n].wait()
        wide[n] = low[n].astype(F32)
        stores[n].start()
    for r, out in enumerate(vectors):
        out[...] = small[r:r + 1, :].reshape(out.shape)
    qb[...] = small[8:9, 0:qb.shape[0]].reshape(qb.shape)
    vb[...] = small[8:9, 256:256 + vb.shape[0]].reshape(vb.shape)
    eb[...] = small[9:10, :].reshape(eb.shape)
    tl[...] = tlow[:, 0:tl.shape[1]]
    th[...] = thigh[:, 0:th.shape[1]]
    for copy in stores + second:
        copy.wait()

def finish(reduce_grad, expand_grad, attn_grads, small, low_grad, high_grad, result, hidden_grad, width, e_lo, e_hi):
    S = jax.ShapeDtypeStruct
    vm = pl.BlockSpec(memory_space=pltpu.VMEM)
    anywhere = pl.BlockSpec(memory_space=pl.ANY)
    model = reduce_grad.shape[1]
    pieces = reduce_grad.shape[0] // width
    count = 2 * pieces + 4
    shapes = (S(reduce_grad.shape, F32), S(expand_grad.shape, F32)) + (S((width, model), F32),) * 4 + (S((model,), F32),) * 8 + (
        S((width,), F32), S((width,), F32), S((model,), F32), S((low_grad.shape[0], e_lo), F32), S((high_grad.shape[0], e_hi), F32),
        S(result.shape, result.dtype), S(hidden_grad.shape, F32))
    dma = pltpu.SemaphoreType.DMA
    return pl.pallas_call(functools.partial(finish_kernel, pieces), out_shape=shapes,
        in_specs=[anywhere] * 3 + [vm] * 3 + [anywhere] * 2, out_specs=(anywhere,) * 6 + (vm,) * 13 + (anywhere,) * 2,
        scratch_shapes=[pltpu.VMEM((count, width, model), BF), pltpu.VMEM((count, width, model), F32), pltpu.VMEM(result.shape, result.dtype), pltpu.VMEM(hidden_grad.shape, F32), dma((count,)), dma((count,)), dma((4,))],
        name="finish", compiler_params=pltpu.CompilerParams(vmem_limit_bytes=63 << 20))(reduce_grad, expand_grad, attn_grads, small, low_grad, high_grad, result, hidden_grad)


def local(
    hidden,
    first_gain,
    first_shift,
    query_weight,
    query_bias,
    key_weight,
    value_weight,
    value_bias,
    output_weight,
    output_bias,
    first_scale,
    second_gain,
    second_shift,
    expand_weight,
    expand_bias,
    reduce_weight,
    reduce_bias,
    second_scale,
    table_low,
    table_high,
    resolution,
    counts,
    index_low,
    index_high,
    cotangent,
):
    floating = jnp.float32
    width = query_weight.shape[1]
    n_low = -(-table_low.shape[0] // (BB * 16)) * 16
    n_high = -(-table_high.shape[0] // (BB * 16)) * 16
    known = lax.axis_size("dp") == 8
    reduce_grad, expand_grad, attn_grads, result, hidden_grad, small, low_grad, high_grad = layer(
        HD ** (-0.5),
        known,
        resolution,
        counts,
        hidden,
        first_gain,
        first_shift,
        query_weight.T,
        query_bias,
        key_weight.T,
        value_weight.T,
        value_bias,
        output_weight,
        output_bias,
        first_scale,
        second_gain,
        second_shift,
        expand_weight,
        expand_bias,
        reduce_weight,
        reduce_bias,
        second_scale,
        cotangent,
        table_low.T,
        table_high.T,
        index_low,
        index_high,
        n_low,
        n_high,
    )
    if known:
        reduce_grad, expand_grad, *rest, low_grad, high_grad, result, hidden_grad = finish(
            reduce_grad,
            expand_grad,
            attn_grads,
            small,
            low_grad,
            high_grad,
            result,
            hidden_grad,
            width,
            table_low.shape[0],
            table_high.shape[0],
        )
        query_grad, key_grad, value_grad, output_grad, *norms, query_row, value_row, expand_row = rest
        return (
            result,
            hidden_grad,
            norms[0],
            norms[1],
            query_grad.T,
            query_row,
            key_grad.T,
            value_grad.T,
            value_row,
            output_grad,
            norms[3],
            norms[2],
            norms[4],
            norms[5],
            expand_grad,
            expand_row,
            reduce_grad,
            norms[7],
            norms[6],
            low_grad.T,
            high_grad.T,
        )
    if not known:
        reduce_grad, expand_grad, attn_grads, tail, low_grad, high_grad = lax.psum(
            (
                reduce_grad.astype(floating),
                expand_grad.astype(floating),
                attn_grads.astype(floating),
                small[8:],
                low_grad,
                high_grad,
            ),
            "dp",
        )
        small = jnp.concatenate((lax.psum(small[:8], ("dp", "tensor")), tail), axis=0)
    return (
        result,
        hidden_grad,
        small[0],
        small[1],
        attn_grads[:width].astype(floating).T,
        small[8, :width],
        attn_grads[width : 2 * width].astype(floating).T,
        attn_grads[2 * width : 3 * width].astype(floating).T,
        small[8, 256 : 256 + width],
        attn_grads[3 * width :].astype(floating),
        small[3],
        small[2],
        small[4],
        small[5],
        expand_grad.astype(floating),
        small[9],
        reduce_grad.astype(floating),
        small[7],
        small[6],
        low_grad[:, : table_low.shape[0]].T,
        high_grad[:, : table_high.shape[0]].T,
    )


def solution(mesh):
    in_specs = (
        P(("dp", "tensor"), None),
        P(),
        P(),
        P(None, "tensor"),
        P("tensor"),
        P(None, "tensor"),
        P(None, "tensor"),
        P("tensor"),
        P("tensor", None),
        P(),
        P(),
        P(),
        P(),
        P(None, "tensor"),
        P("tensor"),
        P("tensor", None),
        P(),
        P(),
        P(None, "tensor"),
        P(None, "tensor"),
        P("dp"),
        P("dp"),
        P(),
        P(),
        P(("dp", "tensor"), None),
    )
    out_specs = (
        P(("dp", "tensor"), None),
        P(("dp", "tensor"), None),
        P(),
        P(),
        P(None, "tensor"),
        P("tensor"),
        P(None, "tensor"),
        P(None, "tensor"),
        P("tensor"),
        P("tensor", None),
        P(),
        P(),
        P(),
        P(),
        P(None, "tensor"),
        P("tensor"),
        P("tensor", None),
        P(),
        P(),
        P(None, "tensor"),
        P(None, "tensor"),
    )
    return jax.shard_map(local, mesh=mesh, in_specs=in_specs, out_specs=out_specs, check_vma=False)
```

```python
import functools

import jax
import jax.numpy as jnp
from jax import lax
from jax.experimental import pallas as pl
from jax.experimental.pallas import tpu as pltpu
from jax.sharding import PartitionSpec as P

HD = 64
P_LO = 197
P_HI = 577
SEQ = 640
SLOTS = 2


eps_norm = 1e-06
masked_score = -1e30
inv_sqrt_two = 0.7071067811865476
inv_sqrt_two_pi = 0.3989422804014327


F32=jnp.float32; BF=jnp.bfloat16
NT=(((1,),(1,)),((),()))
def head_mask(h, width):
    lane = lax.broadcasted_iota(jnp.int32, (1, width), 1)
    return ((lane >= h*HD) & (lane < (h+1)*HD)).astype(F32).astype(BF)


BB=32; UN=16
def scatter_run(idx_ref, g_ref, out, first, last, fresh):
    heads = g_ref.shape[0]; na = out.shape[1]; m = idx_ref.shape[1]
    if fresh:
        out[...] = jnp.zeros_like(out)
    ib = lax.broadcasted_iota(jnp.int32, (16, m), 0).astype(F32)
    def body(r, c):
        ms = []; os = []
        for u in range(UN):
            row = r*UN+u
            idx = jnp.broadcast_to(idx_ref[pl.ds(row,1), :], (16, m))
            ia = (idx >> 5).astype(F32).astype(BF); il = (idx & 31).astype(F32).astype(BF)
            g = [jnp.broadcast_to(g_ref[h, pl.ds(row,1), :], (16, m)).astype(BF) for h in range(heads)]
            hits = [il == (ib + 16.0*k).astype(BF) for k in range(BB//16)]
            ms.append(jnp.concatenate([jnp.where(hits[k], g[h], jnp.zeros_like(g[h])) for h in range(heads) for k in range(BB//16)], axis=0))
            os.append(jnp.concatenate([jnp.where(ia == (ib + 16.0*k).astype(BF), jnp.ones_like(ia), jnp.zeros_like(ia)) for k in range(na//16)], axis=0))
        out[...] += lax.dot_general(jnp.concatenate(ms, axis=1), jnp.concatenate(os, axis=1), NT, preferred_element_type=F32)
        return c
    lax.fori_loop(first, last, body, 0)

PACK=8191.0
MESH = pl.DeviceIdType.MESH

CHUNKS = 9
TN = (((0,), (0,)), ((), ()))

def row(ref):
    return ref[...].reshape(1, ref.shape[0])

def live_of(t, rows, res, counts):
    slot = t * rows // SEQ
    first = t * rows - slot * SEQ
    limit = jnp.where(res[slot] == 1, P_HI, P_LO)
    limit = jnp.where(slot < counts[0], limit, 0)
    place = lax.broadcasted_iota(jnp.int32, (rows, 1), 0) + first
    return jnp.where(place < limit, 1.0, 0.0).astype(F32)

def moments(values):
    center = jnp.mean(values, axis=1, keepdims=True)
    centered = values - center
    inverse = lax.rsqrt(jnp.mean(centered * centered, axis=1, keepdims=True) + eps_norm)
    return centered * inverse, inverse

def norm_back(grad, scaled, inverse, gain):
    inner = grad * gain
    mean_inner = jnp.mean(inner, axis=1, keepdims=True)
    mean_mixed = jnp.mean(inner * scaled, axis=1, keepdims=True)
    return inverse * (inner - mean_inner - scaled * mean_mixed)

def look_up(tab, idx, heads):
    nch = tab.shape[1]
    lane = idx & 127
    ch = idx >> 7
    shift = jnp.where(ch >= nch, 0, 16)
    ch = jnp.where(ch >= nch, ch - nch, ch)
    acc = [None] * heads
    for k in range(nch):
        hit = ch == k
        for h in range(heads):
            v = jnp.take_along_axis(tab[h, k], lane, axis=1)
            acc[h] = v if k == 0 else jnp.where(hit, v, acc[h])
    return [((acc[h] << shift) >> 16).astype(F32) * (1.0 / PACK) for h in range(heads)]

def bias_rows(res, tab_lo, tab_hi, idx_lo, idx_hi, out, first, last, both):
    slots, heads = out.shape[:2]
    def masked(vals, j, limit):
        if (j + 1) * 128 <= limit:
            return vals
        place = lax.broadcasted_iota(jnp.int32, (8, 128), 1) + j * 128
        return [jnp.where(place < limit, v, masked_score) for v in vals]
    def body(r, c):
        for j in range(idx_hi.shape[1] // 128):
            cols = pl.ds(j * 128, 128)
            high = []
            low = []
            for part in range(2):
                rows = pl.ds(pl.multiple_of(r * 16 + part * 8, 8), 8)
                high.append(masked(look_up(tab_hi, idx_hi[rows, cols], heads), j, P_HI))
                if both and j < idx_lo.shape[1] // 128:
                    low.append(masked(look_up(tab_lo, idx_lo[rows, cols], heads), j, P_LO))
                else:
                    low.append([jnp.full((8, 128), masked_score, F32)] * heads)
            for h in range(heads):
                hi = jnp.concatenate([high[0][h], high[1][h]], axis=0).astype(BF)
                lo = jnp.concatenate([low[0][h], low[1][h]], axis=0).astype(BF)
                for s in range(slots):
                    out[s, h, pl.ds(pl.multiple_of(r * 16, 16), 16), cols] = jnp.where(res[s] == 1, hi, lo)
        return c
    lax.fori_loop(first, last, body, 0)

def layer_kernel(scale, sums, res, counts, hidden, gain1, shift1, wq, bq, wk, wv, bv, wo, bo, scale1, gain2, shift2, we, be, wr, rbias, scale2, cot,
                 table_lo, table_hi, ilo_in, ihi_in,
                 o0, o1, o2, result, hidden_grad, small, tlow, thigh,
                 tab_lo, tab_hi, raw, ilo, ihi, flip,
                 g1, gm, gt, ga, q_buf, k_buf, v_buf, mix, dmix, pb, act, pgl, part, acc, attn, x0, x1, x2, ghi, glo, esum,
                 cbuf, ccore, xbuf, xin, acore, across, bcore, bcross, ybuf, zbuf,
                 tlo, thi, wmine, smine, wten, vec, vland, vout, tbl, tland, tout,
                 h_s, h_r, m_s, m_r, t_s, t_r, a_s, a_r, o_s, o_r, n_s, n_r,
                 y_s, y_r, z_s, z_r, g_s, g_r, e_s, e_r, r_s, r_r, w_s, w_r, v_s, v_r):
    d = lax.axis_index("dp")
    t = lax.axis_index("tensor")
    col = d // 2
    side = lax.rem(d, 2)
    neighbour = d + 1 - 2 * side
    sibling = t + 1 - 2 * lax.rem(t, 2)
    cross = lax.rem(t + 2, 4)
    diag = 3 - t
    rows = hidden.shape[0]
    half = rows // 2
    slots, heads = pb.shape[:2]
    width = q_buf.shape[1]
    model = g1.shape[1]
    barrier = pltpu.get_barrier_semaphore()
    for k in range(1, 4):
        pl.semaphore_signal(barrier, inc=1, device_id=(d, lax.rem(t + k, 4)), device_id_type=MESH)
    if sums:
        for k in range(1, 8):
            pl.semaphore_signal(barrier, inc=1, device_id=(lax.rem(d + k, 8), t), device_id_type=MESH)

    def remote(src, dst, send, recv, device):
        return pltpu.make_async_remote_copy(src_ref=src, dst_ref=dst, send_sem=send, recv_sem=recv, device_id=device, device_id_type=MESH)
    def rows_at(who):
        return pl.ds(pl.multiple_of(who * rows, 16), rows)
    def span(who, h):
        return pl.ds(pl.multiple_of(who * rows + h * half, 16), half)
    def gather_x(buf, send, recv, h):
        here = buf.at[span(t, h)]
        return remote(here, here, send.at[h], recv.at[h], (d, cross))
    def gather_near(buf, send, recv, h):
        here = buf.at[span(t, h)]
        return remote(here, here, send.at[2 + h], recv.at[2 + h], (d, sibling))
    def gather_on(buf, send, recv, h):
        here = buf.at[span(cross, h)]
        return remote(here, here, send.at[4 + h], recv.at[4 + h], (d, sibling))
    def sum_far(j, send, recv, h):
        return remote(cbuf.at[0, h], ccore.at[j, 0, h], send.at[h], recv.at[h], (d, sibling))
    def sum_near(j, send, recv, h):
        return remote(cbuf.at[1, h], ccore.at[j, 1, h], send.at[2 + h], recv.at[2 + h], (d, sibling))
    def sum_x(j, send, recv, h):
        return remote(xbuf.at[h], xin.at[j, h], send.at[4 + h], recv.at[4 + h], (d, cross))
    arrays = (x0, x1, x2)
    outs = (o0, o1, o2)
    size = x0.shape[0] // 3
    part_y = size // 2
    part_z = part_y // 4
    def at(n, start, count):
        return pl.ds(pl.multiple_of((n % 3) * size + start, 16), count)
    def y_copy(n):
        return remote(arrays[n // 3].at[at(n, (1 - side) * part_y, part_y)], ybuf.at[n], y_s.at[n], y_r.at[n], (neighbour, t))
    def y_first(n):
        here = pl.ds(pl.multiple_of(n * size + (1 - side) * part_y, 16), part_y)
        return remote(x0.at[here], ybuf.at[n], y_s.at[n], y_r.at[n], (neighbour, t))
    def z_copy(n, k):
        to = lax.rem(col + k, 4)
        return remote(arrays[n // 3].at[at(n, side * part_y + to * part_z, part_z)], zbuf.at[n, k - 1], z_s.at[n, k], z_r.at[n, k], (to * 2 + side, t))
    def g_copy(n, k):
        to = lax.rem(col + k, 4)
        here = outs[n // 3].at[at(n, side * part_y + col * part_z, part_z)]
        return remote(here, here, g_s.at[n, k], g_r.at[n, k], (to * 2 + side, t))
    def e_copy(n):
        here = outs[n // 3].at[at(n, side * part_y, part_y)]
        return remote(here, here, e_s.at[n], e_r.at[n], (neighbour, t))
    def start_y(n):
        y_copy(n).start()
    def step_a(n):
        y_copy(n).wait()
        here = at(n, side * part_y, part_y)
        arrays[n // 3][here] = (arrays[n // 3][here].astype(F32) + ybuf[n].astype(F32)).astype(BF)
        for k in range(1, 4):
            z_copy(n, k).start()
    def step_b(n):
        for k in range(1, 4):
            z_copy(n, k).wait()
        here = at(n, side * part_y + col * part_z, part_z)
        total = arrays[n // 3][here].astype(F32)
        for k in range(3):
            total = total + zbuf[n, k].astype(F32)
        outs[n // 3][here] = total.astype(BF)
        for k in range(1, 4):
            g_copy(n, k).start()
    def step_d(n):
        for k in range(1, 4):
            g_copy(n, k).wait()
        e_copy(n).start()
    if not sums:
        start_y = step_a = step_b = step_d = lambda n: None

    scaled, inverse = moments(hidden[...].astype(F32))
    g1[rows_at(t)] = (scaled * row(gain1) + row(shift1)).astype(BF)
    pl.semaphore_wait(barrier, 10 if sums else 3)
    for h in range(2):
        gather_x(g1, h_s, h_r, h).start()
        gather_near(g1, h_s, h_r, h).start()
    alive = live_of(t, rows, res, counts)
    gm[rows_at(t)] = (cot[...].astype(F32) * alive * row(scale2)).astype(BF)
    ilo[...] = jnp.zeros_like(ilo)
    ilo[0:P_LO, 0:P_LO] = ilo_in[...]
    ihi[...] = jnp.zeros_like(ihi)
    ihi[0:P_HI, 0:P_HI] = ihi_in[...]
    for table, packed in ((table_lo, tab_lo), (table_hi, tab_hi)):
        nch = packed.shape[1]
        raw[...] = jnp.zeros_like(raw)
        raw[:, 0:table.shape[1]] = table[...]
        for k in range(nch):
            low = (raw[:, k * 128:(k + 1) * 128] * PACK + 32768.5).astype(jnp.int32) - 32768
            high = (raw[:, (k + nch) * 128:(k + nch + 1) * 128] * PACK + 32768.5).astype(jnp.int32) - 32768
            word = (high << 16) | (low & 65535)
            for h in range(heads):
                packed[h, k] = jnp.broadcast_to(word[h:h + 1, :], (8, 128))
    look = functools.partial(bias_rows, res, tab_lo, tab_hi, ilo, ihi, pb)
    n_low = -(-P_LO // 16)
    n_high = -(-P_HI // 16)
    middle = (n_low + n_high) // 2
    look(0, n_low, True)
    look(n_low, middle, False)
    for h in range(2):
        gather_x(g1, h_s, h_r, h).wait()
        gather_on(g1, h_s, h_r, h).start()
        gather_x(gm, m_s, m_r, h).start()
        gather_near(gm, m_s, m_r, h).start()
    look(middle, n_high, False)
    pb[:, :, n_high * 16:, :] = jnp.zeros((slots, heads, SEQ - n_high * 16, SEQ), BF)
    for h in range(2):
        gather_near(g1, h_s, h_r, h).wait()
        gather_on(g1, h_s, h_r, h).wait()

    def project(i, c):
        here = rows_at(i)
        g = g1[here]
        q_buf[here] = ((lax.dot_general(g, wq[...], NT, preferred_element_type=F32) + row(bq)) * scale).astype(BF)
        k_buf[here] = lax.dot_general(g, wk[...], NT, preferred_element_type=F32).astype(BF)
        v_buf[here] = (lax.dot_general(g, wv[...], NT, preferred_element_type=F32) + row(bv)).astype(BF)
        return c
    lax.fori_loop(0, 4, project, 0)

    def attend_image(slot):
        here = pl.ds(pl.multiple_of(slot * SEQ, 16), SEQ)
        k = k_buf[here]
        v = v_buf[here]
        vm = [v * head_mask(h, width) for h in range(heads)]
        def piece(i, c):
            first = pl.multiple_of(i * rows, 16)
            there = pl.ds(pl.multiple_of(slot * SEQ + first, 16), rows)
            q = q_buf[there]
            out = jnp.zeros((rows, width), F32)
            for h in range(heads):
                s = lax.dot_general(q * head_mask(h, width), k, NT, preferred_element_type=F32)
                s = s + pb[slot, h, pl.ds(first, rows)].astype(F32)
                peak = jnp.max(s, axis=1, keepdims=True)
                e = jnp.exp(s - peak)
                total = jnp.sum(e, axis=1, keepdims=True)
                p = (e * (1.0 / total)).astype(BF)
                pb[slot, h, pl.ds(first, rows)] = p
                out = out + jnp.dot(p, vm[h], preferred_element_type=F32)
            mix[there] = out.astype(BF)
            return c
        lax.fori_loop(0, SEQ // rows, piece, 0)
    def output_of(who, h):
        return jnp.dot(mix[span(who, h)], wo[...], preferred_element_type=F32)

    mine = t * rows // SEQ
    attend_image(1 - mine)
    for h in range(2):
        cbuf[0, h] = output_of(diag, h).astype(BF)
        sum_far(0, o_s, o_r, h).start()
    for h in range(2):
        total = output_of(cross, h)
        sum_far(0, o_s, o_r, h).wait()
        xbuf[h] = (total + ccore[0, 0, h].astype(F32)).astype(BF)
        sum_x(0, o_s, o_r, h).start()
    attend_image(mine)
    for h in range(2):
        cbuf[1, h] = output_of(sibling, h).astype(BF)
        sum_near(0, o_s, o_r, h).start()
    for h in range(2):
        acc[pl.ds(h * half, half)] = output_of(t, h)
    for h in range(2):
        gather_x(gm, m_s, m_r, h).wait()
        gather_on(gm, m_s, m_r, h).start()
    for h in range(2):
        here = pl.ds(h * half, half)
        sum_near(0, o_s, o_r, h).wait()
        sum_x(0, o_s, o_r, h).wait()
        out = acc[here] + ccore[0, 1, h].astype(F32) + xin[0, h].astype(F32) + row(bo)
        attn[here] = out
        scaled, inverse = moments(hidden[here].astype(F32) + row(scale1) * out)
        gt[span(t, h)] = (scaled * row(gain2) + row(shift2)).astype(BF)
        gather_x(gt, t_s, t_r, h).start()
        gather_near(gt, t_s, t_r, h).start()

    esum[...] = jnp.zeros_like(esum)
    def feed(who, h):
        here = span(who, h)
        pre = jnp.dot(gt[here], we[...], preferred_element_type=F32) + row(be)
        grad = lax.dot_general(gm[here], wr[...], NT, preferred_element_type=F32)
        phi = 0.5 * (1.0 + lax.erf(pre * inv_sqrt_two))
        active = (pre * phi).astype(BF)
        act[here] = active
        grad = grad * (phi + pre * inv_sqrt_two_pi * jnp.exp(-0.5 * pre * pre))
        esum[...] += jnp.sum(grad, axis=0, keepdims=True)
        grad = grad.astype(BF)
        pgl[here] = grad
        part[here] = jnp.dot(active, wr[...], preferred_element_type=F32).astype(BF)
        return lax.dot_general(grad, we[...], NT, preferred_element_type=F32)
    def feed_own(h, c):
        acc[pl.ds(pl.multiple_of(h * half, 16), half)] = feed(t, h)
        return c
    lax.fori_loop(0, 2, feed_own, 0)
    for h in range(2):
        gather_near(gm, m_s, m_r, h).wait()
        gather_near(gt, t_s, t_r, h).wait()
        gather_on(gm, m_s, m_r, h).wait()
    def feed_near(h, c):
        cbuf[1, h] = feed(sibling, h).astype(BF)
        sum_near(1, n_s, n_r, h).start()
        return c
    lax.fori_loop(0, 2, feed_near, 0)
    def feed_far(h, c):
        gather_x(gt, t_s, t_r, h).wait()
        gather_on(gt, t_s, t_r, h).start()
        total = feed(cross, h)
        gather_on(gt, t_s, t_r, h).wait()
        cbuf[0, h] = feed(diag, h).astype(BF)
        sum_far(1, n_s, n_r, h).start()
        sum_far(1, n_s, n_r, h).wait()
        xbuf[h] = (total + ccore[1, 0, h].astype(F32)).astype(BF)
        sum_x(1, n_s, n_r, h).start()
        return c
    lax.fori_loop(0, 2, feed_far, 0)

    tile = 128
    def reduce_grad(i, c):
        cols = pl.ds(pl.multiple_of(i * tile, tile), tile)
        x0[cols] = lax.dot_general(act[:, cols], gm[...], TN, preferred_element_type=F32).astype(BF)
        return c
    third = act.shape[1] // tile // 3
    def reduce_third(n, c):
        lax.fori_loop(n * third, (n + 1) * third, reduce_grad, 0)
        if sums:
            y_first(n).start()
        return c
    lax.fori_loop(0, 3, reduce_third, 0)
    wmine[...] = jnp.zeros_like(wmine)
    def second_back(h):
        here = pl.ds(h * half, half)
        sum_near(1, n_s, n_r, h).wait()
        sum_x(1, n_s, n_r, h).wait()
        grad = acc[here] + ccore[1, 1, h].astype(F32) + xin[1, h].astype(F32)
        out = attn[here]
        scaled, inverse = moments(hidden[here].astype(F32) + row(scale1) * out)
        after = cot[here].astype(F32) * alive[h * half:(h + 1) * half] + norm_back(grad, scaled, inverse, row(gain2))
        hidden_grad[here] = after
        agrad = after * row(scale1)
        ga[span(t, h)] = agrad.astype(BF)
        gather_x(ga, a_s, a_r, h).start()
        gather_near(ga, a_s, a_r, h).start()
        wmine[2:3, :] += jnp.sum(after * out, axis=0, keepdims=True)
        wmine[3:4, :] += jnp.sum(agrad, axis=0, keepdims=True)
        wmine[4:5, :] += jnp.sum(grad * scaled, axis=0, keepdims=True)
        wmine[5:6, :] += jnp.sum(grad, axis=0, keepdims=True)
    second_back(0)
    step_a(0)
    def expand_grad(i, c):
        cols = pl.ds(pl.multiple_of(i * tile, tile), tile)
        x1[cols] = lax.dot_general(gt[:, cols], pgl[...], TN, preferred_element_type=F32).astype(BF)
        return c
    lax.fori_loop(0, 3 * third, expand_grad, 0)
    start_y(3)
    start_y(4)
    step_a(1)
    second_back(1)
    step_b(0)
    step_a(2)
    start_y(5)
    def mixture_of(who):
        here = rows_at(who)
        dmix[here] = lax.dot_general(ga[here], wo[...], NT, preferred_element_type=F32).astype(BF)
    mixture_of(t)
    gather_x(ga, a_s, a_r, 0).wait()
    gather_on(ga, a_s, a_r, 0).start()
    for h in range(2):
        gather_near(ga, a_s, a_r, h).wait()
    mixture_of(sibling)
    step_b(1)
    gather_x(ga, a_s, a_r, 1).wait()
    gather_on(ga, a_s, a_r, 1).start()
    mixture_of(cross)
    step_a(3)
    step_a(4)
    for h in range(2):
        gather_on(ga, a_s, a_r, h).wait()
    mixture_of(diag)
    smine[...] = jnp.zeros_like(smine)
    smine[1:2, :] = esum[...]
    ghi[...] = jnp.zeros_like(ghi)
    glo[...] = jnp.zeros_like(glo)
    def attention_back(slot, c):
        here = pl.ds(pl.multiple_of(slot * SEQ, 16), SEQ)
        q = q_buf[here]
        k = k_buf[here]
        v = v_buf[here]
        dd = dmix[here]
        qt = q.T
        dt = dd.T
        is_high = jnp.where(res[slot] == 1, 1.0, 0.0).astype(F32)
        out = jnp.zeros((SEQ, width), F32)
        dks = []
        dvs = []
        nh = ghi.shape[1]
        nl, ml = glo.shape[1:]
        for h in range(heads):
            mask = head_mask(h, width)
            p = pb[slot, h]
            dp = lax.dot_general(dd * mask, v, NT, preferred_element_type=F32)
            pf = p.astype(F32)
            m = pf * dp
            ds = m - pf * jnp.sum(m, axis=1, keepdims=True)
            ghi[h] += ds[:nh] * is_high
            glo[h] += ds[:nl, :ml] * (1.0 - is_high)
            low = ds.astype(BF)
            out = out + jnp.dot(low, k * mask, preferred_element_type=F32)
            dks.append(jnp.dot(qt[h*HD:(h+1)*HD], low, preferred_element_type=F32))
            dvs.append(jnp.dot(dt[h*HD:(h+1)*HD], p, preferred_element_type=F32))
        out = out * scale
        smine[0:1, 0:width] += jnp.sum(out, axis=0, keepdims=True)
        q_buf[here] = out.astype(BF)
        k_buf[here] = jnp.concatenate(dks, axis=0).T.astype(BF)
        out = jnp.concatenate(dvs, axis=0).T
        smine[0:1, 256:256 + width] += jnp.sum(out, axis=0, keepdims=True)
        v_buf[here] = out.astype(BF)
        return c
    lax.fori_loop(0, slots, attention_back, 0)
    def back(who):
        here = rows_at(who)
        total = jnp.dot(q_buf[here], wq[...], preferred_element_type=F32)
        total = total + jnp.dot(k_buf[here], wk[...], preferred_element_type=F32)
        return total + jnp.dot(v_buf[here], wv[...], preferred_element_type=F32)
    def send(buf, value):
        for h in range(2):
            buf[h] = value[h * half:(h + 1) * half].astype(BF)
    def whole(ref):
        return jnp.concatenate([ref[0], ref[1]], axis=0).astype(F32)
    a_far = remote(cbuf.at[0], acore.at[0], r_s.at[0], r_r.at[0], (d, sibling))
    a_near = remote(cbuf.at[1], acore.at[1], r_s.at[1], r_r.at[1], (d, sibling))
    a_cross = remote(xbuf, across, r_s.at[2], r_r.at[2], (d, cross))
    b_far = remote(part.at[rows_at(diag)], bcore.at[0], r_s.at[3], r_r.at[3], (d, sibling))
    b_near = remote(part.at[rows_at(sibling)], bcore.at[1], r_s.at[4], r_r.at[4], (d, sibling))
    b_cross = remote(xbuf, bcross, r_s.at[5], r_r.at[5], (d, cross))
    send(cbuf.at[0], back(diag))
    a_far.start()
    b_far.start()
    total = back(cross)
    a_far.wait()
    send(xbuf, total + whole(acore.at[0]))
    a_cross.start()
    step_d(1)
    step_b(3)
    for j, (left, right) in list(enumerate(((q_buf, g1), (k_buf, g1), (v_buf, g1), (mix, ga))))[0:2]:
        x2[j * width:(j + 1) * width, :] = lax.dot_general(left[...], right[...], TN, preferred_element_type=F32).astype(BF)
    step_d(0)
    step_b(2)
    start_y(6)
    for j, (left, right) in list(enumerate(((q_buf, g1), (k_buf, g1), (v_buf, g1), (mix, ga))))[2:3]:
        x2[j * width:(j + 1) * width, :] = lax.dot_general(left[...], right[...], TN, preferred_element_type=F32).astype(BF)
    for j, (left, right) in list(enumerate(((q_buf, g1), (k_buf, g1), (v_buf, g1), (mix, ga))))[3:4]:
        x2[j * width:(j + 1) * width, :] = lax.dot_general(left[...], right[...], TN, preferred_element_type=F32).astype(BF)
    step_a(5)
    start_y(7)
    send(cbuf.at[1], back(sibling))
    a_near.start()
    b_near.start()
    acc[...] = back(t)
    b_far.wait()
    n_hi = -(-P_HI // UN)
    done = [0]
    def scatter_part(count):
        first, last = done[0], min(done[0] + count, n_hi)
        scatter_run(ihi, ghi, thi, first, last, first == 0)
        done[0] = last
    scatter_part(3)
    scatter_part(3)
    step_b(4)
    start_y(8)
    a_cross.wait()
    send(xbuf, part[rows_at(cross)].astype(F32) + bcore[0].astype(F32))
    b_cross.start()
    a_near.wait()
    grad = acc[...] + whole(acore.at[1]) + whole(across)
    scaled, inverse = moments(hidden[...].astype(F32))
    wmine[0:1, :] = jnp.sum(grad * scaled, axis=0, keepdims=True)
    wmine[1:2, :] = jnp.sum(grad, axis=0, keepdims=True)
    hidden_grad[...] += norm_back(grad, scaled, inverse, row(gain1))
    scatter_part(3)
    step_b(5)
    scatter_part(3)
    step_a(6)
    scatter_part(3)
    scatter_part(3)
    step_d(5)
    b_near.wait()
    b_cross.wait()
    out = part[rows_at(t)].astype(F32) + bcore[1].astype(F32) + whole(bcross) + row(rbias)
    after = hidden[...].astype(F32) + row(scale1) * attn[...]
    result[...] = ((after + row(scale2) * out) * alive).astype(BF)
    up = cot[...].astype(F32) * alive
    wmine[6:7, :] = jnp.sum(up * out, axis=0, keepdims=True)
    wmine[7:8, :] = jnp.sum(up * row(scale2), axis=0, keepdims=True)
    step_d(4)
    step_a(8)
    def w_copy(k):
        return remote(wmine, wten.at[k], w_s.at[k], w_r.at[k], (d, lax.rem(t + k, 4)))
    def eighth(buf, who):
        count = buf.shape[0] // 8
        return buf.at[pl.ds(pl.multiple_of(who * count, 8), count)]
    def v_copy(j, k):
        buf, land = ((vec, vland), (tbl, tland))[j]
        to = lax.rem(d + k, 8)
        return remote(eighth(buf, to), land.at[k], v_s.at[j, k], v_r.at[j, k], (to, t))
    def u_copy(j, k):
        buf = (vout, tout)[j]
        return remote(eighth(buf, d), eighth(buf, d), v_s.at[2 + j, k], v_r.at[2 + j, k], (lax.rem(d + k, 8), t))
    def small_start(j):
        for k in range(1, 8):
            v_copy(j, k).start()
    def small_turn(j):
        buf, land = ((vec, vland), (tbl, tland))[j]
        total = eighth(buf, d)[...]
        for k in range(1, 8):
            v_copy(j, k).wait()
            total = total + land[k]
        eighth((vout, tout)[j], d)[...] = total
        for k in range(1, 8):
            u_copy(j, k).start()
    def small_end(j):
        for k in range(1, 8):
            u_copy(j, k).wait()
    if not sums:
        def small_turn(j):
            (vout, tout)[j][...] = (vec, tbl)[j][...]
        small_start = small_end = lambda j: None
    if sums:
        for k in range(1, 4):
            w_copy(k).start()
    step_a(7)
    scatter_part(3)
    scatter_part(3)
    step_d(2)
    total = wmine[...]
    if sums:
        for k in range(1, 4):
            w_copy(k).wait()
            total = total + wten[k]
    vec[...] = jnp.zeros_like(vec)
    lanes = model // 128
    for r in range(8):
        for j in range(lanes):
            vec[r * lanes + j:r * lanes + j + 1, :] = total[r:r + 1, j * 128:(j + 1) * 128]
    for r in range(2):
        for j in range(lanes):
            vec[(8 + r) * lanes + j:(8 + r) * lanes + j + 1, :] = smine[r:r + 1, j * 128:(j + 1) * 128]
    small_start(0)
    scatter_part(3)
    step_d(3)
    step_b(6)
    scatter_part(3)
    step_b(8)
    scatter_part(3)
    step_b(7)
    scatter_part(n_hi)
    small_turn(0)
    step_d(6)
    scatter_run(ilo, glo, tlo, 0, -(-P_LO // UN), True)
    step_d(8)
    per = (thi.shape[1] + tlo.shape[1]) // 4
    tbl[...] = jnp.zeros_like(tbl)
    def spread(src, base):
        count = src.shape[1] // 4
        for h in range(heads):
            flip[0:src.shape[1], :] = src[h * BB:(h + 1) * BB, :].T
            pieces = [flip[pl.ds(i, count, stride=4), :] for i in range(4)]
            start = h * per + base
            tbl[start:start + count, :] = jnp.concatenate(pieces, axis=1)
    spread(thi, 0)
    spread(tlo, thi.shape[1] // 4)
    if not sums:
        o0[...] = x0[...]
        o1[...] = x1[...]
        o2[...] = x2[...]
    small_start(1)
    step_d(7)
    small_end(0)
    for r in range(10):
        for j in range(lanes):
            small[r:r + 1, j * 128:(j + 1) * 128] = vout[r * lanes + j:r * lanes + j + 1, :]
    small_turn(1)
    small_end(1)
    for src, base, count in ((thigh, 0, thi.shape[1] // 4), (tlow, thi.shape[1] // 4, tlo.shape[1] // 4)):
        for h in range(heads):
            for r in range(count):
                at_row = h * per + base + r
                src[h:h + 1, r * 128:(r + 1) * 128] = tout[at_row:at_row + 1, :]
    if sums:
        for n in range(CHUNKS):
            e_copy(n).wait()

def layer(scale, sums, res, counts, hidden, gain1, shift1, wq, bq, wk, wv, bv, wo, bo, scale1, gain2, shift2, we, be, wr, rbias, scale2, cot, table_low, table_high, ilo, ihi, n_lo, n_hi):
    rows, model = hidden.shape
    total = rows * 4
    width = wq.shape[0]
    inner = we.shape[1]
    heads, e_lo = table_low.shape
    e_hi = table_high.shape[1]
    vm = pl.BlockSpec(memory_space=pltpu.VMEM)
    sm = pl.BlockSpec(memory_space=pltpu.SMEM)
    dma = pltpu.SemaphoreType.DMA
    V = pltpu.VMEM
    S = jax.ShapeDtypeStruct
    operands = (hidden, gain1, shift1, wq, bq, wk, wv, bv, wo, bo, scale1, gain2, shift2, we, be, wr, rbias, scale2, cot, table_low, table_high, ilo, ihi)
    half = rows // 2
    return pl.pallas_call(functools.partial(layer_kernel, scale, sums),
        out_shape=(S((inner, model), BF), S((model, inner), BF), S((4 * width, model), BF), S((rows, model), BF), S((rows, model), F32), S((16, model), F32), S((heads, n_lo * 32), F32), S((heads, n_hi * 32), F32)),
        in_specs=[sm, sm] + [vm] * len(operands), out_specs=(vm,) * 8,
        scratch_shapes=[V((heads, -(-e_lo // 256), 8, 128), jnp.int32), V((heads, -(-e_hi // 256), 8, 128), jnp.int32), V((heads, -(-e_hi // 256) * 256), F32), V((208, 256), jnp.int32), V((592, SEQ), jnp.int32), V((n_hi, BB), F32)]
            + [V((total, model), BF)] * 4 + [V((total, width), BF)] * 5 + [V((SLOTS, heads, SEQ, SEQ), BF)]
            + [V((total, inner), BF)] * 2 + [V((total, model), BF)] + [V((rows, model), F32)] * 2
            + [V((inner, model), BF), V((model, inner), BF), V((4 * width, model), BF), V((heads, 592, SEQ), F32), V((heads, 208, 256), F32), V((1, inner), F32)]
            + [V((2, 2, half, model), BF), V((2, 2, 2, half, model), BF)] + [V((2, half, model), BF), V((2, 2, half, model), BF)]
            + [V((2, 2, half, model), BF), V((2, half, model), BF), V((2, rows, model), BF), V((2, half, model), BF)]
            + [V((CHUNKS, 128, model), BF), V((CHUNKS, 3, 32, model), BF)]
            + [V((heads * BB, n_lo), F32), V((heads * BB, n_hi), F32)]
            + [V((8, model), F32)] * 2 + [V((4, 8, model), F32), V((64, 128), F32), V((8, 8, 128), F32), V((64, 128), F32), V((128, 128), F32), V((8, 16, 128), F32), V((128, 128), F32)]
            + [dma((6,))] * 12
            + [dma((CHUNKS,)), dma((CHUNKS,)), dma((CHUNKS, 4)), dma((CHUNKS, 4)), dma((CHUNKS, 4)), dma((CHUNKS, 4)), dma((CHUNKS,)), dma((CHUNKS,)),
               dma((6,)), dma((6,)), dma((4,)), dma((4,)), dma((4, 8)), dma((4, 8))],
        name="layer", cost_estimate=pl.CostEstimate(flops=100 * 10**9, bytes_accessed=60 * 10**6, transcendentals=0),
        compiler_params=pltpu.CompilerParams(collective_id=0, has_side_effects=True, vmem_limit_bytes=127 << 19))(res, counts, *operands)


def finish_kernel(pieces, i0, i1, i2, small, tlow, thigh, res_in, hid_in, *refs):
    r_out, e_out, q_out, k_out, v_out, o_out = refs[:6]
    vectors = refs[6:14]
    qb, vb, eb, tl, th, res_out, hid_out, low, wide, res, hid, s_in, s_out, s_x = refs[14:]
    first = [pltpu.make_async_copy(hid_in, hid, s_x.at[0]), pltpu.make_async_copy(res_in, res, s_x.at[1])]
    second = [pltpu.make_async_copy(hid, hid_out, s_x.at[2]), pltpu.make_async_copy(res, res_out, s_x.at[3])]
    rows = low.shape[1]
    places = []
    for src, out in ((i0, r_out), (i1, e_out)):
        for n in range(pieces):
            here = pl.ds(n * rows, rows)
            places.append((src.at[here], out.at[here]))
    for n, out in enumerate((q_out, k_out, v_out, o_out)):
        places.append((i2.at[pl.ds(n * rows, rows)], out))
    loads = [pltpu.make_async_copy(src, low.at[n], s_in.at[n]) for n, (src, _) in enumerate(places)]
    stores = [pltpu.make_async_copy(wide.at[n], out, s_out.at[n]) for n, (_, out) in enumerate(places)]
    for copy in first + loads:
        copy.start()
    for before, after in zip(first, second):
        before.wait()
        after.start()
    for n in range(len(places)):
        loads[n].wait()
        wide[n] = low[n].astype(F32)
        stores[n].start()
    for r, out in enumerate(vectors):
        out[...] = small[r:r + 1, :].reshape(out.shape)
    qb[...] = small[8:9, 0:qb.shape[0]].reshape(qb.shape)
    vb[...] = small[8:9, 256:256 + vb.shape[0]].reshape(vb.shape)
    eb[...] = small[9:10, :].reshape(eb.shape)
    tl[...] = tlow[:, 0:tl.shape[1]]
    th[...] = thigh[:, 0:th.shape[1]]
    for copy in stores + second:
        copy.wait()

def finish(reduce_grad, expand_grad, attn_grads, small, low_grad, high_grad, result, hidden_grad, width, e_lo, e_hi):
    S = jax.ShapeDtypeStruct
    vm = pl.BlockSpec(memory_space=pltpu.VMEM)
    anywhere = pl.BlockSpec(memory_space=pl.ANY)
    model = reduce_grad.shape[1]
    pieces = reduce_grad.shape[0] // width
    count = 2 * pieces + 4
    shapes = (S(reduce_grad.shape, F32), S(expand_grad.shape, F32)) + (S((width, model), F32),) * 4 + (S((model,), F32),) * 8 + (
        S((width,), F32), S((width,), F32), S((model,), F32), S((low_grad.shape[0], e_lo), F32), S((high_grad.shape[0], e_hi), F32),
        S(result.shape, result.dtype), S(hidden_grad.shape, F32))
    dma = pltpu.SemaphoreType.DMA
    return pl.pallas_call(functools.partial(finish_kernel, pieces), out_shape=shapes,
        in_specs=[anywhere] * 3 + [vm] * 3 + [anywhere] * 2, out_specs=(anywhere,) * 6 + (vm,) * 13 + (anywhere,) * 2,
        scratch_shapes=[pltpu.VMEM((count, width, model), BF), pltpu.VMEM((count, width, model), F32), pltpu.VMEM(result.shape, result.dtype), pltpu.VMEM(hidden_grad.shape, F32), dma((count,)), dma((count,)), dma((4,))],
        name="finish", compiler_params=pltpu.CompilerParams(vmem_limit_bytes=63 << 20))(reduce_grad, expand_grad, attn_grads, small, low_grad, high_grad, result, hidden_grad)


def local(
    hidden,
    first_gain,
    first_shift,
    query_weight,
    query_bias,
    key_weight,
    value_weight,
    value_bias,
    output_weight,
    output_bias,
    first_scale,
    second_gain,
    second_shift,
    expand_weight,
    expand_bias,
    reduce_weight,
    reduce_bias,
    second_scale,
    table_low,
    table_high,
    resolution,
    counts,
    index_low,
    index_high,
    cotangent,
):
    floating = jnp.float32
    width = query_weight.shape[1]
    n_low = -(-table_low.shape[0] // (BB * 16)) * 16
    n_high = -(-table_high.shape[0] // (BB * 16)) * 16
    known = lax.axis_size("dp") == 8
    reduce_grad, expand_grad, attn_grads, result, hidden_grad, small, low_grad, high_grad = layer(
        HD ** (-0.5),
        known,
        resolution,
        counts,
        hidden,
        first_gain,
        first_shift,
        query_weight.T,
        query_bias,
        key_weight.T,
        value_weight.T,
        value_bias,
        output_weight,
        output_bias,
        first_scale,
        second_gain,
        second_shift,
        expand_weight,
        expand_bias,
        reduce_weight,
        reduce_bias,
        second_scale,
        cotangent,
        table_low.T,
        table_high.T,
        index_low,
        index_high,
        n_low,
        n_high,
    )
    if known:
        reduce_grad, expand_grad, *rest, low_grad, high_grad, result, hidden_grad = finish(
            reduce_grad,
            expand_grad,
            attn_grads,
            small,
            low_grad,
            high_grad,
            result,
            hidden_grad,
            width,
            table_low.shape[0],
            table_high.shape[0],
        )
        query_grad, key_grad, value_grad, output_grad, *norms, query_row, value_row, expand_row = rest
        return (
            result,
            hidden_grad,
            norms[0],
            norms[1],
            query_grad.T,
            query_row,
            key_grad.T,
            value_grad.T,
            value_row,
            output_grad,
            norms[3],
            norms[2],
            norms[4],
            norms[5],
            expand_grad,
            expand_row,
            reduce_grad,
            norms[7],
            norms[6],
            low_grad.T,
            high_grad.T,
        )
    if not known:
        reduce_grad, expand_grad, attn_grads, tail, low_grad, high_grad = lax.psum(
            (
                reduce_grad.astype(floating),
                expand_grad.astype(floating),
                attn_grads.astype(floating),
                small[8:],
                low_grad,
                high_grad,
            ),
            "dp",
        )
        small = jnp.concatenate((lax.psum(small[:8], ("dp", "tensor")), tail), axis=0)
    return (
        result,
        hidden_grad,
        small[0],
        small[1],
        attn_grads[:width].astype(floating).T,
        small[8, :width],
        attn_grads[width : 2 * width].astype(floating).T,
        attn_grads[2 * width : 3 * width].astype(floating).T,
        small[8, 256 : 256 + width],
        attn_grads[3 * width :].astype(floating),
        small[3],
        small[2],
        small[4],
        small[5],
        expand_grad.astype(floating),
        small[9],
        reduce_grad.astype(floating),
        small[7],
        small[6],
        low_grad[:, : table_low.shape[0]].T,
        high_grad[:, : table_high.shape[0]].T,
    )


def solution(mesh):
    in_specs = (
        P(("dp", "tensor"), None),
        P(),
        P(),
        P(None, "tensor"),
        P("tensor"),
        P(None, "tensor"),
        P(None, "tensor"),
        P("tensor"),
        P("tensor", None),
        P(),
        P(),
        P(),
        P(),
        P(None, "tensor"),
        P("tensor"),
        P("tensor", None),
        P(),
        P(),
        P(None, "tensor"),
        P(None, "tensor"),
        P("dp"),
        P("dp"),
        P(),
        P(),
        P(("dp", "tensor"), None),
    )
    out_specs = (
        P(("dp", "tensor"), None),
        P(("dp", "tensor"), None),
        P(),
        P(),
        P(None, "tensor"),
        P("tensor"),
        P(None, "tensor"),
        P(None, "tensor"),
        P("tensor"),
        P("tensor", None),
        P(),
        P(),
        P(),
        P(),
        P(None, "tensor"),
        P("tensor"),
        P("tensor", None),
        P(),
        P(),
        P(None, "tensor"),
        P(None, "tensor"),
    )
    return jax.shard_map(local, mesh=mesh, in_specs=in_specs, out_specs=out_specs, check_vma=False)
```
